128 devices in a mesh: section: 4 (over x_lo, core), ctx: 8 (over x_hi, z), tp: 4 (over y).
Axes of the slice: x: 4 (x_hi: 2, x_lo: 2; x = x_hi * 2 + x_lo), y: 4, z: 4, core: 2. Of those that a mesh axis runs over, the one named last changes fastest.
Arguments:
- stretch_order: int32 [8, 2], replicated, may hold values from 0 to 15, as said below
- queries: bfloat16 [4, 4096, 2048], P('section', 'ctx', 'tp'), may hold values from -60 to 60
- key_rows: bfloat16 [4, 4096, 512], P('section', 'ctx', 'tp'), may hold values from -7 to 7
- value_rows: bfloat16 [4, 4096, 512], P('section', 'ctx', 'tp'), may hold values from -5 to 5
- out_grad: bfloat16 [4, 4096, 4096], P('section', ('ctx', 'tp')), may hold values from -6 to 6
- query_weight: bfloat16 [4, 4096, 2048], P('section', None, 'tp'), may hold values from -0.09375 to 0.09375
- key_weight: bfloat16 [4, 4096, 512], P('section', None, 'tp'), may hold values from -0.09375 to 0.09375
- value_weight: bfloat16 [4, 4096, 512], P('section', None, 'tp'), may hold values from -0.09375 to 0.09375
- output_weight: bfloat16 [4, 2048, 4096], P('section', 'tp'), may hold values from -0.125 to 0.125
Outputs:
- sent_grad: bfloat16 [4, 4096, 4096], P('section', ('ctx', 'tp'))
- key_grad: bfloat16 [4, 4096, 512], P('section', 'ctx', 'tp')
- value_grad: bfloat16 [4, 4096, 512], P('section', 'ctx', 'tp')
The draws below stay inside these ranges and needn't reach their ends.
Inputs may be any that keep to these rules, and one draw needn't show every extreme that they name: `stretch_order`: row c lists the ids of the two blocks of 256 consecutive positions stored, in that order, at ctx index c; the two ids of a row sum to 15 and every id occurs once.
All inputs are finite; a program needn't handle non-finite values.
Results may differ from the reference program's by a relative error of at most 0.015.
Values may be sent and summed in bfloat16 or wider, within the bound.
No kernel may reach another device: no remote copies, remote signals or barrier semaphores. Data moves between devices by JAX's collectives and lax.ppermute only.
A program may use at most 128 MiB of HBM per device.

```python
import jax
import jax.numpy as jnp
from jax import lax

D = 4096
HD = 128
HQ = 16
KV = 4
TOK_DEV = 512
TOKENS = 4096
SECTIONS = 4
N_CTX = 8
N_TP = 4


def draw_stretch_order(key, part):
    key_perm, key_flip = jax.random.split(jax.random.fold_in(key, 77))
    first = jax.random.permutation(key_perm, N_CTX).astype(jnp.int32)
    second = (2 * N_CTX - 1 - first).astype(jnp.int32)
    flip = jax.random.randint(key_flip, (N_CTX,), 0, 2)
    left = jnp.where(flip == 1, second, first)
    right = jnp.where(flip == 1, first, second)
    return jnp.stack([left, right], axis=1).astype(jnp.int32)


def query_key_pair(key):
    base = jax.random.fold_in(key, 4242)
    key_q, key_k = jax.random.split(base, 2)
    shape_k = (SECTIONS, TOKENS, KV, HD)
    shape_q = (SECTIONS, TOKENS, HQ, HD)
    keys_out = jnp.clip(jax.random.normal(key_k, shape_k, jnp.float32), -4.0, 4.0)
    queries_out = jnp.clip(jax.random.normal(key_q, shape_q, jnp.float32), -4.0, 4.0)
    return (queries_out.reshape(SECTIONS, TOKENS, HQ * HD), keys_out.reshape(SECTIONS, TOKENS, KV * HD))


def draw_queries(key, part):
    return query_key_pair(key)[0].astype(jnp.bfloat16)


def draw_key_rows(key, part):
    return query_key_pair(key)[1].astype(jnp.bfloat16)


def block_levels(rng, extent, cuts, low, high):
    def one(position, shards_of):
        heights = jax.random.uniform(jax.random.fold_in(jax.random.fold_in(rng, 6), position), (shards_of,), jnp.float32, low / len(cuts), high / len(cuts))
        return jnp.repeat(jnp.exp(heights), extent[position] // shards_of).reshape((-1,) + (1,) * (len(extent) - position - 1))

    factor_of = one(*cuts[0])
    for cut in cuts[1:]:
        factor_of = factor_of * one(*cut)
    return factor_of


def centred(rng, shape, deviation, reach, cuts=(), kind=jnp.bfloat16):
    loudness = block_levels(rng, shape, cuts, -0.22, 0.18) if cuts else 1.0
    values = jax.random.normal(rng, shape, jnp.float32) * deviation * loudness
    return jnp.minimum(jnp.maximum(values, -reach), reach).astype(kind)


def setup_inputs(seed: int = 0) -> dict:
    seeds = jax.random.split(jax.random.key(seed), 10)
    stretch_order = draw_stretch_order(jax.random.fold_in(seeds[9], 71), 0)
    queries = draw_queries(jax.random.fold_in(seeds[9], 71), 0)
    key_rows = draw_key_rows(jax.random.fold_in(seeds[9], 71), 0)
    value_rows = centred(seeds[3], (SECTIONS, TOKENS, KV * HD), 1.0, 5.0, ((0, 4), (1, 8), (2, 4)))
    out_grad = centred(seeds[4], (SECTIONS, TOKENS, D), 1.0, 6.0, ((0, 4), (1, 32)))
    query_weight = centred(seeds[5], (SECTIONS, D, HQ * HD), D ** -0.5, 0.09375, ((0, 4), (2, 4)))
    key_weight = centred(seeds[6], (SECTIONS, D, KV * HD), D ** -0.5, 0.09375, ((0, 4), (2, 4)))
    value_weight = centred(seeds[7], (SECTIONS, D, KV * HD), D ** -0.5, 0.09375, ((0, 4), (2, 4)))
    output_weight = centred(seeds[8], (SECTIONS, HQ * HD, D), (HQ * HD) ** -0.5, 0.125, ((0, 4), (1, 4)))
    return {"stretch_order": stretch_order, "queries": queries, "key_rows": key_rows, "value_rows": value_rows, "out_grad": out_grad, "query_weight": query_weight, "key_weight": key_weight, "value_weight": value_weight, "output_weight": output_weight}


def token_positions(stretch_order):
    block_len = TOK_DEV // 2
    row_ids = jnp.arange(N_CTX * TOK_DEV, dtype=jnp.int32)
    flat_order = stretch_order.reshape(-1).astype(jnp.int32)
    return flat_order[row_ids // block_len] * block_len + row_ids % block_len


def section_grads(visible, queries, key_rows, value_rows, out_grad, query_weight, key_weight, value_weight, output_weight):
    score_scale = HD ** -0.5
    group_len = HQ // KV
    attn_grad = jnp.dot(out_grad, output_weight.T, preferred_element_type=jnp.float32).astype(jnp.bfloat16)

    def per_group(kv_idx):
        keys_head = lax.dynamic_slice_in_dim(key_rows, (kv_idx * HD).astype(jnp.int32), HD, 1)
        values_head = lax.dynamic_slice_in_dim(value_rows, (kv_idx * HD).astype(jnp.int32), HD, 1)

        def per_head(head_idx):
            column = ((kv_idx * group_len + head_idx) * HD).astype(jnp.int32)
            query_head = lax.dynamic_slice_in_dim(queries, column, HD, 1)
            grad_head = lax.dynamic_slice_in_dim(attn_grad, column, HD, 1)
            scores = jnp.dot(query_head, keys_head.T, preferred_element_type=jnp.float32) * score_scale
            grad_probs = jnp.dot(grad_head, values_head.T, preferred_element_type=jnp.float32)
            masked = jnp.where(visible, scores, -jnp.inf)
            lse = jax.nn.logsumexp(masked, axis=1)
            probs = jnp.where(visible, jnp.exp(masked - lse[:, None]), 0.0)
            delta = jnp.sum(probs * grad_probs, axis=1)
            dscore = probs * (grad_probs - delta[:, None])
            probs_low = probs.astype(jnp.bfloat16)
            dscore_low = dscore.astype(jnp.bfloat16)
            query_part = jnp.dot(dscore_low, keys_head, preferred_element_type=jnp.float32) * score_scale
            key_part = jnp.dot(dscore_low.T, query_head, preferred_element_type=jnp.float32) * score_scale
            value_part = jnp.dot(probs_low.T, grad_head, preferred_element_type=jnp.float32)
            return query_part, key_part, value_part

        query_parts, key_parts, value_parts = lax.map(per_head, jnp.arange(group_len, dtype=jnp.int32))
        return query_parts, jnp.sum(key_parts, axis=0), jnp.sum(value_parts, axis=0)

    query_all, key_all, value_all = lax.map(per_group, jnp.arange(KV, dtype=jnp.int32))
    seq_len = queries.shape[0]
    query_grad = jnp.transpose(query_all, (2, 0, 1, 3)).reshape(seq_len, HQ * HD).astype(jnp.bfloat16)
    key_grad = jnp.transpose(key_all, (1, 0, 2)).reshape(seq_len, KV * HD).astype(jnp.bfloat16)
    value_grad = jnp.transpose(value_all, (1, 0, 2)).reshape(seq_len, KV * HD).astype(jnp.bfloat16)
    head_cols = HQ * HD // N_TP
    kv_cols = KV * HD // N_TP
    summed = jnp.zeros((seq_len, D), jnp.float32)
    for member in range(N_TP):
        qa, qb = member * head_cols, (member + 1) * head_cols
        ka, kb = member * kv_cols, (member + 1) * kv_cols
        term = jnp.dot(query_grad[:, qa:qb], query_weight[:, qa:qb].T, preferred_element_type=jnp.float32)
        term = term + jnp.dot(key_grad[:, ka:kb], key_weight[:, ka:kb].T, preferred_element_type=jnp.float32)
        term = term + jnp.dot(value_grad[:, ka:kb], value_weight[:, ka:kb].T, preferred_element_type=jnp.float32)
        rounded = lax.optimization_barrier(term.astype(jnp.bfloat16))
        summed = summed + rounded.astype(jnp.float32)
    return summed.astype(jnp.bfloat16), key_grad, value_grad


def reference(stretch_order, queries, key_rows, value_rows, out_grad, query_weight, key_weight, value_weight, output_weight):
    positions = token_positions(stretch_order)
    visible = positions[None, :] <= positions[:, None]
    input_list = []
    key_list = []
    value_list = []
    for section_idx in range(SECTIONS):
        input_grad, key_grad, value_grad = section_grads(visible, queries[section_idx], key_rows[section_idx], value_rows[section_idx], out_grad[section_idx], query_weight[section_idx], key_weight[section_idx], value_weight[section_idx], output_weight[section_idx])
        input_list.append(input_grad)
        key_list.append(key_grad)
        value_list.append(value_grad)
    sent_grad = jnp.roll(jnp.stack(input_list), -1, axis=0)
    return sent_grad, jnp.stack(key_list), jnp.stack(value_list)
```

```python
import jax
import jax.numpy as jnp
from jax import lax
from jax.experimental import pallas as pl
from jax.experimental.pallas import tpu as pltpu
from jax.sharding import PartitionSpec as P

HD = 128
BLK = 256
GROUP = 4
STEPS = 17
SCALE = HD ** (-0.5)
EXP2_SCALE = SCALE * 1.4426950408889634
NEG_LARGE = -1e30


def dot_nt(lhs, rhs):
    return lax.dot_general(lhs, rhs, (((1,), (1,)), ((), ())), preferred_element_type=jnp.float32)


def dot_nn(lhs, rhs):
    return lax.dot_general(lhs, rhs, (((1,), (0,)), ((), ())), preferred_element_type=jnp.float32)


def ring(size, shift):
    return [(i, (i + shift) % size) for i in range(size)]


def z_ring(shift):
    return [(x * 4 + z, x * 4 + (z + shift) % 4) for x in range(2) for z in range(4)]


X_SWAP = [(x * 4 + z, (1 - x) * 4 + z) for x in range(2) for z in range(4)]


def joint_ring(shift):
    return [(s * 4 + t, ((s - 1) % 4) * 4 + (t + shift) % 4) for s in range(4) for t in range(4)]


def step_block(step, split):
    half = (step > split).astype(jnp.int32)
    return half, step - half * (split + 1)


def forward_kernel(split_ref, ids_ref, *refs):
    kv_refs = refs[:8]
    q_ref, p_ref, out_ref, stat_ref, hist_ref, kvs_ref, max_ref, acc_ref = refs[8:]
    step = pl.program_id(0)
    split = split_ref[0]
    half, kb = step_block(step, split)
    diag = (step == split) | (step == STEPS - 1)

    @pl.when(step == 0)
    def _():
        for j in range(8):
            for r in range(2):
                kvs_ref[ids_ref[2 * j + r]] = kv_refs[j][r * BLK : (r + 1) * BLK, :]

    @pl.when(kb == 0)
    def _():
        max_ref[...] = jnp.full_like(max_ref, NEG_LARGE)
        acc_ref[...] = jnp.zeros_like(acc_ref)

    key_blk = kvs_ref[kb, :, :HD]
    value_t = jnp.transpose(kvs_ref[kb, :, HD:].astype(jnp.float32)).astype(jnp.bfloat16)
    lhs = jnp.concatenate([value_t, jnp.ones((16, BLK), jnp.bfloat16)], axis=0)
    gap = lax.broadcasted_iota(jnp.int32, (BLK, BLK), 0) - lax.broadcasted_iota(
        jnp.int32, (BLK, BLK), 1
    )
    visible = gap <= jnp.where(diag, 0, BLK)
    for h in range(GROUP):
        cols = slice(h * BLK, (h + 1) * BLK)
        scores = dot_nt(key_blk, q_ref[:, h * HD : (h + 1) * HD])
        scores = jnp.where(visible, scores, NEG_LARGE)
        old_max = max_ref[0:1, cols]
        new_max = jnp.maximum(old_max, jnp.max(scores, axis=0, keepdims=True))
        probs = jnp.exp2((scores - new_max) * EXP2_SCALE).astype(jnp.bfloat16)
        p_ref[0, h] = probs
        factor = jnp.exp2((old_max - new_max) * EXP2_SCALE)
        acc_ref[:, cols] = acc_ref[:, cols] * factor + dot_nn(lhs, probs)
        max_ref[0:1, cols] = new_max
        hist_ref[0, 0:1, cols] = new_max

    @pl.when(diag)
    def _():
        inv = 1.0 / acc_ref[HD : HD + 1, :]
        out_ref[0] = acc_ref[:HD, :] * inv
        stat_ref[0, 0:1, :] = max_ref[0:1, :]
        stat_ref[0, 1:2, :] = inv


def forward_call(split, ids, kv_chunks, queries):
    def half_of(step, split_ref):
        return (step > split_ref[0]).astype(jnp.int32)

    whole = pl.BlockSpec((2 * BLK, 2 * HD), lambda i, s, d: (0, 0))
    wide = GROUP * BLK
    return pl.pallas_call(
        forward_kernel,
        grid_spec=pltpu.PrefetchScalarGridSpec(
            num_scalar_prefetch=2,
            grid=(STEPS,),
            in_specs=[whole] * 8
            + [pl.BlockSpec((BLK, GROUP * HD), lambda i, s, d: (half_of(i, s), 0))],
            out_specs=[
                pl.BlockSpec((1, GROUP, BLK, BLK), lambda i, s, d: (i, 0, 0, 0)),
                pl.BlockSpec((1, HD, wide), lambda i, s, d: (half_of(i, s), 0, 0)),
                pl.BlockSpec((1, 8, wide), lambda i, s, d: (half_of(i, s), 0, 0)),
                pl.BlockSpec((1, 1, wide), lambda i, s, d: (i, 0, 0)),
                pl.BlockSpec((16, BLK, 2 * HD), lambda i, s, d: (0, 0, 0)),
            ],
            scratch_shapes=[
                pltpu.VMEM((8, wide), jnp.float32),
                pltpu.VMEM((HD + 16, wide), jnp.float32),
            ],
        ),
        out_shape=[
            jax.ShapeDtypeStruct((STEPS, GROUP, BLK, BLK), jnp.bfloat16),
            jax.ShapeDtypeStruct((2, HD, wide), jnp.float32),
            jax.ShapeDtypeStruct((2, 8, wide), jnp.float32),
            jax.ShapeDtypeStruct((STEPS, 1, wide), jnp.float32),
            jax.ShapeDtypeStruct((16, BLK, 2 * HD), jnp.bfloat16),
        ],
        cost_estimate=pl.CostEstimate(
            flops=2 * 2 * STEPS * wide * BLK * HD,
            bytes_accessed=13 << 20,
            transcendentals=STEPS * wide * BLK,
        ),
        name="attn_forward",
    )(split, ids, *kv_chunks, queries)


def backward_kernel(split_ref, ids_ref, rows_ref, *refs):
    grad_refs = refs[:4]
    (
        p_ref, kv_ref, q_ref, out_ref, stat_ref, hist_ref,
        dq_ref, g0_ref, g1_ref, g2_ref, g3_ref,
        grad_ref, delta_ref, dqt_ref, dkv_ref,
    ) = refs[4:]
    step = pl.program_id(0)
    split = split_ref[0]
    half, kb = step_block(step, split)
    diag = (step == split) | (step == STEPS - 1)

    @pl.when(step == 0)
    def _():
        for j in range(4):
            row = pl.multiple_of(rows_ref[j] * 128, 128)
            grad_ref[pl.ds(row, 128), :] = grad_refs[j][...]
        dkv_ref[...] = jnp.zeros_like(dkv_ref)

    start = pl.multiple_of(half * BLK, BLK)

    @pl.when(kb == 0)
    def _():
        dqt_ref[...] = jnp.zeros_like(dqt_ref)
        for h in range(GROUP):
            cols = slice(h * BLK, (h + 1) * BLK)
            grad = grad_ref[pl.ds(start, BLK), h * HD : (h + 1) * HD]
            grad_t = jnp.transpose(grad.astype(jnp.float32))
            delta_ref[0:1, cols] = jnp.sum(out_ref[0, :, cols] * grad_t, axis=0, keepdims=True)

    key_blk = kv_ref[0, :, :HD]
    value_blk = kv_ref[0, :, HD:]
    key_t = jnp.transpose(key_blk.astype(jnp.float32)).astype(jnp.bfloat16)
    dk = jnp.zeros((BLK, HD), jnp.float32)
    dv = jnp.zeros((BLK, HD), jnp.float32)
    for h in range(GROUP):
        cols = slice(h * BLK, (h + 1) * BLK)
        heads = slice(h * HD, (h + 1) * HD)
        grad = grad_ref[pl.ds(start, BLK), heads]
        grad_probs = dot_nt(value_blk, grad)
        norm = (
            jnp.exp2((hist_ref[0, 0:1, cols] - stat_ref[0, 0:1, cols]) * EXP2_SCALE)
            * stat_ref[0, 1:2, cols]
        )
        probs = p_ref[0, h].astype(jnp.float32) * norm
        dscore = (probs * (grad_probs - delta_ref[0:1, cols])).astype(jnp.bfloat16)
        dv = dv + dot_nn(probs.astype(jnp.bfloat16), grad)
        dk = dk + dot_nn(dscore, q_ref[:, heads])
        dqt_ref[:, cols] += dot_nn(key_t, dscore)
    dkv_ref[kb, :, :HD] += dk
    dkv_ref[kb, :, HD:] += dv

    @pl.when(diag)
    def _():
        for h in range(GROUP):
            cols = slice(h * BLK, (h + 1) * BLK)
            dq_ref[:, h * HD : (h + 1) * HD] = jnp.transpose(dqt_ref[:, cols] * SCALE).astype(
                jnp.bfloat16
            )

    @pl.when(step == STEPS - 1)
    def _():
        for g, g_ref in enumerate((g0_ref, g1_ref, g2_ref, g3_ref)):
            for x in range(2):
                for r in range(2):
                    block = ids_ref[4 * g + 2 * x + r]
                    rows = slice(r * BLK, (r + 1) * BLK)
                    g_ref[x, rows, :HD] = (dkv_ref[block, :, :HD] * SCALE).astype(jnp.bfloat16)
                    g_ref[x, rows, HD:] = dkv_ref[block, :, HD:].astype(jnp.bfloat16)


def backward_call(split, ids, rows, grad_chunks, saved, queries):
    probs, outs, stats, hist, kv_sorted = saved

    def half_of(step, split_ref):
        return (step > split_ref[0]).astype(jnp.int32)

    def block_of(step, split_ref):
        return step - half_of(step, split_ref) * (split_ref[0] + 1)

    wide = GROUP * BLK
    group_spec = pl.BlockSpec((2, 2 * BLK, 2 * HD), lambda i, s, d, w: (0, 0, 0))
    group_shape = jax.ShapeDtypeStruct((2, 2 * BLK, 2 * HD), jnp.bfloat16)
    return pl.pallas_call(
        backward_kernel,
        grid_spec=pltpu.PrefetchScalarGridSpec(
            num_scalar_prefetch=3,
            grid=(STEPS,),
            in_specs=[pl.BlockSpec((128, GROUP * HD), lambda i, s, d, w: (0, 0))] * 4
            + [
                pl.BlockSpec((1, GROUP, BLK, BLK), lambda i, s, d, w: (i, 0, 0, 0)),
                pl.BlockSpec((1, BLK, 2 * HD), lambda i, s, d, w: (block_of(i, s), 0, 0)),
                pl.BlockSpec((BLK, GROUP * HD), lambda i, s, d, w: (half_of(i, s), 0)),
                pl.BlockSpec((1, HD, wide), lambda i, s, d, w: (half_of(i, s), 0, 0)),
                pl.BlockSpec((1, 8, wide), lambda i, s, d, w: (half_of(i, s), 0, 0)),
                pl.BlockSpec((1, 1, wide), lambda i, s, d, w: (i, 0, 0)),
            ],
            out_specs=[pl.BlockSpec((BLK, GROUP * HD), lambda i, s, d, w: (half_of(i, s), 0))]
            + [group_spec] * 4,
            scratch_shapes=[
                pltpu.VMEM((2 * BLK, GROUP * HD), jnp.bfloat16),
                pltpu.VMEM((8, wide), jnp.float32),
                pltpu.VMEM((HD, wide), jnp.float32),
                pltpu.VMEM((16, BLK, 2 * HD), jnp.float32),
            ],
        ),
        out_shape=[jax.ShapeDtypeStruct((2 * BLK, GROUP * HD), jnp.bfloat16)] + [group_shape] * 4,
        cost_estimate=pl.CostEstimate(
            flops=2 * 4 * STEPS * wide * BLK * HD,
            bytes_accessed=16 << 20,
            transcendentals=0,
        ),
        name="attn_backward",
    )(split, ids, rows, *grad_chunks, probs, kv_sorted, queries, outs, stats, hist)


def per_device(
    stretch_order,
    queries,
    key_rows,
    value_rows,
    out_grad,
    query_weight,
    key_weight,
    value_weight,
    output_weight,
):
    send = lax.ppermute
    tp = lax.axis_index("tp")
    ctx = lax.axis_index("ctx")
    own_x, own_z = ctx // 4, ctx % 4
    bf16 = jnp.bfloat16

    chunk = out_grad[0]
    half_rows = chunk.shape[0] // 2
    top, low = chunk[:half_rows], chunk[half_rows:]
    left_top = send(top, "tp", ring(4, 1))
    right_low = send(low, "tp", ring(4, -1))
    left_low = send(low, "tp", ring(4, 1))
    right_top = send(top, "tp", ring(4, -1))
    far_top = send(left_top, "tp", ring(4, 1))
    far_low = send(right_low, "tp", ring(4, -1))

    kv_own = jnp.concatenate([key_rows[0], value_rows[0]], axis=1)
    kv_pair = send(kv_own, "ctx", X_SWAP)
    kv_chunks = [kv_own, kv_pair]
    for shift in (-1, 2, 1):
        kv_chunks.append(send(kv_own, "ctx", z_ring(shift)))
        kv_chunks.append(send(kv_pair, "ctx", z_ring(shift)))

    index = jnp.arange(8, dtype=jnp.int32)
    source = ((own_x + index % 2) % 2) * 4 + (own_z + index // 2) % 4
    table = jnp.arange(8, dtype=jnp.int32)
    ids = jnp.sum(
        jnp.where(source[:, None, None] == table[None, :, None], stretch_order[None], 0), axis=1
    ).reshape(16)
    split = ids[:1]
    saved = forward_call(split, ids, kv_chunks, queries[0])

    out_weight = output_weight[0]

    def grad_of(rows):
        return dot_nt(rows, out_weight).astype(bf16)

    grad_chunks = [
        grad_of(chunk),
        grad_of(jnp.concatenate([left_top, left_low], axis=0)),
        grad_of(jnp.concatenate([right_top, right_low], axis=0)),
        grad_of(jnp.concatenate([far_top, far_low], axis=0)),
    ]
    rows = jnp.stack([tp, (tp + 3) % 4, (tp + 1) % 4, (tp + 2) % 4]).astype(jnp.int32)
    query_grad, *groups = backward_call(split, ids, rows, grad_chunks, saved, queries[0])

    f32 = jnp.float32
    summed = groups[0].astype(f32)
    for distance, shift in ((1, 1), (2, 2), (3, -1)):
        summed = summed + send(groups[distance], "ctx", z_ring(shift)).astype(f32)
    from_pair = send(summed[1].astype(bf16), "ctx", X_SWAP)
    kv_grad = (summed[0] + from_pair.astype(f32)).astype(bf16)

    stacked = jnp.concatenate([query_grad, kv_grad], axis=1)
    weights = jnp.concatenate([query_weight[0], key_weight[0], value_weight[0]], axis=1)

    def term_of(distance):
        start = ((tp + distance) % 4) * 128
        return dot_nt(lax.dynamic_slice_in_dim(stacked, start, 128, 0), weights).astype(bf16)

    far = term_of(2)
    from_left = send(far[:half_rows], "tp", ring(4, 1))
    from_right = send(far[half_rows:], "tp", ring(4, -1))
    right = term_of(1)
    left = term_of(3)
    joint = ("section", "tp")
    low_a = send(right[half_rows:], joint, joint_ring(1))
    top_b = send(left[:half_rows], joint, joint_ring(-1))
    own = send(term_of(0), "section", ring(4, -1))
    top_a = send(
        (right[:half_rows].astype(f32) + from_left.astype(f32)).astype(bf16), joint, joint_ring(1)
    )
    low_b = send(
        (left[half_rows:].astype(f32) + from_right.astype(f32)).astype(bf16), joint, joint_ring(-1)
    )
    sent = jnp.concatenate(
        [
            own[:half_rows].astype(f32) + top_a.astype(f32) + top_b.astype(f32),
            own[half_rows:].astype(f32) + low_a.astype(f32) + low_b.astype(f32),
        ],
        axis=0,
    ).astype(bf16)
    return (sent[None], kv_grad[None, :, :HD], kv_grad[None, :, HD:])


def solution(mesh):
    placed = (
        P(),
        P("section", "ctx", "tp"),
        P("section", "ctx", "tp"),
        P("section", "ctx", "tp"),
        P("section", ("ctx", "tp"), None),
        P("section", None, "tp"),
        P("section", None, "tp"),
        P("section", None, "tp"),
        P("section", "tp", None),
    )
    return jax.shard_map(
        per_device,
        mesh=mesh,
        in_specs=placed,
        out_specs=(
            P("section", ("ctx", "tp"), None),
            P("section", "ctx", "tp"),
            P("section", "ctx", "tp"),
        ),
        check_vma=False,
    )
```

```python
import jax
import jax.numpy as jnp
from jax import lax
from jax.experimental import pallas as pl
from jax.experimental.pallas import tpu as pltpu
from jax.sharding import PartitionSpec as P

HD = 128
BLK = 256
GROUP = 4
STEPS = 17
SCALE = HD ** (-0.5)
EXP2_SCALE = SCALE * 1.4426950408889634
NEG_LARGE = -1e30

VMEM_WHOLE = pl.BlockSpec(memory_space=pltpu.VMEM)
PARAMS = pltpu.CompilerParams(vmem_limit_bytes=36 << 20)


def dot_nt(lhs, rhs):
    return lax.dot_general(lhs, rhs, (((1,), (1,)), ((), ())), preferred_element_type=jnp.float32)


def dot_nn(lhs, rhs):
    return lax.dot_general(lhs, rhs, (((1,), (0,)), ((), ())), preferred_element_type=jnp.float32)


def ring(size, shift):
    return [(i, (i + shift) % size) for i in range(size)]


def z_ring(shift):
    return [(x * 4 + z, x * 4 + (z + shift) % 4) for x in range(2) for z in range(4)]


X_SWAP = [(x * 4 + z, (1 - x) * 4 + z) for x in range(2) for z in range(4)]


def joint_ring(shift):
    return [(s * 4 + t, ((s - 1) % 4) * 4 + (t + shift) % 4) for s in range(4) for t in range(4)]


def step_block(step, split):
    half = (step > split).astype(jnp.int32)
    return half, step - half * (split + 1)


def step_args(step, split):
    half, kb = step_block(step, split)
    diag = ((step == split) | (step == STEPS - 1)).astype(jnp.int32)
    return half, kb, diag


def forward_kernel(split_ref, ids_ref, *refs):
    kv_refs = refs[:8]
    (
        q_ref, p_ref, out_ref, stat_ref, hist_ref, kvs_ref,
        max_ref, acc_ref, bias_ref, even_ref, odd_ref, even_top_ref, odd_top_ref,
    ) = refs[8:]
    step = pl.program_id(0)
    split = split_ref[0]
    _, kb, diag = step_args(step, split)

    def score_step(at, score_ref, top_ref):
        at_half, at_kb, at_diag = step_args(at, split)
        start = pl.multiple_of(at_half * BLK, BLK)
        key_blk = kvs_ref[at_kb, :, :HD]
        for h in range(GROUP):
            query = q_ref[pl.ds(start, BLK), h * HD : (h + 1) * HD]
            scores = dot_nt(key_blk, query) + bias_ref[at_diag]
            score_ref[h] = scores
            top_ref[0:1, h * BLK : (h + 1) * BLK] = jnp.max(scores, axis=0, keepdims=True)

    @pl.when(step == 0)
    def _():
        for j in range(8):
            for r in range(2):
                kvs_ref[ids_ref[2 * j + r]] = kv_refs[j][r * BLK : (r + 1) * BLK, :]
        gap = lax.broadcasted_iota(jnp.int32, (BLK, BLK), 0) - lax.broadcasted_iota(
            jnp.int32, (BLK, BLK), 1
        )
        bias_ref[0] = jnp.zeros((BLK, BLK), jnp.float32)
        bias_ref[1] = jnp.where(gap <= 0, 0.0, NEG_LARGE)
        max_ref[...] = jnp.full_like(max_ref, NEG_LARGE)
        acc_ref[...] = jnp.zeros_like(acc_ref)
        score_step(step, even_ref, even_top_ref)

    def softmax_step(now, now_top, later, later_top):
        score_step(jnp.minimum(step + 1, STEPS - 1), later, later_top)
        value_t = jnp.transpose(kvs_ref[kb, :, HD:].astype(jnp.float32)).astype(jnp.bfloat16)
        lhs = jnp.concatenate([value_t, jnp.ones((16, BLK), jnp.bfloat16)], axis=0)
        for h in range(GROUP):
            cols = slice(h * BLK, (h + 1) * BLK)
            old_max = jnp.where(kb == 0, NEG_LARGE, max_ref[0:1, cols])
            new_max = jnp.maximum(old_max, now_top[0:1, cols])
            probs = jnp.exp2((now[h] - new_max) * EXP2_SCALE).astype(jnp.bfloat16)
            p_ref[step, h] = probs
            factor = jnp.exp2((old_max - new_max) * EXP2_SCALE)
            acc_ref[:, cols] = acc_ref[:, cols] * factor + dot_nn(lhs, probs)
            max_ref[0:1, cols] = new_max
            hist_ref[0, 0:1, cols] = new_max

    @pl.when(step % 2 == 0)
    def _():
        softmax_step(even_ref, even_top_ref, odd_ref, odd_top_ref)

    @pl.when(step % 2 == 1)
    def _():
        softmax_step(odd_ref, odd_top_ref, even_ref, even_top_ref)

    @pl.when(diag == 1)
    def _():
        inv = 1.0 / acc_ref[HD : HD + 1, :]
        out_ref[0] = acc_ref[:HD, :] * inv
        stat_ref[0, 0:1, :] = max_ref[0:1, :]
        stat_ref[0, 1:2, :] = inv


def half_of(step, split_ref):
    return (step > split_ref[0]).astype(jnp.int32)


def block_of(step, split_ref):
    return step - half_of(step, split_ref) * (split_ref[0] + 1)


def forward_call(split, ids, kv_chunks, queries):
    whole = pl.BlockSpec((2 * BLK, 2 * HD), lambda i, s, d: (0, 0))
    wide = GROUP * BLK
    return pl.pallas_call(
        forward_kernel,
        grid_spec=pltpu.PrefetchScalarGridSpec(
            num_scalar_prefetch=2,
            grid=(STEPS,),
            in_specs=[whole] * 8 + [pl.BlockSpec((2 * BLK, GROUP * HD), lambda i, s, d: (0, 0))],
            out_specs=[
                VMEM_WHOLE,
                pl.BlockSpec((1, HD, wide), lambda i, s, d: (half_of(i, s), 0, 0)),
                pl.BlockSpec((1, 8, wide), lambda i, s, d: (half_of(i, s), 0, 0)),
                pl.BlockSpec((1, 1, wide), lambda i, s, d: (i, 0, 0)),
                pl.BlockSpec((16, BLK, 2 * HD), lambda i, s, d: (0, 0, 0)),
            ],
            scratch_shapes=[
                pltpu.VMEM((8, wide), jnp.float32),
                pltpu.VMEM((HD + 16, wide), jnp.float32),
                pltpu.VMEM((2, BLK, BLK), jnp.float32),
                pltpu.VMEM((GROUP, BLK, BLK), jnp.float32),
                pltpu.VMEM((GROUP, BLK, BLK), jnp.float32),
                pltpu.VMEM((8, wide), jnp.float32),
                pltpu.VMEM((8, wide), jnp.float32),
            ],
        ),
        out_shape=[
            jax.ShapeDtypeStruct((STEPS, GROUP, BLK, BLK), jnp.bfloat16),
            jax.ShapeDtypeStruct((2, HD, wide), jnp.float32),
            jax.ShapeDtypeStruct((2, 8, wide), jnp.float32),
            jax.ShapeDtypeStruct((STEPS, 1, wide), jnp.float32),
            jax.ShapeDtypeStruct((16, BLK, 2 * HD), jnp.bfloat16),
        ],
        compiler_params=PARAMS,
        cost_estimate=pl.CostEstimate(
            flops=2 * 2 * STEPS * wide * BLK * HD,
            bytes_accessed=13 << 20,
            transcendentals=STEPS * wide * BLK,
        ),
        name="attn_forward",
    )(split, ids, *kv_chunks, queries)


def grad_kernel(rows_ref, *refs):
    pieces = refs[:5]
    weight_ref, out_ref, lhs_ref, acc_ref = refs[5:]
    step = pl.program_id(0)
    depth = lhs_ref.shape[1]

    @pl.when(step == 0)
    def _():
        acc_ref[...] = jnp.zeros_like(acc_ref)

    for j, piece in enumerate(pieces):
        size = piece.shape[0]
        lhs_ref[pl.ds(pl.multiple_of(rows_ref[j], 64), size), :] = piece[...]
    start = pl.multiple_of(step * depth, depth)
    acc_ref[...] += dot_nt(lhs_ref[...], weight_ref[:, pl.ds(start, depth)])

    @pl.when(step == pl.num_programs(0) - 1)
    def _():
        out_ref[...] = acc_ref[...].astype(jnp.bfloat16)


def grad_call(rows, pieces, out_weight):
    depth = 512
    total = out_weight.shape[0]
    return pl.pallas_call(
        grad_kernel,
        grid_spec=pltpu.PrefetchScalarGridSpec(
            num_scalar_prefetch=1,
            grid=(out_weight.shape[1] // depth,),
            in_specs=[pl.BlockSpec((p.shape[0], depth), lambda i, w: (0, i)) for p in pieces]
            + [VMEM_WHOLE],
            out_specs=pl.BlockSpec((2 * BLK, total), lambda i, w: (0, 0)),
            scratch_shapes=[
                pltpu.VMEM((2 * BLK, depth), jnp.bfloat16),
                pltpu.VMEM((2 * BLK, total), jnp.float32),
            ],
        ),
        out_shape=jax.ShapeDtypeStruct((2 * BLK, total), jnp.bfloat16),
        compiler_params=PARAMS,
        cost_estimate=pl.CostEstimate(
            flops=2 * 2 * BLK * total * out_weight.shape[1],
            bytes_accessed=9 << 20,
            transcendentals=0,
        ),
        name="attn_grad",
    )(rows, *pieces, out_weight)


def norm_of(hist_ref, stat_ref, cols):
    gap = (hist_ref[0, 0:1, cols] - stat_ref[0, 0:1, cols]) * EXP2_SCALE
    return jnp.exp2(gap) * stat_ref[0, 1:2, cols]


def write_groups(ids_ref, total_ref, group_refs, scale):
    for g, g_ref in enumerate(group_refs):
        for x in range(2):
            for r in range(2):
                block = ids_ref[4 * g + 2 * x + r]
                g_ref[x, r * BLK : (r + 1) * BLK, :] = (total_ref[block] * scale).astype(
                    jnp.bfloat16
                )


def value_kernel(split_ref, ids_ref, grad_ref, p_ref, stat_ref, hist_ref, *refs):
    group_refs = refs[:4]
    total_ref = refs[4]
    step = pl.program_id(0)
    half, kb, _ = step_args(step, split_ref[0])

    @pl.when(step == 0)
    def _():
        total_ref[...] = jnp.zeros_like(total_ref)

    start = pl.multiple_of(half * BLK, BLK)
    dv = jnp.zeros((BLK, HD), jnp.float32)
    for h in range(GROUP):
        norm = norm_of(hist_ref, stat_ref, slice(h * BLK, (h + 1) * BLK))
        probs = (p_ref[step, h].astype(jnp.float32) * norm).astype(jnp.bfloat16)
        dv = dv + dot_nn(probs, grad_ref[pl.ds(start, BLK), h * HD : (h + 1) * HD])
    total_ref[kb] += dv

    @pl.when(step == STEPS - 1)
    def _():
        write_groups(ids_ref, total_ref, group_refs, 1.0)


def value_call(split, ids, grad, saved):
    probs, _, stats, hist, _ = saved
    wide = GROUP * BLK
    group_spec = pl.BlockSpec((2, 2 * BLK, HD), lambda i, s, d: (0, 0, 0))
    return pl.pallas_call(
        value_kernel,
        grid_spec=pltpu.PrefetchScalarGridSpec(
            num_scalar_prefetch=2,
            grid=(STEPS,),
            in_specs=[
                pl.BlockSpec((2 * BLK, GROUP * HD), lambda i, s, d: (0, 0)),
                VMEM_WHOLE,
                pl.BlockSpec((1, 8, wide), lambda i, s, d: (half_of(i, s), 0, 0)),
                pl.BlockSpec((1, 1, wide), lambda i, s, d: (i, 0, 0)),
            ],
            out_specs=[group_spec] * 4,
            scratch_shapes=[pltpu.VMEM((16, BLK, HD), jnp.float32)],
        ),
        out_shape=[jax.ShapeDtypeStruct((2, 2 * BLK, HD), jnp.bfloat16)] * 4,
        compiler_params=PARAMS,
        cost_estimate=pl.CostEstimate(
            flops=2 * STEPS * wide * BLK * HD, bytes_accessed=11 << 20, transcendentals=0
        ),
        name="attn_value_grad",
    )(split, ids, grad, probs, stats, hist)


def key_kernel(split_ref, ids_ref, grad_ref, q_ref, p_ref, kv_ref, next_ref, out_ref, stat_ref,
               hist_ref, *refs):
    dq_ref = refs[0]
    group_refs = refs[1:5]
    delta_ref, dqt_ref, total_ref, even_ref, odd_ref = refs[5:]
    step = pl.program_id(0)
    split = split_ref[0]
    half, kb, diag = step_args(step, split)

    def grad_probs_step(at, value_blk, gp_ref):
        at_half = (at > split).astype(jnp.int32)
        start = pl.multiple_of(at_half * BLK, BLK)
        for h in range(GROUP):
            gp_ref[h] = dot_nt(
                value_blk, grad_ref[pl.ds(start, BLK), h * HD : (h + 1) * HD]
            )

    @pl.when(step == 0)
    def _():
        total_ref[...] = jnp.zeros_like(total_ref)
        dqt_ref[...] = jnp.zeros_like(dqt_ref)
        grad_probs_step(step, kv_ref[0, :, HD:], even_ref)

    start = pl.multiple_of(half * BLK, BLK)

    @pl.when(kb == 0)
    def _():
        for h in range(GROUP):
            cols = slice(h * BLK, (h + 1) * BLK)
            grad = grad_ref[pl.ds(start, BLK), h * HD : (h + 1) * HD]
            grad_t = jnp.transpose(grad.astype(jnp.float32))
            delta_ref[0:1, cols] = jnp.sum(out_ref[0, :, cols] * grad_t, axis=0, keepdims=True)

    def main_step(now, later):
        grad_probs_step(jnp.minimum(step + 1, STEPS - 1), next_ref[0, :, HD:], later)
        key_t = jnp.transpose(kv_ref[0, :, :HD].astype(jnp.float32)).astype(jnp.bfloat16)
        keep = jnp.where(kb == 0, 0.0, 1.0)
        dk = jnp.zeros((BLK, HD), jnp.float32)
        for h in range(GROUP):
            cols = slice(h * BLK, (h + 1) * BLK)
            probs = p_ref[step, h].astype(jnp.float32) * norm_of(hist_ref, stat_ref, cols)
            dscore = (probs * (now[h] - delta_ref[0:1, cols])).astype(jnp.bfloat16)
            dk = dk + dot_nn(dscore, q_ref[pl.ds(start, BLK), h * HD : (h + 1) * HD])
            dqt_ref[:, cols] = dqt_ref[:, cols] * keep + dot_nn(key_t, dscore)
        total_ref[kb] += dk

    @pl.when(step % 2 == 0)
    def _():
        main_step(even_ref, odd_ref)

    @pl.when(step % 2 == 1)
    def _():
        main_step(odd_ref, even_ref)

    @pl.when(diag == 1)
    def _():
        for h in range(GROUP):
            cols = slice(h * BLK, (h + 1) * BLK)
            dq_ref[:, h * HD : (h + 1) * HD] = jnp.transpose(dqt_ref[:, cols] * SCALE).astype(
                jnp.bfloat16
            )

    @pl.when(step == STEPS - 1)
    def _():
        write_groups(ids_ref, total_ref, group_refs, SCALE)


def key_call(split, ids, grad, saved, queries):
    probs, outs, stats, hist, kv_sorted = saved
    wide = GROUP * BLK
    group_spec = pl.BlockSpec((2, 2 * BLK, HD), lambda i, s, d: (0, 0, 0))
    whole = pl.BlockSpec((2 * BLK, GROUP * HD), lambda i, s, d: (0, 0))

    def next_block(i, s, d):
        return (block_of(jnp.minimum(i + 1, STEPS - 1), s), 0, 0)

    return pl.pallas_call(
        key_kernel,
        grid_spec=pltpu.PrefetchScalarGridSpec(
            num_scalar_prefetch=2,
            grid=(STEPS,),
            in_specs=[
                whole,
                whole,
                VMEM_WHOLE,
                pl.BlockSpec((1, BLK, 2 * HD), lambda i, s, d: (block_of(i, s), 0, 0)),
                pl.BlockSpec((1, BLK, 2 * HD), next_block),
                pl.BlockSpec((1, HD, wide), lambda i, s, d: (half_of(i, s), 0, 0)),
                pl.BlockSpec((1, 8, wide), lambda i, s, d: (half_of(i, s), 0, 0)),
                pl.BlockSpec((1, 1, wide), lambda i, s, d: (i, 0, 0)),
            ],
            out_specs=[pl.BlockSpec((BLK, GROUP * HD), lambda i, s, d: (half_of(i, s), 0))]
            + [group_spec] * 4,
            scratch_shapes=[
                pltpu.VMEM((8, wide), jnp.float32),
                pltpu.VMEM((HD, wide), jnp.float32),
                pltpu.VMEM((16, BLK, HD), jnp.float32),
                pltpu.VMEM((GROUP, BLK, BLK), jnp.float32),
                pltpu.VMEM((GROUP, BLK, BLK), jnp.float32),
            ],
        ),
        out_shape=[jax.ShapeDtypeStruct((2 * BLK, GROUP * HD), jnp.bfloat16)]
        + [jax.ShapeDtypeStruct((2, 2 * BLK, HD), jnp.bfloat16)] * 4,
        compiler_params=PARAMS,
        cost_estimate=pl.CostEstimate(
            flops=2 * 3 * STEPS * wide * BLK * HD, bytes_accessed=14 << 20, transcendentals=0
        ),
        name="attn_key_grad",
    )(split, ids, grad, queries, probs, kv_sorted, kv_sorted, outs, stats, hist)


def per_device(
    stretch_order,
    queries,
    key_rows,
    value_rows,
    out_grad,
    query_weight,
    key_weight,
    value_weight,
    output_weight,
):
    send = lax.ppermute
    tp = lax.axis_index("tp")
    ctx = lax.axis_index("ctx")
    own_x, own_z = ctx // 4, ctx % 4
    bf16 = jnp.bfloat16

    kv_own = jnp.concatenate([key_rows[0], value_rows[0]], axis=1)
    kv_pair = send(kv_own, "ctx", X_SWAP)

    chunk = out_grad[0]
    half_rows = chunk.shape[0] // 2
    left_chunk = send(chunk, "tp", ring(4, 1))
    right_chunk = send(chunk, "tp", ring(4, -1))
    far_top = send(left_chunk[:half_rows], "tp", ring(4, 1))
    far_low = send(right_chunk[half_rows:], "tp", ring(4, -1))

    kv_chunks = [kv_own, kv_pair]
    for shift in (-1, 2, 1):
        kv_chunks.append(send(kv_own, "ctx", z_ring(shift)))
        kv_chunks.append(send(kv_pair, "ctx", z_ring(shift)))

    index = jnp.arange(8, dtype=jnp.int32)
    source = ((own_x + index % 2) % 2) * 4 + (own_z + index // 2) % 4
    table = jnp.arange(8, dtype=jnp.int32)
    ids = jnp.sum(
        jnp.where(source[:, None, None] == table[None, :, None], stretch_order[None], 0), axis=1
    ).reshape(16)
    split = ids[:1]
    saved = forward_call(split, ids, kv_chunks, queries[0])

    left, right, far = (tp + 3) % 4, (tp + 1) % 4, (tp + 2) % 4
    pieces = (chunk, left_chunk, right_chunk, far_top, far_low)
    places = (2 * tp, 2 * left, 2 * right, 2 * far, 2 * far + 1)
    grad = grad_call(
        (jnp.stack(places) * half_rows).astype(jnp.int32), pieces, output_weight[0]
    )

    f32 = jnp.float32

    def along_z(groups):
        total = groups[0].astype(f32)
        for distance, shift in ((1, 1), (2, 2), (3, -1)):
            received = send(groups[distance], "ctx", z_ring(shift))
            total = total + received.astype(f32)
        return total

    groups, grad = lax.optimization_barrier((value_call(split, ids, grad, saved), grad))
    value_sum = along_z(groups)
    query_grad, *groups = key_call(split, ids, grad, saved, queries[0])
    key_sum = along_z(groups)
    for_pair = jnp.concatenate([key_sum[1], value_sum[1]], axis=1).astype(bf16)
    own_sum = jnp.concatenate([key_sum[0], value_sum[0]], axis=1)
    kv_grad = (own_sum + send(for_pair, "ctx", X_SWAP).astype(f32)).astype(bf16)

    stacked = jnp.concatenate([query_grad, kv_grad], axis=1)
    weights = jnp.concatenate([query_weight[0], key_weight[0], value_weight[0]], axis=1)

    def term_of(distance):
        start = ((tp + distance) % 4) * 128
        return dot_nt(lax.dynamic_slice_in_dim(stacked, start, 128, 0), weights).astype(bf16)

    far = term_of(2)
    from_left = send(far[:half_rows], "tp", ring(4, 1))
    from_right = send(far[half_rows:], "tp", ring(4, -1))
    own_term = term_of(0)
    own = send(own_term, "section", ring(4, -1))
    right, left = lax.optimization_barrier((term_of(1), term_of(3)))
    empty = jnp.zeros_like(from_left, dtype=f32)
    right = (right.astype(f32) + jnp.concatenate([from_left.astype(f32), empty])).astype(bf16)
    left = (left.astype(f32) + jnp.concatenate([empty, from_right.astype(f32)])).astype(bf16)
    joint = ("section", "tp")
    part_a = send(right, joint, joint_ring(1))
    part_b = send(left, joint, joint_ring(-1))
    sent = (own.astype(f32) + part_a.astype(f32) + part_b.astype(f32)).astype(bf16)
    return (sent[None], kv_grad[None, :, :HD], kv_grad[None, :, HD:])


def solution(mesh):
    placed = (
        P(),
        P("section", "ctx", "tp"),
        P("section", "ctx", "tp"),
        P("section", "ctx", "tp"),
        P("section", ("ctx", "tp"), None),
        P("section", None, "tp"),
        P("section", None, "tp"),
        P("section", None, "tp"),
        P("section", "tp", None),
    )

    return jax.shard_map(
        per_device,
        mesh=mesh,
        in_specs=placed,
        out_specs=(
            P("section", ("ctx", "tp"), None),
            P("section", "ctx", "tp"),
            P("section", "ctx", "tp"),
        ),
        check_vma=False,
    )
```

```python
import jax
import jax.numpy as jnp
from jax import lax
from jax.experimental import pallas as pl
from jax.experimental.pallas import tpu as pltpu
from jax.sharding import PartitionSpec as P

HD = 128
BLK = 256
GROUP = 4
STEPS = 17
SCALE = HD ** (-0.5)
EXP2_SCALE = SCALE * 1.4426950408889634
NEG_LARGE = -1e30

VMEM_WHOLE = pl.BlockSpec(memory_space=pltpu.VMEM)
PARAMS = pltpu.CompilerParams(vmem_limit_bytes=36 << 20)


def dot_nt(lhs, rhs):
    return lax.dot_general(lhs, rhs, (((1,), (1,)), ((), ())), preferred_element_type=jnp.float32)


def dot_nn(lhs, rhs):
    return lax.dot_general(lhs, rhs, (((1,), (0,)), ((), ())), preferred_element_type=jnp.float32)


def ring(size, shift):
    return [(i, (i + shift) % size) for i in range(size)]


def z_ring(shift):
    return [(x * 4 + z, x * 4 + (z + shift) % 4) for x in range(2) for z in range(4)]


X_SWAP = [(x * 4 + z, (1 - x) * 4 + z) for x in range(2) for z in range(4)]


def joint_ring(shift):
    return [(s * 4 + t, ((s - 1) % 4) * 4 + (t + shift) % 4) for s in range(4) for t in range(4)]


def step_block(step, split):
    half = (step > split).astype(jnp.int32)
    return half, step - half * (split + 1)


def step_args(step, split):
    half, kb = step_block(step, split)
    diag = ((step == split) | (step == STEPS - 1)).astype(jnp.int32)
    return half, kb, diag


def forward_kernel(split_ref, ids_ref, *refs):
    kv_refs = refs[:8]
    (
        q_ref, p_ref, out_ref, stat_ref, hist_ref, kvs_ref,
        max_ref, acc_ref, bias_ref, even_ref, odd_ref, even_top_ref, odd_top_ref,
    ) = refs[8:]
    step = pl.program_id(0)
    split = split_ref[0]
    _, kb, diag = step_args(step, split)

    def score_step(at, score_ref, top_ref):
        at_half, at_kb, at_diag = step_args(at, split)
        start = pl.multiple_of(at_half * BLK, BLK)
        key_blk = kvs_ref[at_kb, :, :HD]
        for h in range(GROUP):
            query = q_ref[pl.ds(start, BLK), h * HD : (h + 1) * HD]
            scores = dot_nt(key_blk, query) + bias_ref[at_diag]
            score_ref[h] = scores
            top_ref[0:1, h * BLK : (h + 1) * BLK] = jnp.max(scores, axis=0, keepdims=True)

    @pl.when(step == 0)
    def _():
        for j in range(8):
            for r in range(2):
                kvs_ref[ids_ref[2 * j + r]] = kv_refs[j][r * BLK : (r + 1) * BLK, :]
        gap = lax.broadcasted_iota(jnp.int32, (BLK, BLK), 0) - lax.broadcasted_iota(
            jnp.int32, (BLK, BLK), 1
        )
        bias_ref[0] = jnp.zeros((BLK, BLK), jnp.float32)
        bias_ref[1] = jnp.where(gap <= 0, 0.0, NEG_LARGE)
        max_ref[...] = jnp.full_like(max_ref, NEG_LARGE)
        acc_ref[...] = jnp.zeros_like(acc_ref)
        score_step(step, even_ref, even_top_ref)

    def softmax_step(now, now_top, later, later_top):
        score_step(jnp.minimum(step + 1, STEPS - 1), later, later_top)
        value_t = jnp.transpose(kvs_ref[kb, :, HD:].astype(jnp.float32)).astype(jnp.bfloat16)
        lhs = jnp.concatenate([value_t, jnp.ones((16, BLK), jnp.bfloat16)], axis=0)
        for h in range(GROUP):
            cols = slice(h * BLK, (h + 1) * BLK)
            old_max = jnp.where(kb == 0, NEG_LARGE, max_ref[0:1, cols])
            new_max = jnp.maximum(old_max, now_top[0:1, cols])
            probs = jnp.exp2((now[h] - new_max) * EXP2_SCALE).astype(jnp.bfloat16)
            p_ref[step, h] = probs
            factor = jnp.exp2((old_max - new_max) * EXP2_SCALE)
            acc_ref[:, cols] = acc_ref[:, cols] * factor + dot_nn(lhs, probs)
            max_ref[0:1, cols] = new_max
            hist_ref[0, 0:1, cols] = new_max

    @pl.when(step % 2 == 0)
    def _():
        softmax_step(even_ref, even_top_ref, odd_ref, odd_top_ref)

    @pl.when(step % 2 == 1)
    def _():
        softmax_step(odd_ref, odd_top_ref, even_ref, even_top_ref)

    @pl.when(diag == 1)
    def _():
        inv = 1.0 / acc_ref[HD : HD + 1, :]
        out_ref[0] = acc_ref[:HD, :] * inv
        stat_ref[0, 0:1, :] = max_ref[0:1, :]
        stat_ref[0, 1:2, :] = inv


def half_of(step, split_ref):
    return (step > split_ref[0]).astype(jnp.int32)


def block_of(step, split_ref):
    return step - half_of(step, split_ref) * (split_ref[0] + 1)


def forward_call(split, ids, kv_chunks, queries):
    whole = pl.BlockSpec((2 * BLK, 2 * HD), lambda i, s, d: (0, 0))
    wide = GROUP * BLK
    return pl.pallas_call(
        forward_kernel,
        grid_spec=pltpu.PrefetchScalarGridSpec(
            num_scalar_prefetch=2,
            grid=(STEPS,),
            in_specs=[whole] * 8 + [pl.BlockSpec((2 * BLK, GROUP * HD), lambda i, s, d: (0, 0))],
            out_specs=[
                VMEM_WHOLE,
                pl.BlockSpec((1, HD, wide), lambda i, s, d: (half_of(i, s), 0, 0)),
                pl.BlockSpec((1, 8, wide), lambda i, s, d: (half_of(i, s), 0, 0)),
                pl.BlockSpec((1, 1, wide), lambda i, s, d: (i, 0, 0)),
                pl.BlockSpec((16, BLK, 2 * HD), lambda i, s, d: (0, 0, 0)),
            ],
            scratch_shapes=[
                pltpu.VMEM((8, wide), jnp.float32),
                pltpu.VMEM((HD + 16, wide), jnp.float32),
                pltpu.VMEM((2, BLK, BLK), jnp.float32),
                pltpu.VMEM((GROUP, BLK, BLK), jnp.float32),
                pltpu.VMEM((GROUP, BLK, BLK), jnp.float32),
                pltpu.VMEM((8, wide), jnp.float32),
                pltpu.VMEM((8, wide), jnp.float32),
            ],
        ),
        out_shape=[
            jax.ShapeDtypeStruct((STEPS, GROUP, BLK, BLK), jnp.bfloat16),
            jax.ShapeDtypeStruct((2, HD, wide), jnp.float32),
            jax.ShapeDtypeStruct((2, 8, wide), jnp.float32),
            jax.ShapeDtypeStruct((STEPS, 1, wide), jnp.float32),
            jax.ShapeDtypeStruct((16, BLK, 2 * HD), jnp.bfloat16),
        ],
        compiler_params=PARAMS,
        cost_estimate=pl.CostEstimate(
            flops=2 * 2 * STEPS * wide * BLK * HD,
            bytes_accessed=13 << 20,
            transcendentals=STEPS * wide * BLK,
        ),
        name="attn_forward",
    )(split, ids, *kv_chunks, queries)


def grad_kernel(rows_ref, *refs):
    pieces = refs[:7]
    weight_ref, out_ref, lhs_ref, acc_ref = refs[7:]
    step = pl.program_id(0)
    depth = lhs_ref.shape[1]

    @pl.when(step == 0)
    def _():
        acc_ref[...] = jnp.zeros_like(acc_ref)

    for j, piece in enumerate(pieces):
        size = piece.shape[0]
        lhs_ref[pl.ds(pl.multiple_of(rows_ref[j], 64), size), :] = piece[...]
    start = pl.multiple_of(step * depth, depth)
    acc_ref[...] += dot_nt(lhs_ref[...], weight_ref[:, pl.ds(start, depth)])

    @pl.when(step == pl.num_programs(0) - 1)
    def _():
        out_ref[...] = acc_ref[...].astype(jnp.bfloat16)


def grad_call(rows, pieces, out_weight):
    depth = 512
    total = out_weight.shape[0]
    return pl.pallas_call(
        grad_kernel,
        grid_spec=pltpu.PrefetchScalarGridSpec(
            num_scalar_prefetch=1,
            grid=(out_weight.shape[1] // depth,),
            in_specs=[pl.BlockSpec((p.shape[0], depth), lambda i, w: (0, i)) for p in pieces]
            + [VMEM_WHOLE],
            out_specs=pl.BlockSpec((2 * BLK, total), lambda i, w: (0, 0)),
            scratch_shapes=[
                pltpu.VMEM((2 * BLK, depth), jnp.bfloat16),
                pltpu.VMEM((2 * BLK, total), jnp.float32),
            ],
        ),
        out_shape=jax.ShapeDtypeStruct((2 * BLK, total), jnp.bfloat16),
        compiler_params=PARAMS,
        cost_estimate=pl.CostEstimate(
            flops=2 * 2 * BLK * total * out_weight.shape[1],
            bytes_accessed=9 << 20,
            transcendentals=0,
        ),
        name="attn_grad",
    )(rows, *pieces, out_weight)


def norm_of(hist_ref, stat_ref, cols):
    gap = (hist_ref[0, 0:1, cols] - stat_ref[0, 0:1, cols]) * EXP2_SCALE
    return jnp.exp2(gap) * stat_ref[0, 1:2, cols]


def write_groups(ids_ref, total_ref, group_refs, scale):
    for g, g_ref in enumerate(group_refs):
        for x in range(2):
            for r in range(2):
                block = ids_ref[4 * g + 2 * x + r]
                g_ref[x, r * BLK : (r + 1) * BLK, :] = (total_ref[block] * scale).astype(
                    jnp.bfloat16
                )


def value_kernel(split_ref, ids_ref, grad_ref, p_ref, stat_ref, hist_ref, *refs):
    group_refs = refs[:4]
    total_ref = refs[4]
    step = pl.program_id(0)
    half, kb, _ = step_args(step, split_ref[0])

    @pl.when(step == 0)
    def _():
        total_ref[...] = jnp.zeros_like(total_ref)

    start = pl.multiple_of(half * BLK, BLK)
    dv = jnp.zeros((BLK, HD), jnp.float32)
    for h in range(GROUP):
        norm = norm_of(hist_ref, stat_ref, slice(h * BLK, (h + 1) * BLK))
        probs = (p_ref[step, h].astype(jnp.float32) * norm).astype(jnp.bfloat16)
        dv = dv + dot_nn(probs, grad_ref[pl.ds(start, BLK), h * HD : (h + 1) * HD])
    total_ref[kb] += dv

    @pl.when(step == STEPS - 1)
    def _():
        write_groups(ids_ref, total_ref, group_refs, 1.0)


def value_call(split, ids, grad, saved):
    probs, _, stats, hist, _ = saved
    wide = GROUP * BLK
    group_spec = pl.BlockSpec((2, 2 * BLK, HD), lambda i, s, d: (0, 0, 0))
    return pl.pallas_call(
        value_kernel,
        grid_spec=pltpu.PrefetchScalarGridSpec(
            num_scalar_prefetch=2,
            grid=(STEPS,),
            in_specs=[
                pl.BlockSpec((2 * BLK, GROUP * HD), lambda i, s, d: (0, 0)),
                VMEM_WHOLE,
                pl.BlockSpec((1, 8, wide), lambda i, s, d: (half_of(i, s), 0, 0)),
                pl.BlockSpec((1, 1, wide), lambda i, s, d: (i, 0, 0)),
            ],
            out_specs=[group_spec] * 4,
            scratch_shapes=[pltpu.VMEM((16, BLK, HD), jnp.float32)],
        ),
        out_shape=[jax.ShapeDtypeStruct((2, 2 * BLK, HD), jnp.bfloat16)] * 4,
        compiler_params=PARAMS,
        cost_estimate=pl.CostEstimate(
            flops=2 * STEPS * wide * BLK * HD, bytes_accessed=11 << 20, transcendentals=0
        ),
        name="attn_value_grad",
    )(split, ids, grad, probs, stats, hist)


def key_kernel(split_ref, ids_ref, grad_ref, q_ref, p_ref, kv_ref, next_ref, out_ref, stat_ref,
               hist_ref, *refs):
    dq_ref = refs[0]
    group_refs = refs[1:5]
    delta_ref, dqt_ref, total_ref, even_ref, odd_ref = refs[5:]
    step = pl.program_id(0)
    split = split_ref[0]
    half, kb, diag = step_args(step, split)

    def grad_probs_step(at, value_blk, gp_ref):
        at_half = (at > split).astype(jnp.int32)
        start = pl.multiple_of(at_half * BLK, BLK)
        for h in range(GROUP):
            gp_ref[h] = dot_nt(
                value_blk, grad_ref[pl.ds(start, BLK), h * HD : (h + 1) * HD]
            )

    @pl.when(step == 0)
    def _():
        total_ref[...] = jnp.zeros_like(total_ref)
        dqt_ref[...] = jnp.zeros_like(dqt_ref)
        grad_probs_step(step, kv_ref[0, :, HD:], even_ref)

    start = pl.multiple_of(half * BLK, BLK)

    @pl.when(kb == 0)
    def _():
        for h in range(GROUP):
            cols = slice(h * BLK, (h + 1) * BLK)
            grad = grad_ref[pl.ds(start, BLK), h * HD : (h + 1) * HD]
            grad_t = jnp.transpose(grad.astype(jnp.float32))
            delta_ref[0:1, cols] = jnp.sum(out_ref[0, :, cols] * grad_t, axis=0, keepdims=True)

    def main_step(now, later):
        grad_probs_step(jnp.minimum(step + 1, STEPS - 1), next_ref[0, :, HD:], later)
        key_t = jnp.transpose(kv_ref[0, :, :HD].astype(jnp.float32)).astype(jnp.bfloat16)
        keep = jnp.where(kb == 0, 0.0, 1.0)
        dk = jnp.zeros((BLK, HD), jnp.float32)
        for h in range(GROUP):
            cols = slice(h * BLK, (h + 1) * BLK)
            probs = p_ref[step, h].astype(jnp.float32) * norm_of(hist_ref, stat_ref, cols)
            dscore = (probs * (now[h] - delta_ref[0:1, cols])).astype(jnp.bfloat16)
            dk = dk + dot_nn(dscore, q_ref[pl.ds(start, BLK), h * HD : (h + 1) * HD])
            dqt_ref[:, cols] = dqt_ref[:, cols] * keep + dot_nn(key_t, dscore)
        total_ref[kb] += dk

    @pl.when(step % 2 == 0)
    def _():
        main_step(even_ref, odd_ref)

    @pl.when(step % 2 == 1)
    def _():
        main_step(odd_ref, even_ref)

    @pl.when(diag == 1)
    def _():
        for h in range(GROUP):
            cols = slice(h * BLK, (h + 1) * BLK)
            dq_ref[:, h * HD : (h + 1) * HD] = jnp.transpose(dqt_ref[:, cols] * SCALE).astype(
                jnp.bfloat16
            )

    @pl.when(step == STEPS - 1)
    def _():
        write_groups(ids_ref, total_ref, group_refs, SCALE)


def key_call(split, ids, grad, saved, queries):
    probs, outs, stats, hist, kv_sorted = saved
    wide = GROUP * BLK
    group_spec = pl.BlockSpec((2, 2 * BLK, HD), lambda i, s, d: (0, 0, 0))
    whole = pl.BlockSpec((2 * BLK, GROUP * HD), lambda i, s, d: (0, 0))

    def next_block(i, s, d):
        return (block_of(jnp.minimum(i + 1, STEPS - 1), s), 0, 0)

    return pl.pallas_call(
        key_kernel,
        grid_spec=pltpu.PrefetchScalarGridSpec(
            num_scalar_prefetch=2,
            grid=(STEPS,),
            in_specs=[
                whole,
                whole,
                VMEM_WHOLE,
                pl.BlockSpec((1, BLK, 2 * HD), lambda i, s, d: (block_of(i, s), 0, 0)),
                pl.BlockSpec((1, BLK, 2 * HD), next_block),
                pl.BlockSpec((1, HD, wide), lambda i, s, d: (half_of(i, s), 0, 0)),
                pl.BlockSpec((1, 8, wide), lambda i, s, d: (half_of(i, s), 0, 0)),
                pl.BlockSpec((1, 1, wide), lambda i, s, d: (i, 0, 0)),
            ],
            out_specs=[pl.BlockSpec((BLK, GROUP * HD), lambda i, s, d: (half_of(i, s), 0))]
            + [group_spec] * 4,
            scratch_shapes=[
                pltpu.VMEM((8, wide), jnp.float32),
                pltpu.VMEM((HD, wide), jnp.float32),
                pltpu.VMEM((16, BLK, HD), jnp.float32),
                pltpu.VMEM((GROUP, BLK, BLK), jnp.float32),
                pltpu.VMEM((GROUP, BLK, BLK), jnp.float32),
            ],
        ),
        out_shape=[jax.ShapeDtypeStruct((2 * BLK, GROUP * HD), jnp.bfloat16)]
        + [jax.ShapeDtypeStruct((2, 2 * BLK, HD), jnp.bfloat16)] * 4,
        compiler_params=PARAMS,
        cost_estimate=pl.CostEstimate(
            flops=2 * 3 * STEPS * wide * BLK * HD, bytes_accessed=14 << 20, transcendentals=0
        ),
        name="attn_key_grad",
    )(split, ids, grad, queries, probs, kv_sorted, kv_sorted, outs, stats, hist)


def per_device(
    stretch_order,
    queries,
    key_rows,
    value_rows,
    out_grad,
    query_weight,
    key_weight,
    value_weight,
    output_weight,
):
    send = lax.ppermute
    tp = lax.axis_index("tp")
    ctx = lax.axis_index("ctx")
    own_x, own_z = ctx // 4, ctx % 4
    bf16 = jnp.bfloat16

    chunk = out_grad[0]
    half_rows = chunk.shape[0] // 2
    top, low = chunk[:half_rows], chunk[half_rows:]
    left_top = send(top, "tp", ring(4, 1))
    right_low = send(low, "tp", ring(4, -1))
    far_top = send(left_top, "tp", ring(4, 1))
    far_low = send(right_low, "tp", ring(4, -1))
    left_low = send(low, "tp", ring(4, 1))
    right_top = send(top, "tp", ring(4, -1))

    kv_own = jnp.concatenate([key_rows[0], value_rows[0]], axis=1)
    kv_pair = send(kv_own, "ctx", X_SWAP)
    kv_chunks = [kv_own, kv_pair]
    for shift in (-1, 2, 1):
        kv_chunks.append(send(kv_own, "ctx", z_ring(shift)))
        kv_chunks.append(send(kv_pair, "ctx", z_ring(shift)))

    index = jnp.arange(8, dtype=jnp.int32)
    source = ((own_x + index % 2) % 2) * 4 + (own_z + index // 2) % 4
    table = jnp.arange(8, dtype=jnp.int32)
    ids = jnp.sum(
        jnp.where(source[:, None, None] == table[None, :, None], stretch_order[None], 0), axis=1
    ).reshape(16)
    split = ids[:1]
    saved = forward_call(split, ids, kv_chunks, queries[0])

    left, right, far = (tp + 3) % 4, (tp + 1) % 4, (tp + 2) % 4
    pieces = (chunk, left_top, left_low, right_top, right_low, far_top, far_low)
    places = (2 * tp, 2 * left, 2 * left + 1, 2 * right, 2 * right + 1, 2 * far, 2 * far + 1)
    grad = grad_call(
        (jnp.stack(places) * half_rows).astype(jnp.int32), pieces, output_weight[0]
    )

    f32 = jnp.float32

    def along_z(groups):
        total = groups[0].astype(f32)
        for distance, shift in ((1, 1), (2, 2), (3, -1)):
            received = send(groups[distance], "ctx", z_ring(shift))
            total = total + received.astype(f32)
        return total

    groups, grad = lax.optimization_barrier((value_call(split, ids, grad, saved), grad))
    value_sum = along_z(groups)
    query_grad, *groups = key_call(split, ids, grad, saved, queries[0])
    key_sum = along_z(groups)

    def with_pair(total):
        received = send(total[1].astype(bf16), "ctx", X_SWAP)
        return (total[0] + received.astype(f32)).astype(bf16)

    value_grad = with_pair(value_sum)
    key_grad = with_pair(key_sum)

    stacked = jnp.concatenate([query_grad, key_grad, value_grad], axis=1)
    weights = jnp.concatenate([query_weight[0], key_weight[0], value_weight[0]], axis=1)

    def term_of(distance):
        start = ((tp + distance) % 4) * 128
        rows = lax.dynamic_slice_in_dim(stacked, start, 128, 0)
        return dot_nt(rows, weights).astype(bf16)

    far = term_of(2)
    from_left = send(far[:half_rows], "tp", ring(4, 1))
    from_right = send(far[half_rows:], "tp", ring(4, -1))
    own_term = term_of(0)
    own = send(own_term, "section", ring(4, -1))
    right, left = lax.optimization_barrier((term_of(1), term_of(3)))
    empty = jnp.zeros_like(from_left, dtype=f32)
    right = (right.astype(f32) + jnp.concatenate([from_left.astype(f32), empty])).astype(bf16)
    left = (left.astype(f32) + jnp.concatenate([empty, from_right.astype(f32)])).astype(bf16)
    joint = ("section", "tp")
    part_a = send(right, joint, joint_ring(1))
    part_b = send(left, joint, joint_ring(-1))
    sent = (own.astype(f32) + part_a.astype(f32) + part_b.astype(f32)).astype(bf16)
    return (sent[None], key_grad[None], value_grad[None])


def solution(mesh):
    placed = (
        P(),
        P("section", "ctx", "tp"),
        P("section", "ctx", "tp"),
        P("section", "ctx", "tp"),
        P("section", ("ctx", "tp"), None),
        P("section", None, "tp"),
        P("section", None, "tp"),
        P("section", None, "tp"),
        P("section", "tp", None),
    )

    return jax.shard_map(
        per_device,
        mesh=mesh,
        in_specs=placed,
        out_specs=(
            P("section", ("ctx", "tp"), None),
            P("section", "ctx", "tp"),
            P("section", "ctx", "tp"),
        ),
        check_vma=False,
    )
```

```python
import jax
import jax.numpy as jnp
from jax import lax
from jax.experimental import pallas as pl
from jax.experimental.pallas import tpu as pltpu
from jax.sharding import PartitionSpec as P

HD = 128
BLK = 256
GROUP = 4
STEPS = 17
SCALE = HD ** (-0.5)
EXP2_SCALE = SCALE * 1.4426950408889634
NEG_LARGE = -1e30

VMEM_WHOLE = pl.BlockSpec(memory_space=pltpu.VMEM)
PARAMS = pltpu.CompilerParams(vmem_limit_bytes=36 << 20)


def dot_nt(lhs, rhs):
    return lax.dot_general(lhs, rhs, (((1,), (1,)), ((), ())), preferred_element_type=jnp.float32)


def dot_nn(lhs, rhs):
    return lax.dot_general(lhs, rhs, (((1,), (0,)), ((), ())), preferred_element_type=jnp.float32)


def ring(size, shift):
    return [(i, (i + shift) % size) for i in range(size)]


def z_ring(shift):
    return [(x * 4 + z, x * 4 + (z + shift) % 4) for x in range(2) for z in range(4)]


X_SWAP = [(x * 4 + z, (1 - x) * 4 + z) for x in range(2) for z in range(4)]


def joint_ring(shift):
    return [(s * 4 + t, ((s - 1) % 4) * 4 + (t + shift) % 4) for s in range(4) for t in range(4)]


def step_block(step, split):
    half = (step > split).astype(jnp.int32)
    return half, step - half * (split + 1)


def step_args(step, split):
    half, kb = step_block(step, split)
    diag = ((step == split) | (step == STEPS - 1)).astype(jnp.int32)
    return half, kb, diag


def forward_kernel(split_ref, ids_ref, *refs):
    kv_refs = refs[:8]
    (
        q_ref, p_ref, out_ref, stat_ref, hist_ref, kvs_ref,
        max_ref, acc_ref, bias_ref, even_ref, odd_ref, even_top_ref, odd_top_ref,
    ) = refs[8:]
    step = pl.program_id(0)
    split = split_ref[0]
    _, kb, diag = step_args(step, split)

    def score_step(at, score_ref, top_ref):
        at_half, at_kb, at_diag = step_args(at, split)
        start = pl.multiple_of(at_half * BLK, BLK)
        key_blk = kvs_ref[at_kb, :, :HD]
        for h in range(GROUP):
            query = q_ref[pl.ds(start, BLK), h * HD : (h + 1) * HD]
            scores = dot_nt(key_blk, query) + bias_ref[at_diag]
            score_ref[h] = scores
            top_ref[0:1, h * BLK : (h + 1) * BLK] = jnp.max(scores, axis=0, keepdims=True)

    @pl.when(step == 0)
    def _():
        for j in range(8):
            for r in range(2):
                kvs_ref[ids_ref[2 * j + r]] = kv_refs[j][r * BLK : (r + 1) * BLK, :]
        gap = lax.broadcasted_iota(jnp.int32, (BLK, BLK), 0) - lax.broadcasted_iota(
            jnp.int32, (BLK, BLK), 1
        )
        bias_ref[0] = jnp.zeros((BLK, BLK), jnp.float32)
        bias_ref[1] = jnp.where(gap <= 0, 0.0, NEG_LARGE)
        max_ref[...] = jnp.full_like(max_ref, NEG_LARGE)
        acc_ref[...] = jnp.zeros_like(acc_ref)
        score_step(step, even_ref, even_top_ref)

    def softmax_step(now, now_top, later, later_top):
        score_step(jnp.minimum(step + 1, STEPS - 1), later, later_top)
        value_t = jnp.transpose(kvs_ref[kb, :, HD:].astype(jnp.float32)).astype(jnp.bfloat16)
        lhs = jnp.concatenate([value_t, jnp.ones((16, BLK), jnp.bfloat16)], axis=0)
        for h in range(GROUP):
            cols = slice(h * BLK, (h + 1) * BLK)
            old_max = jnp.where(kb == 0, NEG_LARGE, max_ref[0:1, cols])
            new_max = jnp.maximum(old_max, now_top[0:1, cols])
            probs = jnp.exp2((now[h] - new_max) * EXP2_SCALE).astype(jnp.bfloat16)
            p_ref[step, h] = probs
            factor = jnp.exp2((old_max - new_max) * EXP2_SCALE)
            acc_ref[:, cols] = acc_ref[:, cols] * factor + dot_nn(lhs, probs)
            max_ref[0:1, cols] = new_max
            hist_ref[0, 0:1, cols] = new_max

    @pl.when(step % 2 == 0)
    def _():
        softmax_step(even_ref, even_top_ref, odd_ref, odd_top_ref)

    @pl.when(step % 2 == 1)
    def _():
        softmax_step(odd_ref, odd_top_ref, even_ref, even_top_ref)

    @pl.when(diag == 1)
    def _():
        inv = 1.0 / acc_ref[HD : HD + 1, :]
        out_ref[0] = acc_ref[:HD, :] * inv
        stat_ref[0, 0:1, :] = max_ref[0:1, :]
        stat_ref[0, 1:2, :] = inv


def half_of(step, split_ref):
    return (step > split_ref[0]).astype(jnp.int32)


def block_of(step, split_ref):
    return step - half_of(step, split_ref) * (split_ref[0] + 1)


def forward_call(split, ids, kv_chunks, queries):
    whole = pl.BlockSpec((2 * BLK, 2 * HD), lambda i, s, d: (0, 0))
    wide = GROUP * BLK
    return pl.pallas_call(
        forward_kernel,
        grid_spec=pltpu.PrefetchScalarGridSpec(
            num_scalar_prefetch=2,
            grid=(STEPS,),
            in_specs=[whole] * 8 + [pl.BlockSpec((2 * BLK, GROUP * HD), lambda i, s, d: (0, 0))],
            out_specs=[
                VMEM_WHOLE,
                pl.BlockSpec((1, HD, wide), lambda i, s, d: (half_of(i, s), 0, 0)),
                pl.BlockSpec((1, 8, wide), lambda i, s, d: (half_of(i, s), 0, 0)),
                pl.BlockSpec((1, 1, wide), lambda i, s, d: (i, 0, 0)),
                pl.BlockSpec((16, BLK, 2 * HD), lambda i, s, d: (0, 0, 0)),
            ],
            scratch_shapes=[
                pltpu.VMEM((8, wide), jnp.float32),
                pltpu.VMEM((HD + 16, wide), jnp.float32),
                pltpu.VMEM((2, BLK, BLK), jnp.float32),
                pltpu.VMEM((GROUP, BLK, BLK), jnp.float32),
                pltpu.VMEM((GROUP, BLK, BLK), jnp.float32),
                pltpu.VMEM((8, wide), jnp.float32),
                pltpu.VMEM((8, wide), jnp.float32),
            ],
        ),
        out_shape=[
            jax.ShapeDtypeStruct((STEPS, GROUP, BLK, BLK), jnp.bfloat16),
            jax.ShapeDtypeStruct((2, HD, wide), jnp.float32),
            jax.ShapeDtypeStruct((2, 8, wide), jnp.float32),
            jax.ShapeDtypeStruct((STEPS, 1, wide), jnp.float32),
            jax.ShapeDtypeStruct((16, BLK, 2 * HD), jnp.bfloat16),
        ],
        compiler_params=PARAMS,
        cost_estimate=pl.CostEstimate(
            flops=2 * 2 * STEPS * wide * BLK * HD,
            bytes_accessed=13 << 20,
            transcendentals=STEPS * wide * BLK,
        ),
        name="attn_forward",
    )(split, ids, *kv_chunks, queries)


def grad_kernel(rows_ref, *refs):
    pieces = refs[:7]
    weight_ref, out_ref, lhs_ref, acc_ref = refs[7:]
    step = pl.program_id(0)
    depth = lhs_ref.shape[1]

    @pl.when(step == 0)
    def _():
        acc_ref[...] = jnp.zeros_like(acc_ref)

    for j, piece in enumerate(pieces):
        size = piece.shape[0]
        lhs_ref[pl.ds(pl.multiple_of(rows_ref[j], 64), size), :] = piece[...]
    start = pl.multiple_of(step * depth, depth)
    acc_ref[...] += dot_nt(lhs_ref[...], weight_ref[:, pl.ds(start, depth)])

    @pl.when(step == pl.num_programs(0) - 1)
    def _():
        out_ref[...] = acc_ref[...].astype(jnp.bfloat16)


def grad_call(rows, pieces, out_weight):
    depth = 512
    total = out_weight.shape[0]
    return pl.pallas_call(
        grad_kernel,
        grid_spec=pltpu.PrefetchScalarGridSpec(
            num_scalar_prefetch=1,
            grid=(out_weight.shape[1] // depth,),
            in_specs=[pl.BlockSpec((p.shape[0], depth), lambda i, w: (0, i)) for p in pieces]
            + [VMEM_WHOLE],
            out_specs=pl.BlockSpec((2 * BLK, total), lambda i, w: (0, 0)),
            scratch_shapes=[
                pltpu.VMEM((2 * BLK, depth), jnp.bfloat16),
                pltpu.VMEM((2 * BLK, total), jnp.float32),
            ],
        ),
        out_shape=jax.ShapeDtypeStruct((2 * BLK, total), jnp.bfloat16),
        compiler_params=PARAMS,
        cost_estimate=pl.CostEstimate(
            flops=2 * 2 * BLK * total * out_weight.shape[1],
            bytes_accessed=9 << 20,
            transcendentals=0,
        ),
        name="attn_grad",
    )(rows, *pieces, out_weight)


def norm_of(hist_ref, stat_ref, cols):
    gap = (hist_ref[0, 0:1, cols] - stat_ref[0, 0:1, cols]) * EXP2_SCALE
    return jnp.exp2(gap) * stat_ref[0, 1:2, cols]


def write_groups(ids_ref, total_ref, group_refs, scale):
    for g, g_ref in enumerate(group_refs):
        for x in range(2):
            for r in range(2):
                block = ids_ref[4 * g + 2 * x + r]
                g_ref[x, r * BLK : (r + 1) * BLK, :] = (total_ref[block] * scale).astype(
                    jnp.bfloat16
                )


def value_kernel(split_ref, ids_ref, grad_ref, p_ref, stat_ref, hist_ref, *refs):
    group_refs = refs[:4]
    total_ref = refs[4]
    step = pl.program_id(0)
    half, kb, _ = step_args(step, split_ref[0])

    @pl.when(step == 0)
    def _():
        total_ref[...] = jnp.zeros_like(total_ref)

    start = pl.multiple_of(half * BLK, BLK)
    dv = jnp.zeros((BLK, HD), jnp.float32)
    for h in range(GROUP):
        norm = norm_of(hist_ref, stat_ref, slice(h * BLK, (h + 1) * BLK))
        probs = (p_ref[step, h].astype(jnp.float32) * norm).astype(jnp.bfloat16)
        dv = dv + dot_nn(probs, grad_ref[pl.ds(start, BLK), h * HD : (h + 1) * HD])
    total_ref[kb] += dv

    @pl.when(step == STEPS - 1)
    def _():
        write_groups(ids_ref, total_ref, group_refs, 1.0)


def value_call(split, ids, grad, saved):
    probs, _, stats, hist, _ = saved
    wide = GROUP * BLK
    group_spec = pl.BlockSpec((2, 2 * BLK, HD), lambda i, s, d: (0, 0, 0))
    return pl.pallas_call(
        value_kernel,
        grid_spec=pltpu.PrefetchScalarGridSpec(
            num_scalar_prefetch=2,
            grid=(STEPS,),
            in_specs=[
                pl.BlockSpec((2 * BLK, GROUP * HD), lambda i, s, d: (0, 0)),
                VMEM_WHOLE,
                pl.BlockSpec((1, 8, wide), lambda i, s, d: (half_of(i, s), 0, 0)),
                pl.BlockSpec((1, 1, wide), lambda i, s, d: (i, 0, 0)),
            ],
            out_specs=[group_spec] * 4,
            scratch_shapes=[pltpu.VMEM((16, BLK, HD), jnp.float32)],
        ),
        out_shape=[jax.ShapeDtypeStruct((2, 2 * BLK, HD), jnp.bfloat16)] * 4,
        compiler_params=PARAMS,
        cost_estimate=pl.CostEstimate(
            flops=2 * STEPS * wide * BLK * HD, bytes_accessed=11 << 20, transcendentals=0
        ),
        name="attn_value_grad",
    )(split, ids, grad, probs, stats, hist)


def key_kernel(split_ref, ids_ref, grad_ref, q_ref, p_ref, kv_ref, next_ref, out_ref, stat_ref,
               hist_ref, *refs):
    dq_ref = refs[0]
    group_refs = refs[1:5]
    delta_ref, dqt_ref, total_ref, even_ref, odd_ref = refs[5:]
    step = pl.program_id(0)
    split = split_ref[0]
    half, kb, diag = step_args(step, split)

    def grad_probs_step(at, value_blk, gp_ref):
        at_half = (at > split).astype(jnp.int32)
        start = pl.multiple_of(at_half * BLK, BLK)
        for h in range(GROUP):
            gp_ref[h] = dot_nt(
                value_blk, grad_ref[pl.ds(start, BLK), h * HD : (h + 1) * HD]
            )

    @pl.when(step == 0)
    def _():
        total_ref[...] = jnp.zeros_like(total_ref)
        dqt_ref[...] = jnp.zeros_like(dqt_ref)
        grad_probs_step(step, kv_ref[0, :, HD:], even_ref)

    start = pl.multiple_of(half * BLK, BLK)

    @pl.when(kb == 0)
    def _():
        for h in range(GROUP):
            cols = slice(h * BLK, (h + 1) * BLK)
            grad = grad_ref[pl.ds(start, BLK), h * HD : (h + 1) * HD]
            grad_t = jnp.transpose(grad.astype(jnp.float32))
            delta_ref[0:1, cols] = jnp.sum(out_ref[0, :, cols] * grad_t, axis=0, keepdims=True)

    def main_step(now, later):
        grad_probs_step(jnp.minimum(step + 1, STEPS - 1), next_ref[0, :, HD:], later)
        key_t = jnp.transpose(kv_ref[0, :, :HD].astype(jnp.float32)).astype(jnp.bfloat16)
        keep = jnp.where(kb == 0, 0.0, 1.0)
        dk = jnp.zeros((BLK, HD), jnp.float32)
        for h in range(GROUP):
            cols = slice(h * BLK, (h + 1) * BLK)
            probs = p_ref[step, h].astype(jnp.float32) * norm_of(hist_ref, stat_ref, cols)
            dscore = (probs * (now[h] - delta_ref[0:1, cols])).astype(jnp.bfloat16)
            dk = dk + dot_nn(dscore, q_ref[pl.ds(start, BLK), h * HD : (h + 1) * HD])
            dqt_ref[:, cols] = dqt_ref[:, cols] * keep + dot_nn(key_t, dscore)
        total_ref[kb] += dk

    @pl.when(step % 2 == 0)
    def _():
        main_step(even_ref, odd_ref)

    @pl.when(step % 2 == 1)
    def _():
        main_step(odd_ref, even_ref)

    @pl.when(diag == 1)
    def _():
        for h in range(GROUP):
            cols = slice(h * BLK, (h + 1) * BLK)
            dq_ref[:, h * HD : (h + 1) * HD] = jnp.transpose(dqt_ref[:, cols] * SCALE).astype(
                jnp.bfloat16
            )

    @pl.when(step == STEPS - 1)
    def _():
        write_groups(ids_ref, total_ref, group_refs, SCALE)


def key_call(split, ids, grad, saved, queries):
    probs, outs, stats, hist, kv_sorted = saved
    wide = GROUP * BLK
    group_spec = pl.BlockSpec((2, 2 * BLK, HD), lambda i, s, d: (0, 0, 0))
    whole = pl.BlockSpec((2 * BLK, GROUP * HD), lambda i, s, d: (0, 0))

    def next_block(i, s, d):
        return (block_of(jnp.minimum(i + 1, STEPS - 1), s), 0, 0)

    return pl.pallas_call(
        key_kernel,
        grid_spec=pltpu.PrefetchScalarGridSpec(
            num_scalar_prefetch=2,
            grid=(STEPS,),
            in_specs=[
                whole,
                whole,
                VMEM_WHOLE,
                pl.BlockSpec((1, BLK, 2 * HD), lambda i, s, d: (block_of(i, s), 0, 0)),
                pl.BlockSpec((1, BLK, 2 * HD), next_block),
                pl.BlockSpec((1, HD, wide), lambda i, s, d: (half_of(i, s), 0, 0)),
                pl.BlockSpec((1, 8, wide), lambda i, s, d: (half_of(i, s), 0, 0)),
                pl.BlockSpec((1, 1, wide), lambda i, s, d: (i, 0, 0)),
            ],
            out_specs=[pl.BlockSpec((BLK, GROUP * HD), lambda i, s, d: (half_of(i, s), 0))]
            + [group_spec] * 4,
            scratch_shapes=[
                pltpu.VMEM((8, wide), jnp.float32),
                pltpu.VMEM((HD, wide), jnp.float32),
                pltpu.VMEM((16, BLK, HD), jnp.float32),
                pltpu.VMEM((GROUP, BLK, BLK), jnp.float32),
                pltpu.VMEM((GROUP, BLK, BLK), jnp.float32),
            ],
        ),
        out_shape=[jax.ShapeDtypeStruct((2 * BLK, GROUP * HD), jnp.bfloat16)]
        + [jax.ShapeDtypeStruct((2, 2 * BLK, HD), jnp.bfloat16)] * 4,
        compiler_params=PARAMS,
        cost_estimate=pl.CostEstimate(
            flops=2 * 3 * STEPS * wide * BLK * HD, bytes_accessed=14 << 20, transcendentals=0
        ),
        name="attn_key_grad",
    )(split, ids, grad, queries, probs, kv_sorted, kv_sorted, outs, stats, hist)


def per_device(
    stretch_order,
    queries,
    key_rows,
    value_rows,
    out_grad,
    query_weight,
    key_weight,
    value_weight,
    output_weight,
):
    send = lax.ppermute
    tp = lax.axis_index("tp")
    ctx = lax.axis_index("ctx")
    own_x, own_z = ctx // 4, ctx % 4
    bf16 = jnp.bfloat16

    chunk = out_grad[0]
    half_rows = chunk.shape[0] // 2
    top, low = chunk[:half_rows], chunk[half_rows:]
    left_top = send(top, "tp", ring(4, 1))
    right_low = send(low, "tp", ring(4, -1))
    far_top = send(left_top, "tp", ring(4, 1))
    far_low = send(right_low, "tp", ring(4, -1))
    left_low = send(low, "tp", ring(4, 1))
    right_top = send(top, "tp", ring(4, -1))

    kv_own = jnp.concatenate([key_rows[0], value_rows[0]], axis=1)
    kv_pair = send(kv_own, "ctx", X_SWAP)
    along, crossed = {}, {}
    for distance, shift in ((2, 2), (1, -1), (3, 1)):
        along[distance] = send(kv_own, "ctx", z_ring(shift))
    for distance, shift in ((1, -1), (3, 1)):
        crossed[distance] = send(kv_pair, "ctx", z_ring(shift))
    crossed[2] = send(along[2], "ctx", X_SWAP)
    kv_chunks = [kv_own, kv_pair]
    for distance in (1, 2, 3):
        kv_chunks += [along[distance], crossed[distance]]

    joint = ("section", "tp")
    kv_weights = jnp.concatenate([key_weight[0], value_weight[0]], axis=1)
    own_weights = send(kv_weights, "section", ring(4, -1))
    far_weights = send(kv_weights, joint, joint_ring(2))

    index = jnp.arange(8, dtype=jnp.int32)
    source = ((own_x + index % 2) % 2) * 4 + (own_z + index // 2) % 4
    table = jnp.arange(8, dtype=jnp.int32)
    ids = jnp.sum(
        jnp.where(source[:, None, None] == table[None, :, None], stretch_order[None], 0), axis=1
    ).reshape(16)
    split = ids[:1]
    saved = forward_call(split, ids, kv_chunks, queries[0])

    left, right, far = (tp + 3) % 4, (tp + 1) % 4, (tp + 2) % 4
    pieces = (chunk, left_top, left_low, right_top, right_low, far_top, far_low)
    places = (2 * tp, 2 * left, 2 * left + 1, 2 * right, 2 * right + 1, 2 * far, 2 * far + 1)
    grad = grad_call(
        (jnp.stack(places) * half_rows).astype(jnp.int32), pieces, output_weight[0]
    )

    f32 = jnp.float32

    def along_z(groups):
        total = groups[0].astype(f32)
        for distance, shift in ((1, 1), (2, 2), (3, -1)):
            received = send(groups[distance], "ctx", z_ring(shift))
            total = total + received.astype(f32)
        return total

    groups, grad = lax.optimization_barrier((value_call(split, ids, grad, saved), grad))
    value_sum = along_z(groups)
    query_grad, *groups = key_call(split, ids, grad, saved, queries[0])
    key_sum = along_z(groups)

    def with_pair(total):
        received = send(total[1].astype(bf16), "ctx", X_SWAP)
        return (total[0] + received.astype(f32)).astype(bf16)

    def chunk_of(array, distance):
        return lax.dynamic_slice_in_dim(array, ((tp + distance) % 4) * 128, 128, 0)

    def query_term(distance):
        return dot_nt(chunk_of(query_grad, distance), query_weight[0])

    far_term = query_term(2).astype(bf16)
    from_left = send(far_term[:half_rows], "tp", ring(4, 1))
    from_right = send(far_term[half_rows:], "tp", ring(4, -1))
    own_term = query_term(0).astype(bf16)
    own = send(own_term, "section", ring(4, -1))
    right, left = lax.optimization_barrier((query_term(1), query_term(3)))

    value_grad = with_pair(value_sum)
    key_grad = with_pair(key_sum)

    kv_grad = jnp.concatenate([key_grad, value_grad], axis=1)
    empty = jnp.zeros_like(from_left, dtype=f32)
    right = right + dot_nt(chunk_of(kv_grad, 1), kv_weights)
    right = (right + jnp.concatenate([from_left.astype(f32), empty])).astype(bf16)
    left = left + dot_nt(chunk_of(kv_grad, 3), kv_weights)
    left = (left + jnp.concatenate([empty, from_right.astype(f32)])).astype(bf16)
    part_a = send(right, joint, joint_ring(1))
    part_b = send(left, joint, joint_ring(-1))
    far_rows = send(chunk_of(kv_grad, 2), joint, joint_ring(2))
    own_rows = send(chunk_of(kv_grad, 0), "section", ring(4, -1))
    rest = own.astype(f32) + dot_nt(own_rows, own_weights) + dot_nt(far_rows, far_weights)
    rest = lax.optimization_barrier(rest)
    sent = (rest + part_a.astype(f32) + part_b.astype(f32)).astype(bf16)
    return (sent[None], key_grad[None], value_grad[None])


def solution(mesh):
    placed = (
        P(),
        P("section", "ctx", "tp"),
        P("section", "ctx", "tp"),
        P("section", "ctx", "tp"),
        P("section", ("ctx", "tp"), None),
        P("section", None, "tp"),
        P("section", None, "tp"),
        P("section", None, "tp"),
        P("section", "tp", None),
    )

    return jax.shard_map(
        per_device,
        mesh=mesh,
        in_specs=placed,
        out_specs=(
            P("section", ("ctx", "tp"), None),
            P("section", "ctx", "tp"),
            P("section", "ctx", "tp"),
        ),
        check_vma=False,
    )
```

```python
import jax
import jax.numpy as jnp
from jax import lax
from jax.experimental import pallas as pl
from jax.experimental.pallas import tpu as pltpu
from jax.sharding import PartitionSpec as P

HD = 128
BLK = 256
GROUP = 4
STEPS = 17
SCALE = HD ** (-0.5)
EXP2_SCALE = SCALE * 1.4426950408889634
NEG_LARGE = -1e30

VMEM_WHOLE = pl.BlockSpec(memory_space=pltpu.VMEM)
TP, CTX, SECTION = "tp", "ctx", "section"
PARAMS = pltpu.CompilerParams(vmem_limit_bytes=36 << 20)


def dot_nt(lhs, rhs):
    return lax.dot_general(lhs, rhs, (((1,), (1,)), ((), ())), preferred_element_type=jnp.float32)


def dot_nn(lhs, rhs):
    return lax.dot_general(lhs, rhs, (((1,), (0,)), ((), ())), preferred_element_type=jnp.float32)


def ring(size, shift):
    return [(i, (i + shift) % size) for i in range(size)]


def z_ring(shift):
    return [(x * 4 + z, x * 4 + (z + shift) % 4) for x in range(2) for z in range(4)]


X_SWAP = [(x * 4 + z, (1 - x) * 4 + z) for x in range(2) for z in range(4)]


def joint_ring(shift):
    return [(s * 4 + t, ((s - 1) % 4) * 4 + (t + shift) % 4) for s in range(4) for t in range(4)]


def step_block(step, split):
    half = (step > split).astype(jnp.int32)
    return half, step - half * (split + 1)


def step_args(step, split):
    half, kb = step_block(step, split)
    diag = ((step == split) | (step == STEPS - 1)).astype(jnp.int32)
    return half, kb, diag


def forward_kernel(split_ref, ids_ref, *refs):
    kv_refs = refs[:8]
    (
        q_ref, p_ref, out_ref, stat_ref, hist_ref, kvs_ref,
        max_ref, acc_ref, bias_ref, even_ref, odd_ref, even_top_ref, odd_top_ref,
    ) = refs[8:]
    step = pl.program_id(0)
    split = split_ref[0]
    _, kb, diag = step_args(step, split)

    def score_step(at, score_ref, top_ref):
        at_half, at_kb, at_diag = step_args(at, split)
        start = pl.multiple_of(at_half * BLK, BLK)
        key_blk = kvs_ref[at_kb, :, :HD]
        for h in range(GROUP):
            query = q_ref[pl.ds(start, BLK), h * HD : (h + 1) * HD]
            scores = dot_nt(key_blk, query) + bias_ref[at_diag]
            score_ref[h] = scores
            top_ref[0:1, h * BLK : (h + 1) * BLK] = jnp.max(scores, axis=0, keepdims=True)

    @pl.when(step == 0)
    def _():
        for j in range(8):
            for r in range(2):
                kvs_ref[ids_ref[2 * j + r]] = kv_refs[j][r * BLK : (r + 1) * BLK, :]
        gap = lax.broadcasted_iota(jnp.int32, (BLK, BLK), 0) - lax.broadcasted_iota(
            jnp.int32, (BLK, BLK), 1
        )
        bias_ref[0] = jnp.zeros((BLK, BLK), jnp.float32)
        bias_ref[1] = jnp.where(gap <= 0, 0.0, NEG_LARGE)
        max_ref[...] = jnp.full_like(max_ref, NEG_LARGE)
        acc_ref[...] = jnp.zeros_like(acc_ref)
        score_step(step, even_ref, even_top_ref)

    def softmax_step(now, now_top, later, later_top):
        score_step(jnp.minimum(step + 1, STEPS - 1), later, later_top)
        value_t = jnp.transpose(kvs_ref[kb, :, HD:].astype(jnp.float32)).astype(jnp.bfloat16)
        lhs = jnp.concatenate([value_t, jnp.ones((16, BLK), jnp.bfloat16)], axis=0)
        for h in range(GROUP):
            cols = slice(h * BLK, (h + 1) * BLK)
            old_max = jnp.where(kb == 0, NEG_LARGE, max_ref[0:1, cols])
            new_max = jnp.maximum(old_max, now_top[0:1, cols])
            probs = jnp.exp2((now[h] - new_max) * EXP2_SCALE).astype(jnp.bfloat16)
            p_ref[step, h] = probs
            factor = jnp.exp2((old_max - new_max) * EXP2_SCALE)
            acc_ref[:, cols] = acc_ref[:, cols] * factor + dot_nn(lhs, probs)
            max_ref[0:1, cols] = new_max
            hist_ref[0, 0:1, cols] = new_max

    @pl.when(step % 2 == 0)
    def _():
        softmax_step(even_ref, even_top_ref, odd_ref, odd_top_ref)

    @pl.when(step % 2 == 1)
    def _():
        softmax_step(odd_ref, odd_top_ref, even_ref, even_top_ref)

    @pl.when(diag == 1)
    def _():
        inv = 1.0 / acc_ref[HD : HD + 1, :]
        out_ref[0] = acc_ref[:HD, :] * inv
        stat_ref[0, 0:1, :] = max_ref[0:1, :]
        stat_ref[0, 1:2, :] = inv


def half_of(step, split_ref):
    return (step > split_ref[0]).astype(jnp.int32)


def block_of(step, split_ref):
    return step - half_of(step, split_ref) * (split_ref[0] + 1)


def forward_call(split, ids, kv_chunks, queries):
    whole = pl.BlockSpec((2 * BLK, 2 * HD), lambda i, s, d: (0, 0))
    wide = GROUP * BLK
    return pl.pallas_call(
        forward_kernel,
        grid_spec=pltpu.PrefetchScalarGridSpec(
            num_scalar_prefetch=2,
            grid=(STEPS,),
            in_specs=[whole] * 8 + [pl.BlockSpec((2 * BLK, GROUP * HD), lambda i, s, d: (0, 0))],
            out_specs=[
                VMEM_WHOLE,
                pl.BlockSpec((1, HD, wide), lambda i, s, d: (half_of(i, s), 0, 0)),
                pl.BlockSpec((1, 8, wide), lambda i, s, d: (half_of(i, s), 0, 0)),
                pl.BlockSpec((1, 1, wide), lambda i, s, d: (i, 0, 0)),
                pl.BlockSpec((16, BLK, 2 * HD), lambda i, s, d: (0, 0, 0)),
            ],
            scratch_shapes=[
                pltpu.VMEM((8, wide), jnp.float32),
                pltpu.VMEM((HD + 16, wide), jnp.float32),
                pltpu.VMEM((2, BLK, BLK), jnp.float32),
                pltpu.VMEM((GROUP, BLK, BLK), jnp.float32),
                pltpu.VMEM((GROUP, BLK, BLK), jnp.float32),
                pltpu.VMEM((8, wide), jnp.float32),
                pltpu.VMEM((8, wide), jnp.float32),
            ],
        ),
        out_shape=[
            jax.ShapeDtypeStruct((STEPS, GROUP, BLK, BLK), jnp.bfloat16),
            jax.ShapeDtypeStruct((2, HD, wide), jnp.float32),
            jax.ShapeDtypeStruct((2, 8, wide), jnp.float32),
            jax.ShapeDtypeStruct((STEPS, 1, wide), jnp.float32),
            jax.ShapeDtypeStruct((16, BLK, 2 * HD), jnp.bfloat16),
        ],
        compiler_params=PARAMS,
        cost_estimate=pl.CostEstimate(
            flops=2 * 2 * STEPS * wide * BLK * HD,
            bytes_accessed=13 << 20,
            transcendentals=STEPS * wide * BLK,
        ),
    )(split, ids, *kv_chunks, queries)


def grad_kernel(rows_ref, *refs):
    pieces = refs[:7]
    weight_ref, out_ref, lhs_ref, acc_ref = refs[7:]
    step = pl.program_id(0)
    depth = lhs_ref.shape[1]

    @pl.when(step == 0)
    def _():
        acc_ref[...] = jnp.zeros_like(acc_ref)

    for j, piece in enumerate(pieces):
        size = piece.shape[0]
        lhs_ref[pl.ds(pl.multiple_of(rows_ref[j], 64), size), :] = piece[...]
    start = pl.multiple_of(step * depth, depth)
    acc_ref[...] += dot_nt(lhs_ref[...], weight_ref[:, pl.ds(start, depth)])

    @pl.when(step == pl.num_programs(0) - 1)
    def _():
        out_ref[...] = acc_ref[...].astype(jnp.bfloat16)


def grad_call(rows, pieces, out_weight):
    depth = 512
    total = out_weight.shape[0]
    return pl.pallas_call(
        grad_kernel,
        grid_spec=pltpu.PrefetchScalarGridSpec(
            num_scalar_prefetch=1,
            grid=(out_weight.shape[1] // depth,),
            in_specs=[pl.BlockSpec((p.shape[0], depth), lambda i, w: (0, i)) for p in pieces]
            + [VMEM_WHOLE],
            out_specs=pl.BlockSpec((2 * BLK, total), lambda i, w: (0, 0)),
            scratch_shapes=[
                pltpu.VMEM((2 * BLK, depth), jnp.bfloat16),
                pltpu.VMEM((2 * BLK, total), jnp.float32),
            ],
        ),
        out_shape=jax.ShapeDtypeStruct((2 * BLK, total), jnp.bfloat16),
        compiler_params=PARAMS,
        cost_estimate=pl.CostEstimate(
            flops=2 * 2 * BLK * total * out_weight.shape[1],
            bytes_accessed=9 << 20,
            transcendentals=0,
        ),
        name="attn_grad",
    )(rows, *pieces, out_weight)


def norm_of(hist_ref, stat_ref, cols):
    gap = (hist_ref[0, 0:1, cols] - stat_ref[0, 0:1, cols]) * EXP2_SCALE
    return jnp.exp2(gap) * stat_ref[0, 1:2, cols]


def write_groups(ids_ref, total_ref, group_refs, scale):
    for g, g_ref in enumerate(group_refs):
        for x in range(2):
            for r in range(2):
                block = ids_ref[4 * g + 2 * x + r]
                g_ref[x, r * BLK : (r + 1) * BLK, :] = (total_ref[block] * scale).astype(
                    jnp.bfloat16
                )


def value_kernel(split_ref, ids_ref, grad_ref, p_ref, stat_ref, hist_ref, *refs):
    group_refs = refs[:4]
    total_ref = refs[4]
    step = pl.program_id(0)
    half, kb, _ = step_args(step, split_ref[0])

    @pl.when(step == 0)
    def _():
        total_ref[...] = jnp.zeros_like(total_ref)

    start = pl.multiple_of(half * BLK, BLK)
    dv = jnp.zeros((BLK, HD), jnp.float32)
    for h in range(GROUP):
        norm = norm_of(hist_ref, stat_ref, slice(h * BLK, (h + 1) * BLK))
        probs = (p_ref[step, h].astype(jnp.float32) * norm).astype(jnp.bfloat16)
        dv = dv + dot_nn(probs, grad_ref[pl.ds(start, BLK), h * HD : (h + 1) * HD])
    total_ref[kb] += dv

    @pl.when(step == STEPS - 1)
    def _():
        write_groups(ids_ref, total_ref, group_refs, 1.0)


def value_call(split, ids, grad, saved):
    probs, _, stats, hist, _ = saved
    wide = GROUP * BLK
    group_spec = pl.BlockSpec((2, 2 * BLK, HD), lambda i, s, d: (0, 0, 0))
    return pl.pallas_call(
        value_kernel,
        grid_spec=pltpu.PrefetchScalarGridSpec(
            num_scalar_prefetch=2,
            grid=(STEPS,),
            in_specs=[
                pl.BlockSpec((2 * BLK, GROUP * HD), lambda i, s, d: (0, 0)),
                VMEM_WHOLE,
                pl.BlockSpec((1, 8, wide), lambda i, s, d: (half_of(i, s), 0, 0)),
                pl.BlockSpec((1, 1, wide), lambda i, s, d: (i, 0, 0)),
            ],
            out_specs=[group_spec] * 4,
            scratch_shapes=[pltpu.VMEM((16, BLK, HD), jnp.float32)],
        ),
        out_shape=[jax.ShapeDtypeStruct((2, 2 * BLK, HD), jnp.bfloat16)] * 4,
        compiler_params=PARAMS,
        cost_estimate=pl.CostEstimate(
            flops=2 * STEPS * wide * BLK * HD, bytes_accessed=11 << 20, transcendentals=0
        ),
        name="attn_value_grad",
    )(split, ids, grad, probs, stats, hist)


def key_kernel(split_ref, ids_ref, grad_ref, q_ref, p_ref, kv_ref, next_ref, out_ref, stat_ref,
               hist_ref, *refs):
    dq_ref = refs[0]
    group_refs = refs[1:5]
    delta_ref, dqt_ref, total_ref, even_ref, odd_ref = refs[5:]
    step = pl.program_id(0)
    split = split_ref[0]
    half, kb, diag = step_args(step, split)

    def grad_probs_step(at, value_blk, gp_ref):
        at_half = (at > split).astype(jnp.int32)
        start = pl.multiple_of(at_half * BLK, BLK)
        for h in range(GROUP):
            gp_ref[h] = dot_nt(
                value_blk, grad_ref[pl.ds(start, BLK), h * HD : (h + 1) * HD]
            )

    @pl.when(step == 0)
    def _():
        total_ref[...] = jnp.zeros_like(total_ref)
        dqt_ref[...] = jnp.zeros_like(dqt_ref)
        grad_probs_step(step, kv_ref[0, :, HD:], even_ref)

    start = pl.multiple_of(half * BLK, BLK)

    @pl.when(kb == 0)
    def _():
        for h in range(GROUP):
            cols = slice(h * BLK, (h + 1) * BLK)
            grad = grad_ref[pl.ds(start, BLK), h * HD : (h + 1) * HD]
            grad_t = jnp.transpose(grad.astype(jnp.float32))
            delta_ref[0:1, cols] = jnp.sum(out_ref[0, :, cols] * grad_t, axis=0, keepdims=True)

    def main_step(now, later):
        grad_probs_step(jnp.minimum(step + 1, STEPS - 1), next_ref[0, :, HD:], later)
        key_t = jnp.transpose(kv_ref[0, :, :HD].astype(jnp.float32)).astype(jnp.bfloat16)
        keep = jnp.where(kb == 0, 0.0, 1.0)
        dk = jnp.zeros((BLK, HD), jnp.float32)
        for h in range(GROUP):
            cols = slice(h * BLK, (h + 1) * BLK)
            probs = p_ref[step, h].astype(jnp.float32) * norm_of(hist_ref, stat_ref, cols)
            dscore = (probs * (now[h] - delta_ref[0:1, cols])).astype(jnp.bfloat16)
            dk = dk + dot_nn(dscore, q_ref[pl.ds(start, BLK), h * HD : (h + 1) * HD])
            dqt_ref[:, cols] = dqt_ref[:, cols] * keep + dot_nn(key_t, dscore)
        total_ref[kb] += dk

    @pl.when(step % 2 == 0)
    def _():
        main_step(even_ref, odd_ref)

    @pl.when(step % 2 == 1)
    def _():
        main_step(odd_ref, even_ref)

    @pl.when(diag == 1)
    def _():
        for h in range(GROUP):
            cols = slice(h * BLK, (h + 1) * BLK)
            dq_ref[:, h * HD : (h + 1) * HD] = jnp.transpose(dqt_ref[:, cols] * SCALE).astype(
                jnp.bfloat16
            )

    @pl.when(step == STEPS - 1)
    def _():
        write_groups(ids_ref, total_ref, group_refs, SCALE)


def key_call(split, ids, grad, saved, queries):
    probs, outs, stats, hist, kv_sorted = saved
    wide = GROUP * BLK
    group_spec = pl.BlockSpec((2, 2 * BLK, HD), lambda i, s, d: (0, 0, 0))
    whole = pl.BlockSpec((2 * BLK, GROUP * HD), lambda i, s, d: (0, 0))

    def next_block(i, s, d):
        return (block_of(jnp.minimum(i + 1, STEPS - 1), s), 0, 0)

    return pl.pallas_call(
        key_kernel,
        grid_spec=pltpu.PrefetchScalarGridSpec(
            num_scalar_prefetch=2,
            grid=(STEPS,),
            in_specs=[
                whole,
                whole,
                VMEM_WHOLE,
                pl.BlockSpec((1, BLK, 2 * HD), lambda i, s, d: (block_of(i, s), 0, 0)),
                pl.BlockSpec((1, BLK, 2 * HD), next_block),
                pl.BlockSpec((1, HD, wide), lambda i, s, d: (half_of(i, s), 0, 0)),
                pl.BlockSpec((1, 8, wide), lambda i, s, d: (half_of(i, s), 0, 0)),
                pl.BlockSpec((1, 1, wide), lambda i, s, d: (i, 0, 0)),
            ],
            out_specs=[pl.BlockSpec((BLK, GROUP * HD), lambda i, s, d: (half_of(i, s), 0))]
            + [group_spec] * 4,
            scratch_shapes=[
                pltpu.VMEM((8, wide), jnp.float32),
                pltpu.VMEM((HD, wide), jnp.float32),
                pltpu.VMEM((16, BLK, HD), jnp.float32),
                pltpu.VMEM((GROUP, BLK, BLK), jnp.float32),
                pltpu.VMEM((GROUP, BLK, BLK), jnp.float32),
            ],
        ),
        out_shape=[jax.ShapeDtypeStruct((2 * BLK, GROUP * HD), jnp.bfloat16)]
        + [jax.ShapeDtypeStruct((2, 2 * BLK, HD), jnp.bfloat16)] * 4,
        compiler_params=PARAMS,
        cost_estimate=pl.CostEstimate(
            flops=2 * 3 * STEPS * wide * BLK * HD, bytes_accessed=14 << 20, transcendentals=0
        ),
    )(split, ids, grad, queries, probs, kv_sorted, kv_sorted, outs, stats, hist)


def per_device(
    stretch_order,
    queries,
    key_rows,
    value_rows,
    out_grad,
    query_weight,
    key_weight,
    value_weight,
    output_weight,
):
    send = lax.ppermute
    tp = lax.axis_index(TP)
    ctx = lax.axis_index(CTX)
    own_x, own_z = ctx // 4, ctx % 4
    bf16 = jnp.bfloat16

    chunk = out_grad[0]
    half_rows = chunk.shape[0] // 2
    top, low = chunk[:half_rows], chunk[half_rows:]
    left_top = send(top, TP, ring(4, 1))
    right_low = send(low, TP, ring(4, -1))
    far_top = send(left_top, TP, ring(4, 1))
    far_low = send(right_low, TP, ring(4, -1))
    left_low = send(low, TP, ring(4, 1))
    right_top = send(top, TP, ring(4, -1))

    kv_own = jnp.concatenate([key_rows[0], value_rows[0]], axis=1)
    kv_pair = send(kv_own, CTX, X_SWAP)
    along, crossed = {}, {}
    for distance, shift in ((2, 2), (1, -1), (3, 1)):
        along[distance] = send(kv_own, CTX, z_ring(shift))
    for distance, shift in ((1, -1), (3, 1)):
        crossed[distance] = send(kv_pair, CTX, z_ring(shift))
    crossed[2] = send(along[2], CTX, X_SWAP)
    kv_chunks = [kv_own, kv_pair]
    for distance in (1, 2, 3):
        kv_chunks += [along[distance], crossed[distance]]

    index = jnp.arange(8, dtype=jnp.int32)
    source = ((own_x + index % 2) % 2) * 4 + (own_z + index // 2) % 4
    table = jnp.arange(8, dtype=jnp.int32)
    ids = jnp.sum(
        jnp.where(source[:, None, None] == table[None, :, None], stretch_order[None], 0), axis=1
    ).reshape(16)
    split = ids[:1]
    saved = forward_call(split, ids, kv_chunks, queries[0])

    left, right, far = (tp + 3) % 4, (tp + 1) % 4, (tp + 2) % 4
    pieces = (chunk, left_top, left_low, right_top, right_low, far_top, far_low)
    places = (2 * tp, 2 * left, 2 * left + 1, 2 * right, 2 * right + 1, 2 * far, 2 * far + 1)
    grad = grad_call(
        (jnp.stack(places) * half_rows).astype(jnp.int32), pieces, output_weight[0]
    )

    f32 = jnp.float32

    def along_z(groups):
        total = groups[0].astype(f32)
        for distance, shift in ((1, 1), (2, 2), (3, -1)):
            received = send(groups[distance], CTX, z_ring(shift))
            total = total + received.astype(f32)
        return total

    groups, grad = lax.optimization_barrier((value_call(split, ids, grad, saved), grad))
    value_sum = along_z(groups)
    query_grad, *groups = key_call(split, ids, grad, saved, queries[0])
    key_sum = along_z(groups)

    def with_pair(total):
        received = send(total[1].astype(bf16), CTX, X_SWAP)
        return (total[0] + received.astype(f32)).astype(bf16)

    value_grad = with_pair(value_sum)
    key_grad = with_pair(key_sum)

    stacked = jnp.concatenate([query_grad, key_grad, value_grad], axis=1)
    weights = jnp.concatenate([query_weight[0], key_weight[0], value_weight[0]], axis=1)

    def term_of(distance):
        start = ((tp + distance) % 4) * 128
        rows = lax.dynamic_slice_in_dim(stacked, start, 128, 0)
        return dot_nt(rows, weights).astype(bf16)

    far = term_of(2)
    from_left = send(far[:half_rows], TP, ring(4, 1))
    from_right = send(far[half_rows:], TP, ring(4, -1))
    own_term = term_of(0)
    own = send(own_term, SECTION, ring(4, -1))
    right, left = lax.optimization_barrier((term_of(1), term_of(3)))
    empty = jnp.zeros_like(from_left, dtype=f32)
    right = (right.astype(f32) + jnp.concatenate([from_left.astype(f32), empty])).astype(bf16)
    left = (left.astype(f32) + jnp.concatenate([empty, from_right.astype(f32)])).astype(bf16)
    joint = (SECTION, TP)
    part_a = send(right, joint, joint_ring(1))
    part_b = send(left, joint, joint_ring(-1))
    sent = (own.astype(f32) + part_a.astype(f32) + part_b.astype(f32)).astype(bf16)
    return (sent[None], key_grad[None], value_grad[None])


def solution(mesh):
    placed = (
        P(),
        P(SECTION, CTX, TP),
        P(SECTION, CTX, TP),
        P(SECTION, CTX, TP),
        P(SECTION, (CTX, TP), None),
        P(SECTION, None, TP),
        P(SECTION, None, TP),
        P(SECTION, None, TP),
        P(SECTION, TP, None),
    )

    return jax.shard_map(
        per_device,
        mesh=mesh,
        in_specs=placed,
        out_specs=(
            P(SECTION, (CTX, TP), None),
            P(SECTION, CTX, TP),
            P(SECTION, CTX, TP),
        ),
        check_vma=False,
    )
```

```python
import jax
import jax.numpy as jnp
from jax import lax
from jax.experimental import pallas as pl
from jax.experimental.pallas import tpu as pltpu
from jax.sharding import PartitionSpec as P

HD = 128
BLK = 256
GROUP = 4
STEPS = 17
SCALE = HD ** (-0.5)
EXP2_SCALE = SCALE * 1.4426950408889634
NEG_LARGE = -1e30

VMEM_WHOLE = pl.BlockSpec(memory_space=pltpu.VMEM)
TP, CTX, SECTION = "tp", "ctx", "section"
PARAMS = pltpu.CompilerParams(vmem_limit_bytes=36 << 20)


def dot_nt(lhs, rhs):
    return lax.dot_general(lhs, rhs, (((1,), (1,)), ((), ())), preferred_element_type=jnp.float32)


def dot_nn(lhs, rhs):
    return lax.dot_general(lhs, rhs, (((1,), (0,)), ((), ())), preferred_element_type=jnp.float32)


def ring(size, shift):
    return [(i, (i + shift) % size) for i in range(size)]


def z_ring(shift):
    return [(x * 4 + z, x * 4 + (z + shift) % 4) for x in range(2) for z in range(4)]


X_SWAP = [(x * 4 + z, (1 - x) * 4 + z) for x in range(2) for z in range(4)]


def joint_ring(shift):
    return [(s * 4 + t, ((s - 1) % 4) * 4 + (t + shift) % 4) for s in range(4) for t in range(4)]


def step_block(step, split):
    half = (step > split).astype(jnp.int32)
    return half, step - half * (split + 1)


def step_args(step, split):
    half, kb = step_block(step, split)
    diag = ((step == split) | (step == STEPS - 1)).astype(jnp.int32)
    return half, kb, diag


def forward_kernel(split_ref, ids_ref, *refs):
    kv_refs = refs[:8]
    (
        q_ref, p_ref, out_ref, stat_ref, hist_ref, kvs_ref,
        max_ref, acc_ref, bias_ref, even_ref, odd_ref, even_top_ref, odd_top_ref,
    ) = refs[8:]
    step = pl.program_id(0)
    split = split_ref[0]
    _, kb, diag = step_args(step, split)

    def score_step(at, score_ref, top_ref):
        at_half, at_kb, at_diag = step_args(at, split)
        start = pl.multiple_of(at_half * BLK, BLK)
        key_blk = kvs_ref[at_kb, :, :HD]
        for h in range(GROUP):
            query = q_ref[pl.ds(start, BLK), h * HD : (h + 1) * HD]
            scores = dot_nt(key_blk, query) + bias_ref[at_diag]
            score_ref[h] = scores
            top_ref[0:1, h * BLK : (h + 1) * BLK] = jnp.max(scores, axis=0, keepdims=True)

    @pl.when(step == 0)
    def _():
        for j in range(8):
            for r in range(2):
                kvs_ref[ids_ref[2 * j + r]] = kv_refs[j][r * BLK : (r + 1) * BLK, :]
        gap = lax.broadcasted_iota(jnp.int32, (BLK, BLK), 0) - lax.broadcasted_iota(
            jnp.int32, (BLK, BLK), 1
        )
        bias_ref[0] = jnp.zeros((BLK, BLK), jnp.float32)
        bias_ref[1] = jnp.where(gap <= 0, 0.0, NEG_LARGE)
        max_ref[...] = jnp.full_like(max_ref, NEG_LARGE)
        acc_ref[...] = jnp.zeros_like(acc_ref)
        score_step(step, even_ref, even_top_ref)

    def softmax_step(now, now_top, later, later_top):
        score_step(jnp.minimum(step + 1, STEPS - 1), later, later_top)
        value_t = jnp.transpose(kvs_ref[kb, :, HD:].astype(jnp.float32)).astype(jnp.bfloat16)
        lhs = jnp.concatenate([value_t, jnp.ones((16, BLK), jnp.bfloat16)], axis=0)
        for h in range(GROUP):
            cols = slice(h * BLK, (h + 1) * BLK)
            old_max = jnp.where(kb == 0, NEG_LARGE, max_ref[0:1, cols])
            new_max = jnp.maximum(old_max, now_top[0:1, cols])
            probs = jnp.exp2((now[h] - new_max) * EXP2_SCALE).astype(jnp.bfloat16)
            p_ref[step, h] = probs
            factor = jnp.exp2((old_max - new_max) * EXP2_SCALE)
            acc_ref[:, cols] = acc_ref[:, cols] * factor + dot_nn(lhs, probs)
            max_ref[0:1, cols] = new_max
            hist_ref[0, 0:1, cols] = new_max

    @pl.when(step % 2 == 0)
    def _():
        softmax_step(even_ref, even_top_ref, odd_ref, odd_top_ref)

    @pl.when(step % 2 == 1)
    def _():
        softmax_step(odd_ref, odd_top_ref, even_ref, even_top_ref)

    @pl.when(diag == 1)
    def _():
        inv = 1.0 / acc_ref[HD : HD + 1, :]
        out_ref[0] = acc_ref[:HD, :] * inv
        stat_ref[0, 0:1, :] = max_ref[0:1, :]
        stat_ref[0, 1:2, :] = inv


def half_of(step, split_ref):
    return (step > split_ref[0]).astype(jnp.int32)


def block_of(step, split_ref):
    return step - half_of(step, split_ref) * (split_ref[0] + 1)


def forward_call(split, ids, kv_chunks, queries):
    whole = pl.BlockSpec((2 * BLK, 2 * HD), lambda i, s, d: (0, 0))
    wide = GROUP * BLK
    return pl.pallas_call(
        forward_kernel,
        grid_spec=pltpu.PrefetchScalarGridSpec(
            num_scalar_prefetch=2,
            grid=(STEPS,),
            in_specs=[whole] * 8 + [pl.BlockSpec((2 * BLK, GROUP * HD), lambda i, s, d: (0, 0))],
            out_specs=[
                VMEM_WHOLE,
                pl.BlockSpec((1, HD, wide), lambda i, s, d: (half_of(i, s), 0, 0)),
                pl.BlockSpec((1, 8, wide), lambda i, s, d: (half_of(i, s), 0, 0)),
                pl.BlockSpec((1, 1, wide), lambda i, s, d: (i, 0, 0)),
                pl.BlockSpec((16, BLK, 2 * HD), lambda i, s, d: (0, 0, 0)),
            ],
            scratch_shapes=[
                pltpu.VMEM((8, wide), jnp.float32),
                pltpu.VMEM((HD + 16, wide), jnp.float32),
                pltpu.VMEM((2, BLK, BLK), jnp.float32),
                pltpu.VMEM((GROUP, BLK, BLK), jnp.float32),
                pltpu.VMEM((GROUP, BLK, BLK), jnp.float32),
                pltpu.VMEM((8, wide), jnp.float32),
                pltpu.VMEM((8, wide), jnp.float32),
            ],
        ),
        out_shape=[
            jax.ShapeDtypeStruct((STEPS, GROUP, BLK, BLK), jnp.bfloat16),
            jax.ShapeDtypeStruct((2, HD, wide), jnp.float32),
            jax.ShapeDtypeStruct((2, 8, wide), jnp.float32),
            jax.ShapeDtypeStruct((STEPS, 1, wide), jnp.float32),
            jax.ShapeDtypeStruct((16, BLK, 2 * HD), jnp.bfloat16),
        ],
        compiler_params=PARAMS,
        cost_estimate=pl.CostEstimate(
            flops=2 * 2 * STEPS * wide * BLK * HD,
            bytes_accessed=13 << 20,
            transcendentals=STEPS * wide * BLK,
        ),
    )(split, ids, *kv_chunks, queries)


def grad_kernel(rows_ref, *refs):
    pieces = refs[:7]
    weight_ref, out_ref, lhs_ref, acc_ref = refs[7:]
    step = pl.program_id(0)
    depth = lhs_ref.shape[1]

    @pl.when(step == 0)
    def _():
        acc_ref[...] = jnp.zeros_like(acc_ref)

    for j, piece in enumerate(pieces):
        size = piece.shape[0]
        lhs_ref[pl.ds(pl.multiple_of(rows_ref[j], 64), size), :] = piece[...]
    start = pl.multiple_of(step * depth, depth)
    acc_ref[...] += dot_nt(lhs_ref[...], weight_ref[:, pl.ds(start, depth)])

    @pl.when(step == pl.num_programs(0) - 1)
    def _():
        out_ref[...] = acc_ref[...].astype(jnp.bfloat16)


def grad_call(rows, pieces, out_weight):
    depth = 1024
    total = out_weight.shape[0]
    return pl.pallas_call(
        grad_kernel,
        grid_spec=pltpu.PrefetchScalarGridSpec(
            num_scalar_prefetch=1,
            grid=(out_weight.shape[1] // depth,),
            in_specs=[pl.BlockSpec((p.shape[0], depth), lambda i, w: (0, i)) for p in pieces]
            + [VMEM_WHOLE],
            out_specs=pl.BlockSpec((2 * BLK, total), lambda i, w: (0, 0)),
            scratch_shapes=[
                pltpu.VMEM((2 * BLK, depth), jnp.bfloat16),
                pltpu.VMEM((2 * BLK, total), jnp.float32),
            ],
        ),
        out_shape=jax.ShapeDtypeStruct((2 * BLK, total), jnp.bfloat16),
        compiler_params=PARAMS,
        cost_estimate=pl.CostEstimate(
            flops=2 * 2 * BLK * total * out_weight.shape[1],
            bytes_accessed=9 << 20,
            transcendentals=0,
        ),
        name="attn_grad",
    )(rows, *pieces, out_weight)


def norm_of(hist_ref, stat_ref, cols):
    gap = (hist_ref[0, 0:1, cols] - stat_ref[0, 0:1, cols]) * EXP2_SCALE
    return jnp.exp2(gap) * stat_ref[0, 1:2, cols]


def write_groups(ids_ref, total_ref, group_refs, scale):
    for g, g_ref in enumerate(group_refs):
        for x in range(2):
            for r in range(2):
                block = ids_ref[4 * g + 2 * x + r]
                g_ref[x, r * BLK : (r + 1) * BLK, :] = (total_ref[block] * scale).astype(
                    jnp.bfloat16
                )


def value_kernel(split_ref, ids_ref, grad_ref, p_ref, stat_ref, hist_ref, *refs):
    group_refs = refs[:4]
    total_ref = refs[4]
    step = pl.program_id(0)
    half, kb, _ = step_args(step, split_ref[0])

    @pl.when(step == 0)
    def _():
        total_ref[...] = jnp.zeros_like(total_ref)

    start = pl.multiple_of(half * BLK, BLK)
    dv = jnp.zeros((BLK, HD), jnp.float32)
    for h in range(GROUP):
        norm = norm_of(hist_ref, stat_ref, slice(h * BLK, (h + 1) * BLK))
        probs = (p_ref[step, h].astype(jnp.float32) * norm).astype(jnp.bfloat16)
        dv = dv + dot_nn(probs, grad_ref[pl.ds(start, BLK), h * HD : (h + 1) * HD])
    total_ref[kb] += dv

    @pl.when(step == STEPS - 1)
    def _():
        write_groups(ids_ref, total_ref, group_refs, 1.0)


def value_call(split, ids, grad, saved):
    probs, _, stats, hist, _ = saved
    wide = GROUP * BLK
    group_spec = pl.BlockSpec((2, 2 * BLK, HD), lambda i, s, d: (0, 0, 0))
    return pl.pallas_call(
        value_kernel,
        grid_spec=pltpu.PrefetchScalarGridSpec(
            num_scalar_prefetch=2,
            grid=(STEPS,),
            in_specs=[
                pl.BlockSpec((2 * BLK, GROUP * HD), lambda i, s, d: (0, 0)),
                VMEM_WHOLE,
                pl.BlockSpec((1, 8, wide), lambda i, s, d: (half_of(i, s), 0, 0)),
                pl.BlockSpec((1, 1, wide), lambda i, s, d: (i, 0, 0)),
            ],
            out_specs=[group_spec] * 4,
            scratch_shapes=[pltpu.VMEM((16, BLK, HD), jnp.float32)],
        ),
        out_shape=[jax.ShapeDtypeStruct((2, 2 * BLK, HD), jnp.bfloat16)] * 4,
        compiler_params=PARAMS,
        cost_estimate=pl.CostEstimate(
            flops=2 * STEPS * wide * BLK * HD, bytes_accessed=11 << 20, transcendentals=0
        ),
        name="attn_value_grad",
    )(split, ids, grad, probs, stats, hist)


def key_kernel(split_ref, ids_ref, grad_ref, q_ref, p_ref, kv_ref, next_ref, out_ref, stat_ref,
               hist_ref, *refs):
    dq_ref = refs[0]
    group_refs = refs[1:5]
    delta_ref, dqt_ref, total_ref, even_ref, odd_ref = refs[5:]
    step = pl.program_id(0)
    split = split_ref[0]
    half, kb, diag = step_args(step, split)

    def grad_probs_step(at, value_blk, gp_ref):
        at_half = (at > split).astype(jnp.int32)
        start = pl.multiple_of(at_half * BLK, BLK)
        for h in range(GROUP):
            gp_ref[h] = dot_nt(
                value_blk, grad_ref[pl.ds(start, BLK), h * HD : (h + 1) * HD]
            )

    @pl.when(step == 0)
    def _():
        total_ref[...] = jnp.zeros_like(total_ref)
        dqt_ref[...] = jnp.zeros_like(dqt_ref)
        grad_probs_step(step, kv_ref[0, :, HD:], even_ref)

    start = pl.multiple_of(half * BLK, BLK)

    @pl.when(kb == 0)
    def _():
        for h in range(GROUP):
            cols = slice(h * BLK, (h + 1) * BLK)
            grad = grad_ref[pl.ds(start, BLK), h * HD : (h + 1) * HD]
            grad_t = jnp.transpose(grad.astype(jnp.float32))
            delta_ref[0:1, cols] = jnp.sum(out_ref[0, :, cols] * grad_t, axis=0, keepdims=True)

    def main_step(now, later):
        grad_probs_step(jnp.minimum(step + 1, STEPS - 1), next_ref[0, :, HD:], later)
        key_t = jnp.transpose(kv_ref[0, :, :HD].astype(jnp.float32)).astype(jnp.bfloat16)
        keep = jnp.where(kb == 0, 0.0, 1.0)
        dk = jnp.zeros((BLK, HD), jnp.float32)
        for h in range(GROUP):
            cols = slice(h * BLK, (h + 1) * BLK)
            probs = p_ref[step, h].astype(jnp.float32) * norm_of(hist_ref, stat_ref, cols)
            dscore = (probs * (now[h] - delta_ref[0:1, cols])).astype(jnp.bfloat16)
            dk = dk + dot_nn(dscore, q_ref[pl.ds(start, BLK), h * HD : (h + 1) * HD])
            dqt_ref[:, cols] = dqt_ref[:, cols] * keep + dot_nn(key_t, dscore)
        total_ref[kb] += dk

    @pl.when(step % 2 == 0)
    def _():
        main_step(even_ref, odd_ref)

    @pl.when(step % 2 == 1)
    def _():
        main_step(odd_ref, even_ref)

    @pl.when(diag == 1)
    def _():
        for h in range(GROUP):
            cols = slice(h * BLK, (h + 1) * BLK)
            dq_ref[:, h * HD : (h + 1) * HD] = jnp.transpose(dqt_ref[:, cols] * SCALE).astype(
                jnp.bfloat16
            )

    @pl.when(step == STEPS - 1)
    def _():
        write_groups(ids_ref, total_ref, group_refs, SCALE)


def key_call(split, ids, grad, saved, queries):
    probs, outs, stats, hist, kv_sorted = saved
    wide = GROUP * BLK
    group_spec = pl.BlockSpec((2, 2 * BLK, HD), lambda i, s, d: (0, 0, 0))
    whole = pl.BlockSpec((2 * BLK, GROUP * HD), lambda i, s, d: (0, 0))

    def next_block(i, s, d):
        return (block_of(jnp.minimum(i + 1, STEPS - 1), s), 0, 0)

    return pl.pallas_call(
        key_kernel,
        grid_spec=pltpu.PrefetchScalarGridSpec(
            num_scalar_prefetch=2,
            grid=(STEPS,),
            in_specs=[
                whole,
                whole,
                VMEM_WHOLE,
                pl.BlockSpec((1, BLK, 2 * HD), lambda i, s, d: (block_of(i, s), 0, 0)),
                pl.BlockSpec((1, BLK, 2 * HD), next_block),
                pl.BlockSpec((1, HD, wide), lambda i, s, d: (half_of(i, s), 0, 0)),
                pl.BlockSpec((1, 8, wide), lambda i, s, d: (half_of(i, s), 0, 0)),
                pl.BlockSpec((1, 1, wide), lambda i, s, d: (i, 0, 0)),
            ],
            out_specs=[pl.BlockSpec((BLK, GROUP * HD), lambda i, s, d: (half_of(i, s), 0))]
            + [group_spec] * 4,
            scratch_shapes=[
                pltpu.VMEM((8, wide), jnp.float32),
                pltpu.VMEM((HD, wide), jnp.float32),
                pltpu.VMEM((16, BLK, HD), jnp.float32),
                pltpu.VMEM((GROUP, BLK, BLK), jnp.float32),
                pltpu.VMEM((GROUP, BLK, BLK), jnp.float32),
            ],
        ),
        out_shape=[jax.ShapeDtypeStruct((2 * BLK, GROUP * HD), jnp.bfloat16)]
        + [jax.ShapeDtypeStruct((2, 2 * BLK, HD), jnp.bfloat16)] * 4,
        compiler_params=PARAMS,
        cost_estimate=pl.CostEstimate(
            flops=2 * 3 * STEPS * wide * BLK * HD, bytes_accessed=14 << 20, transcendentals=0
        ),
    )(split, ids, grad, queries, probs, kv_sorted, kv_sorted, outs, stats, hist)


def per_device(
    stretch_order,
    queries,
    key_rows,
    value_rows,
    out_grad,
    query_weight,
    key_weight,
    value_weight,
    output_weight,
):
    send = lax.ppermute
    tp = lax.axis_index(TP)
    ctx = lax.axis_index(CTX)
    own_x, own_z = ctx // 4, ctx % 4
    bf16 = jnp.bfloat16

    chunk = out_grad[0]
    half_rows = chunk.shape[0] // 2
    top, low = chunk[:half_rows], chunk[half_rows:]
    left_top = send(top, TP, ring(4, 1))
    right_low = send(low, TP, ring(4, -1))
    far_top = send(left_top, TP, ring(4, 1))
    far_low = send(right_low, TP, ring(4, -1))
    left_low = send(low, TP, ring(4, 1))
    right_top = send(top, TP, ring(4, -1))

    kv_own = jnp.concatenate([key_rows[0], value_rows[0]], axis=1)
    kv_pair = send(kv_own, CTX, X_SWAP)
    along, crossed = {}, {}
    for distance, shift in ((2, 2), (1, -1), (3, 1)):
        along[distance] = send(kv_own, CTX, z_ring(shift))
    for distance, shift in ((1, -1), (3, 1)):
        crossed[distance] = send(kv_pair, CTX, z_ring(shift))
    crossed[2] = send(along[2], CTX, X_SWAP)
    kv_chunks = [kv_own, kv_pair]
    for distance in (1, 2, 3):
        kv_chunks += [along[distance], crossed[distance]]

    index = jnp.arange(8, dtype=jnp.int32)
    source = ((own_x + index % 2) % 2) * 4 + (own_z + index // 2) % 4
    table = jnp.arange(8, dtype=jnp.int32)
    ids = jnp.sum(
        jnp.where(source[:, None, None] == table[None, :, None], stretch_order[None], 0), axis=1
    ).reshape(16)
    split = ids[:1]
    saved = forward_call(split, ids, kv_chunks, queries[0])

    left, right, far = (tp + 3) % 4, (tp + 1) % 4, (tp + 2) % 4
    pieces = (chunk, left_top, left_low, right_top, right_low, far_top, far_low)
    places = (2 * tp, 2 * left, 2 * left + 1, 2 * right, 2 * right + 1, 2 * far, 2 * far + 1)
    grad = grad_call(
        (jnp.stack(places) * half_rows).astype(jnp.int32), pieces, output_weight[0]
    )

    f32 = jnp.float32

    def along_z(groups):
        total = groups[0].astype(f32)
        for distance, shift in ((1, 1), (2, 2), (3, -1)):
            received = send(groups[distance], CTX, z_ring(shift))
            total = total + received.astype(f32)
        return total

    groups, grad = lax.optimization_barrier((value_call(split, ids, grad, saved), grad))
    value_sum = along_z(groups)
    query_grad, *groups = key_call(split, ids, grad, saved, queries[0])
    key_sum = along_z(groups)

    def with_pair(total):
        received = send(total[1].astype(bf16), CTX, X_SWAP)
        return (total[0] + received.astype(f32)).astype(bf16)

    def chunk_of(array, distance):
        return lax.dynamic_slice_in_dim(array, ((tp + distance) % 4) * 128, 128, 0)

    query_terms = []
    for distance in range(4):
        query_terms.append(dot_nt(chunk_of(query_grad, distance), query_weight[0]))
    query_terms = lax.optimization_barrier(tuple(query_terms))

    value_grad = with_pair(value_sum)
    key_grad = with_pair(key_sum)

    kv_grad = jnp.concatenate([key_grad, value_grad], axis=1)
    kv_weights = jnp.concatenate([key_weight[0], value_weight[0]], axis=1)

    def term_of(distance):
        rows = chunk_of(kv_grad, distance)
        return (query_terms[distance] + dot_nt(rows, kv_weights)).astype(bf16)

    far = term_of(2)
    from_left = send(far[:half_rows], TP, ring(4, 1))
    from_right = send(far[half_rows:], TP, ring(4, -1))
    own_term = term_of(0)
    own = send(own_term, SECTION, ring(4, -1))
    right, left = lax.optimization_barrier((term_of(1), term_of(3)))
    joint = (SECTION, TP)
    low_a = send(right[half_rows:], joint, joint_ring(1))
    top_b = send(left[:half_rows], joint, joint_ring(-1))
    top_a = (right[:half_rows].astype(f32) + from_left.astype(f32)).astype(bf16)
    top_a = send(top_a, joint, joint_ring(1))
    low_b = (left[half_rows:].astype(f32) + from_right.astype(f32)).astype(bf16)
    low_b = send(low_b, joint, joint_ring(-1))
    sent = jnp.concatenate(
        [
            own[:half_rows].astype(f32) + top_a.astype(f32) + top_b.astype(f32),
            own[half_rows:].astype(f32) + low_a.astype(f32) + low_b.astype(f32),
        ],
        axis=0,
    ).astype(bf16)
    return (sent[None], key_grad[None], value_grad[None])


def solution(mesh):
    placed = (
        P(),
        P(SECTION, CTX, TP),
        P(SECTION, CTX, TP),
        P(SECTION, CTX, TP),
        P(SECTION, (CTX, TP), None),
        P(SECTION, None, TP),
        P(SECTION, None, TP),
        P(SECTION, None, TP),
        P(SECTION, TP, None),
    )

    return jax.shard_map(
        per_device,
        mesh=mesh,
        in_specs=placed,
        out_specs=(
            P(SECTION, (CTX, TP), None),
            P(SECTION, CTX, TP),
            P(SECTION, CTX, TP),
        ),
        check_vma=False,
    )
```

```python
import jax
import jax.numpy as jnp
from jax import lax
from jax.experimental import pallas as pl
from jax.experimental.pallas import tpu as pltpu
from jax.sharding import PartitionSpec as P

HD = 128
BLK = 256
GROUP = 4
STEPS = 17
SCALE = HD ** (-0.5)
EXP2_SCALE = SCALE * 1.4426950408889634
NEG_LARGE = -1e30

VMEM_WHOLE = pl.BlockSpec(memory_space=pltpu.VMEM)
TP, CTX, SECTION = "tp", "ctx", "section"
PARAMS = pltpu.CompilerParams(vmem_limit_bytes=36 << 20)


def dot_nt(lhs, rhs):
    return lax.dot_general(lhs, rhs, (((1,), (1,)), ((), ())), preferred_element_type=jnp.float32)


def dot_nn(lhs, rhs):
    return lax.dot_general(lhs, rhs, (((1,), (0,)), ((), ())), preferred_element_type=jnp.float32)


def ring(size, shift):
    return [(i, (i + shift) % size) for i in range(size)]


def z_ring(shift):
    return [(x * 4 + z, x * 4 + (z + shift) % 4) for x in range(2) for z in range(4)]


X_SWAP = [(x * 4 + z, (1 - x) * 4 + z) for x in range(2) for z in range(4)]


def joint_ring(shift):
    return [(s * 4 + t, ((s - 1) % 4) * 4 + (t + shift) % 4) for s in range(4) for t in range(4)]


def step_block(step, split):
    half = (step > split).astype(jnp.int32)
    return half, step - half * (split + 1)


def step_args(step, split):
    half, kb = step_block(step, split)
    diag = ((step == split) | (step == STEPS - 1)).astype(jnp.int32)
    return half, kb, diag


def forward_kernel(split_ref, ids_ref, *refs):
    kv_refs = refs[:8]
    (
        q_ref, p_ref, out_ref, stat_ref, hist_ref, kvs_ref,
        max_ref, acc_ref, bias_ref, even_ref, odd_ref, even_top_ref, odd_top_ref,
    ) = refs[8:]
    step = pl.program_id(0)
    split = split_ref[0]
    _, kb, diag = step_args(step, split)

    def score_step(at, score_ref, top_ref):
        at_half, at_kb, at_diag = step_args(at, split)
        start = pl.multiple_of(at_half * BLK, BLK)
        key_blk = kvs_ref[at_kb, :, :HD]
        for h in range(GROUP):
            query = q_ref[pl.ds(start, BLK), h * HD : (h + 1) * HD]
            scores = dot_nt(key_blk, query) + bias_ref[at_diag]
            score_ref[h] = scores
            top_ref[0:1, h * BLK : (h + 1) * BLK] = jnp.max(scores, axis=0, keepdims=True)

    @pl.when(step == 0)
    def _():
        for j in range(8):
            for r in range(2):
                kvs_ref[ids_ref[2 * j + r]] = kv_refs[j][r * BLK : (r + 1) * BLK, :]
        gap = lax.broadcasted_iota(jnp.int32, (BLK, BLK), 0) - lax.broadcasted_iota(
            jnp.int32, (BLK, BLK), 1
        )
        bias_ref[0] = jnp.zeros((BLK, BLK), jnp.float32)
        bias_ref[1] = jnp.where(gap <= 0, 0.0, NEG_LARGE)
        max_ref[...] = jnp.full_like(max_ref, NEG_LARGE)
        acc_ref[...] = jnp.zeros_like(acc_ref)
        score_step(step, even_ref, even_top_ref)

    def softmax_step(now, now_top, later, later_top):
        score_step(jnp.minimum(step + 1, STEPS - 1), later, later_top)
        value_t = jnp.transpose(kvs_ref[kb, :, HD:].astype(jnp.float32)).astype(jnp.bfloat16)
        lhs = jnp.concatenate([value_t, jnp.ones((16, BLK), jnp.bfloat16)], axis=0)
        for h in range(GROUP):
            cols = slice(h * BLK, (h + 1) * BLK)
            old_max = jnp.where(kb == 0, NEG_LARGE, max_ref[0:1, cols])
            new_max = jnp.maximum(old_max, now_top[0:1, cols])
            probs = jnp.exp2((now[h] - new_max) * EXP2_SCALE).astype(jnp.bfloat16)
            p_ref[step, h] = probs
            factor = jnp.exp2((old_max - new_max) * EXP2_SCALE)
            acc_ref[:, cols] = acc_ref[:, cols] * factor + dot_nn(lhs, probs)
            max_ref[0:1, cols] = new_max
            hist_ref[0, 0:1, cols] = new_max

    @pl.when(step % 2 == 0)
    def _():
        softmax_step(even_ref, even_top_ref, odd_ref, odd_top_ref)

    @pl.when(step % 2 == 1)
    def _():
        softmax_step(odd_ref, odd_top_ref, even_ref, even_top_ref)

    @pl.when(diag == 1)
    def _():
        inv = 1.0 / acc_ref[HD : HD + 1, :]
        out_ref[0] = acc_ref[:HD, :] * inv
        stat_ref[0, 0:1, :] = max_ref[0:1, :]
        stat_ref[0, 1:2, :] = inv


def half_of(step, split_ref):
    return (step > split_ref[0]).astype(jnp.int32)


def block_of(step, split_ref):
    return step - half_of(step, split_ref) * (split_ref[0] + 1)


def forward_call(split, ids, kv_chunks, queries):
    whole = pl.BlockSpec((2 * BLK, 2 * HD), lambda i, s, d: (0, 0))
    wide = GROUP * BLK
    return pl.pallas_call(
        forward_kernel,
        grid_spec=pltpu.PrefetchScalarGridSpec(
            num_scalar_prefetch=2,
            grid=(STEPS,),
            in_specs=[whole] * 8 + [pl.BlockSpec((2 * BLK, GROUP * HD), lambda i, s, d: (0, 0))],
            out_specs=[
                VMEM_WHOLE,
                pl.BlockSpec((1, HD, wide), lambda i, s, d: (half_of(i, s), 0, 0)),
                pl.BlockSpec((1, 8, wide), lambda i, s, d: (half_of(i, s), 0, 0)),
                pl.BlockSpec((1, 1, wide), lambda i, s, d: (i, 0, 0)),
                pl.BlockSpec((16, BLK, 2 * HD), lambda i, s, d: (0, 0, 0)),
            ],
            scratch_shapes=[
                pltpu.VMEM((8, wide), jnp.float32),
                pltpu.VMEM((HD + 16, wide), jnp.float32),
                pltpu.VMEM((2, BLK, BLK), jnp.float32),
                pltpu.VMEM((GROUP, BLK, BLK), jnp.float32),
                pltpu.VMEM((GROUP, BLK, BLK), jnp.float32),
                pltpu.VMEM((8, wide), jnp.float32),
                pltpu.VMEM((8, wide), jnp.float32),
            ],
        ),
        out_shape=[
            jax.ShapeDtypeStruct((STEPS, GROUP, BLK, BLK), jnp.bfloat16),
            jax.ShapeDtypeStruct((2, HD, wide), jnp.float32),
            jax.ShapeDtypeStruct((2, 8, wide), jnp.float32),
            jax.ShapeDtypeStruct((STEPS, 1, wide), jnp.float32),
            jax.ShapeDtypeStruct((16, BLK, 2 * HD), jnp.bfloat16),
        ],
        compiler_params=PARAMS,
        cost_estimate=pl.CostEstimate(
            flops=2 * 2 * STEPS * wide * BLK * HD,
            bytes_accessed=13 << 20,
            transcendentals=STEPS * wide * BLK,
        ),
    )(split, ids, *kv_chunks, queries)


def grad_kernel(rows_ref, *refs):
    pieces = refs[:7]
    weight_ref, out_ref, lhs_ref, acc_ref = refs[7:]
    step = pl.program_id(0)
    depth = lhs_ref.shape[1]

    @pl.when(step == 0)
    def _():
        acc_ref[...] = jnp.zeros_like(acc_ref)

    for j, piece in enumerate(pieces):
        size = piece.shape[0]
        lhs_ref[pl.ds(pl.multiple_of(rows_ref[j], 64), size), :] = piece[...]
    start = pl.multiple_of(step * depth, depth)
    acc_ref[...] += dot_nt(lhs_ref[...], weight_ref[:, pl.ds(start, depth)])

    @pl.when(step == pl.num_programs(0) - 1)
    def _():
        out_ref[...] = acc_ref[...].astype(jnp.bfloat16)


def grad_call(rows, pieces, out_weight):
    depth = 1024
    total = out_weight.shape[0]
    return pl.pallas_call(
        grad_kernel,
        grid_spec=pltpu.PrefetchScalarGridSpec(
            num_scalar_prefetch=1,
            grid=(out_weight.shape[1] // depth,),
            in_specs=[pl.BlockSpec((p.shape[0], depth), lambda i, w: (0, i)) for p in pieces]
            + [VMEM_WHOLE],
            out_specs=pl.BlockSpec((2 * BLK, total), lambda i, w: (0, 0)),
            scratch_shapes=[
                pltpu.VMEM((2 * BLK, depth), jnp.bfloat16),
                pltpu.VMEM((2 * BLK, total), jnp.float32),
            ],
        ),
        out_shape=jax.ShapeDtypeStruct((2 * BLK, total), jnp.bfloat16),
        compiler_params=PARAMS,
        cost_estimate=pl.CostEstimate(
            flops=2 * 2 * BLK * total * out_weight.shape[1],
            bytes_accessed=9 << 20,
            transcendentals=0,
        ),
    )(rows, *pieces, out_weight)


def norm_of(hist_ref, stat_ref, cols):
    gap = (hist_ref[0, 0:1, cols] - stat_ref[0, 0:1, cols]) * EXP2_SCALE
    return jnp.exp2(gap) * stat_ref[0, 1:2, cols]


def write_groups(ids_ref, total_ref, group_refs, scale):
    for g, g_ref in enumerate(group_refs):
        for x in range(2):
            for r in range(2):
                block = ids_ref[4 * g + 2 * x + r]
                g_ref[x, r * BLK : (r + 1) * BLK, :] = (total_ref[block] * scale).astype(
                    jnp.bfloat16
                )


def value_kernel(split_ref, ids_ref, grad_ref, p_ref, stat_ref, hist_ref, *refs):
    group_refs = refs[:4]
    total_ref = refs[4]
    step = pl.program_id(0)
    half, kb, _ = step_args(step, split_ref[0])

    @pl.when(step == 0)
    def _():
        total_ref[...] = jnp.zeros_like(total_ref)

    start = pl.multiple_of(half * BLK, BLK)
    dv = jnp.zeros((BLK, HD), jnp.float32)
    for h in range(GROUP):
        norm = norm_of(hist_ref, stat_ref, slice(h * BLK, (h + 1) * BLK))
        probs = (p_ref[step, h].astype(jnp.float32) * norm).astype(jnp.bfloat16)
        dv = dv + dot_nn(probs, grad_ref[pl.ds(start, BLK), h * HD : (h + 1) * HD])
    total_ref[kb] += dv

    @pl.when(step == STEPS - 1)
    def _():
        write_groups(ids_ref, total_ref, group_refs, 1.0)


def value_call(split, ids, grad, saved):
    probs, _, stats, hist, _ = saved
    wide = GROUP * BLK
    group_spec = pl.BlockSpec((2, 2 * BLK, HD), lambda i, s, d: (0, 0, 0))
    return pl.pallas_call(
        value_kernel,
        grid_spec=pltpu.PrefetchScalarGridSpec(
            num_scalar_prefetch=2,
            grid=(STEPS,),
            in_specs=[
                pl.BlockSpec((2 * BLK, GROUP * HD), lambda i, s, d: (0, 0)),
                VMEM_WHOLE,
                pl.BlockSpec((1, 8, wide), lambda i, s, d: (half_of(i, s), 0, 0)),
                pl.BlockSpec((1, 1, wide), lambda i, s, d: (i, 0, 0)),
            ],
            out_specs=[group_spec] * 4,
            scratch_shapes=[pltpu.VMEM((16, BLK, HD), jnp.float32)],
        ),
        out_shape=[jax.ShapeDtypeStruct((2, 2 * BLK, HD), jnp.bfloat16)] * 4,
        compiler_params=PARAMS,
        cost_estimate=pl.CostEstimate(
            flops=2 * STEPS * wide * BLK * HD, bytes_accessed=11 << 20, transcendentals=0
        ),
        name="attn_value_grad",
    )(split, ids, grad, probs, stats, hist)


def key_kernel(split_ref, ids_ref, grad_ref, q_ref, p_ref, kv_ref, next_ref, out_ref, stat_ref,
               hist_ref, *refs):
    dq_ref = refs[0]
    group_refs = refs[1:5]
    delta_ref, dqt_ref, total_ref, even_ref, odd_ref = refs[5:]
    step = pl.program_id(0)
    split = split_ref[0]
    half, kb, diag = step_args(step, split)

    def grad_probs_step(at, value_blk, gp_ref):
        at_half = (at > split).astype(jnp.int32)
        start = pl.multiple_of(at_half * BLK, BLK)
        for h in range(GROUP):
            gp_ref[h] = dot_nt(
                value_blk, grad_ref[pl.ds(start, BLK), h * HD : (h + 1) * HD]
            )

    @pl.when(step == 0)
    def _():
        total_ref[...] = jnp.zeros_like(total_ref)
        dqt_ref[...] = jnp.zeros_like(dqt_ref)
        grad_probs_step(step, kv_ref[0, :, HD:], even_ref)

    start = pl.multiple_of(half * BLK, BLK)

    @pl.when(kb == 0)
    def _():
        for h in range(GROUP):
            cols = slice(h * BLK, (h + 1) * BLK)
            grad = grad_ref[pl.ds(start, BLK), h * HD : (h + 1) * HD]
            grad_t = jnp.transpose(grad.astype(jnp.float32))
            delta_ref[0:1, cols] = jnp.sum(out_ref[0, :, cols] * grad_t, axis=0, keepdims=True)

    def main_step(now, later):
        grad_probs_step(jnp.minimum(step + 1, STEPS - 1), next_ref[0, :, HD:], later)
        key_t = jnp.transpose(kv_ref[0, :, :HD].astype(jnp.float32)).astype(jnp.bfloat16)
        keep = jnp.where(kb == 0, 0.0, 1.0)
        dk = jnp.zeros((BLK, HD), jnp.float32)
        for h in range(GROUP):
            cols = slice(h * BLK, (h + 1) * BLK)
            probs = p_ref[step, h].astype(jnp.float32) * norm_of(hist_ref, stat_ref, cols)
            dscore = (probs * (now[h] - delta_ref[0:1, cols])).astype(jnp.bfloat16)
            dk = dk + dot_nn(dscore, q_ref[pl.ds(start, BLK), h * HD : (h + 1) * HD])
            dqt_ref[:, cols] = dqt_ref[:, cols] * keep + dot_nn(key_t, dscore)
        total_ref[kb] += dk

    @pl.when(step % 2 == 0)
    def _():
        main_step(even_ref, odd_ref)

    @pl.when(step % 2 == 1)
    def _():
        main_step(odd_ref, even_ref)

    @pl.when(diag == 1)
    def _():
        for h in range(GROUP):
            cols = slice(h * BLK, (h + 1) * BLK)
            dq_ref[:, h * HD : (h + 1) * HD] = jnp.transpose(dqt_ref[:, cols] * SCALE).astype(
                jnp.bfloat16
            )

    @pl.when(step == STEPS - 1)
    def _():
        write_groups(ids_ref, total_ref, group_refs, SCALE)


def key_call(split, ids, grad, saved, queries):
    probs, outs, stats, hist, kv_sorted = saved
    wide = GROUP * BLK
    group_spec = pl.BlockSpec((2, 2 * BLK, HD), lambda i, s, d: (0, 0, 0))
    whole = pl.BlockSpec((2 * BLK, GROUP * HD), lambda i, s, d: (0, 0))

    def next_block(i, s, d):
        return (block_of(jnp.minimum(i + 1, STEPS - 1), s), 0, 0)

    return pl.pallas_call(
        key_kernel,
        grid_spec=pltpu.PrefetchScalarGridSpec(
            num_scalar_prefetch=2,
            grid=(STEPS,),
            in_specs=[
                whole,
                whole,
                VMEM_WHOLE,
                pl.BlockSpec((1, BLK, 2 * HD), lambda i, s, d: (block_of(i, s), 0, 0)),
                pl.BlockSpec((1, BLK, 2 * HD), next_block),
                pl.BlockSpec((1, HD, wide), lambda i, s, d: (half_of(i, s), 0, 0)),
                pl.BlockSpec((1, 8, wide), lambda i, s, d: (half_of(i, s), 0, 0)),
                pl.BlockSpec((1, 1, wide), lambda i, s, d: (i, 0, 0)),
            ],
            out_specs=[pl.BlockSpec((BLK, GROUP * HD), lambda i, s, d: (half_of(i, s), 0))]
            + [group_spec] * 4,
            scratch_shapes=[
                pltpu.VMEM((8, wide), jnp.float32),
                pltpu.VMEM((HD, wide), jnp.float32),
                pltpu.VMEM((16, BLK, HD), jnp.float32),
                pltpu.VMEM((GROUP, BLK, BLK), jnp.float32),
                pltpu.VMEM((GROUP, BLK, BLK), jnp.float32),
            ],
        ),
        out_shape=[jax.ShapeDtypeStruct((2 * BLK, GROUP * HD), jnp.bfloat16)]
        + [jax.ShapeDtypeStruct((2, 2 * BLK, HD), jnp.bfloat16)] * 4,
        compiler_params=PARAMS,
        cost_estimate=pl.CostEstimate(
            flops=2 * 3 * STEPS * wide * BLK * HD, bytes_accessed=14 << 20, transcendentals=0
        ),
    )(split, ids, grad, queries, probs, kv_sorted, kv_sorted, outs, stats, hist)


def per_device(
    stretch_order,
    queries,
    key_rows,
    value_rows,
    out_grad,
    query_weight,
    key_weight,
    value_weight,
    output_weight,
):
    send = lax.ppermute
    tp = lax.axis_index(TP)
    ctx = lax.axis_index(CTX)
    own_x, own_z = ctx // 4, ctx % 4
    bf16 = jnp.bfloat16

    chunk = out_grad[0]
    half_rows = chunk.shape[0] // 2
    top, low = chunk[:half_rows], chunk[half_rows:]
    left_top = send(top, TP, ring(4, 1))
    right_low = send(low, TP, ring(4, -1))
    far_top = send(left_top, TP, ring(4, 1))
    far_low = send(right_low, TP, ring(4, -1))
    left_low = send(low, TP, ring(4, 1))
    right_top = send(top, TP, ring(4, -1))

    kv_own = jnp.concatenate([key_rows[0], value_rows[0]], axis=1)
    kv_pair = send(kv_own, CTX, X_SWAP)
    along, crossed = {}, {}
    for distance, shift in ((2, 2), (1, -1), (3, 1)):
        along[distance] = send(kv_own, CTX, z_ring(shift))
    for distance, shift in ((1, -1), (3, 1)):
        crossed[distance] = send(kv_pair, CTX, z_ring(shift))
    crossed[2] = send(along[2], CTX, X_SWAP)
    kv_chunks = [kv_own, kv_pair]
    for distance in (1, 2, 3):
        kv_chunks += [along[distance], crossed[distance]]

    sent_key_weight = send(key_weight[0], SECTION, ring(4, -1))
    sent_value_weight = send(value_weight[0], SECTION, ring(4, -1))

    index = jnp.arange(8, dtype=jnp.int32)
    source = ((own_x + index % 2) % 2) * 4 + (own_z + index // 2) % 4
    table = jnp.arange(8, dtype=jnp.int32)
    ids = jnp.sum(
        jnp.where(source[:, None, None] == table[None, :, None], stretch_order[None], 0), axis=1
    ).reshape(16)
    split = ids[:1]
    saved = forward_call(split, ids, kv_chunks, queries[0])

    left, right, far = (tp + 3) % 4, (tp + 1) % 4, (tp + 2) % 4
    pieces = (chunk, left_top, left_low, right_top, right_low, far_top, far_low)
    places = (2 * tp, 2 * left, 2 * left + 1, 2 * right, 2 * right + 1, 2 * far, 2 * far + 1)
    grad = grad_call(
        (jnp.stack(places) * half_rows).astype(jnp.int32), pieces, output_weight[0]
    )

    f32 = jnp.float32

    def along_z(groups):
        total = groups[0].astype(f32)
        for distance, shift in ((1, 1), (2, 2), (3, -1)):
            received = send(groups[distance], CTX, z_ring(shift))
            total = total + received.astype(f32)
        return total

    groups, grad = lax.optimization_barrier((value_call(split, ids, grad, saved), grad))
    value_sum = along_z(groups)
    query_grad, *groups = key_call(split, ids, grad, saved, queries[0])
    key_sum = along_z(groups)

    def with_pair(total):
        received = send(total[1].astype(bf16), CTX, X_SWAP)
        return (total[0] + received.astype(f32)).astype(bf16)

    def chunk_of(array, distance):
        return lax.dynamic_slice_in_dim(array, ((tp + distance) % 4) * 128, 128, 0)

    query_terms = []
    for distance in range(4):
        query_terms.append(dot_nt(chunk_of(query_grad, distance), query_weight[0]))
    query_terms[0] = query_terms[0].astype(bf16)
    query_terms = lax.optimization_barrier(tuple(query_terms))
    own = send(query_terms[0], SECTION, ring(4, -1))

    value_grad = with_pair(value_sum)
    key_grad = with_pair(key_sum)

    kv_grad = jnp.concatenate([key_grad, value_grad], axis=1)
    kv_weights = jnp.concatenate([key_weight[0], value_weight[0]], axis=1)

    def term_of(distance):
        rows = chunk_of(kv_grad, distance)
        return (query_terms[distance] + dot_nt(rows, kv_weights)).astype(bf16)

    far = term_of(2)
    from_left = send(far[:half_rows], TP, ring(4, 1))
    from_right = send(far[half_rows:], TP, ring(4, -1))
    right, left = lax.optimization_barrier((term_of(1), term_of(3)))
    joint = (SECTION, TP)
    low_a = send(right[half_rows:], joint, joint_ring(1))
    top_b = send(left[:half_rows], joint, joint_ring(-1))
    rows = send(chunk_of(kv_grad, 0), SECTION, ring(4, -1))
    own = own.astype(f32) + dot_nt(rows[:, :HD], sent_key_weight)
    own = lax.optimization_barrier(own + dot_nt(rows[:, HD:], sent_value_weight))
    top_a = (right[:half_rows].astype(f32) + from_left.astype(f32)).astype(bf16)
    top_a = send(top_a, joint, joint_ring(1))
    low_b = (left[half_rows:].astype(f32) + from_right.astype(f32)).astype(bf16)
    low_b = send(low_b, joint, joint_ring(-1))
    sent = jnp.concatenate(
        [
            own[:half_rows] + top_a.astype(f32) + top_b.astype(f32),
            own[half_rows:] + low_a.astype(f32) + low_b.astype(f32),
        ],
        axis=0,
    ).astype(bf16)
    return (sent[None], key_grad[None], value_grad[None])


def solution(mesh):
    placed = (
        P(),
        P(SECTION, CTX, TP),
        P(SECTION, CTX, TP),
        P(SECTION, CTX, TP),
        P(SECTION, (CTX, TP), None),
        P(SECTION, None, TP),
        P(SECTION, None, TP),
        P(SECTION, None, TP),
        P(SECTION, TP, None),
    )

    return jax.shard_map(
        per_device,
        mesh=mesh,
        in_specs=placed,
        out_specs=(
            P(SECTION, (CTX, TP), None),
            P(SECTION, CTX, TP),
            P(SECTION, CTX, TP),
        ),
        check_vma=False,
    )
```

```python
import jax
import jax.numpy as jnp
from jax import lax
from jax.experimental import pallas as pl
from jax.experimental.pallas import tpu as pltpu
from jax.sharding import PartitionSpec as P

HD = 128
BLK = 256
GROUP = 4
STEPS = 17
SCALE = HD ** (-0.5)
EXP2_SCALE = SCALE * 1.4426950408889634
NEG_LARGE = -1e30

VMEM_WHOLE = pl.BlockSpec(memory_space=pltpu.VMEM)
TP, CTX, SECTION = "tp", "ctx", "section"
PARAMS = pltpu.CompilerParams(vmem_limit_bytes=36 << 20)


def dot_nt(lhs, rhs):
    return lax.dot_general(lhs, rhs, (((1,), (1,)), ((), ())), preferred_element_type=jnp.float32)


def dot_nn(lhs, rhs):
    return lax.dot_general(lhs, rhs, (((1,), (0,)), ((), ())), preferred_element_type=jnp.float32)


def ring(size, shift):
    return [(i, (i + shift) % size) for i in range(size)]


def z_ring(shift):
    return [(x * 4 + z, x * 4 + (z + shift) % 4) for x in range(2) for z in range(4)]


X_SWAP = [(x * 4 + z, (1 - x) * 4 + z) for x in range(2) for z in range(4)]


def joint_ring(shift):
    return [(s * 4 + t, ((s - 1) % 4) * 4 + (t + shift) % 4) for s in range(4) for t in range(4)]


def step_block(step, split):
    half = (step > split).astype(jnp.int32)
    return half, step - half * (split + 1)


def step_args(step, split):
    half, kb = step_block(step, split)
    diag = ((step == split) | (step == STEPS - 1)).astype(jnp.int32)
    return half, kb, diag


def forward_kernel(split_ref, ids_ref, *refs):
    kv_refs = refs[:8]
    (
        q_ref, p_ref, out_ref, stat_ref, hist_ref, kvs_ref,
        max_ref, acc_ref, bias_ref, even_ref, odd_ref, even_top_ref, odd_top_ref,
    ) = refs[8:]
    step = pl.program_id(0)
    split = split_ref[0]
    _, kb, diag = step_args(step, split)

    def score_step(at, score_ref, top_ref):
        at_half, at_kb, at_diag = step_args(at, split)
        start = pl.multiple_of(at_half * BLK, BLK)
        key_blk = kvs_ref[at_kb, :, :HD]
        for h in range(GROUP):
            query = q_ref[pl.ds(start, BLK), h * HD : (h + 1) * HD]
            scores = dot_nt(key_blk, query) + bias_ref[at_diag]
            score_ref[h] = scores
            top_ref[0:1, h * BLK : (h + 1) * BLK] = jnp.max(scores, axis=0, keepdims=True)

    @pl.when(step == 0)
    def _():
        for j in range(8):
            for r in range(2):
                kvs_ref[ids_ref[2 * j + r]] = kv_refs[j][r * BLK : (r + 1) * BLK, :]
        gap = lax.broadcasted_iota(jnp.int32, (BLK, BLK), 0) - lax.broadcasted_iota(
            jnp.int32, (BLK, BLK), 1
        )
        bias_ref[0] = jnp.zeros((BLK, BLK), jnp.float32)
        bias_ref[1] = jnp.where(gap <= 0, 0.0, NEG_LARGE)
        max_ref[...] = jnp.full_like(max_ref, NEG_LARGE)
        acc_ref[...] = jnp.zeros_like(acc_ref)
        score_step(step, even_ref, even_top_ref)

    def softmax_step(now, now_top, later, later_top):
        score_step(jnp.minimum(step + 1, STEPS - 1), later, later_top)
        value_t = jnp.transpose(kvs_ref[kb, :, HD:].astype(jnp.float32)).astype(jnp.bfloat16)
        lhs = jnp.concatenate([value_t, jnp.ones((16, BLK), jnp.bfloat16)], axis=0)
        for h in range(GROUP):
            cols = slice(h * BLK, (h + 1) * BLK)
            old_max = jnp.where(kb == 0, NEG_LARGE, max_ref[0:1, cols])
            new_max = jnp.maximum(old_max, now_top[0:1, cols])
            probs = jnp.exp2((now[h] - new_max) * EXP2_SCALE).astype(jnp.bfloat16)
            p_ref[step, h] = probs
            factor = jnp.exp2((old_max - new_max) * EXP2_SCALE)
            acc_ref[:, cols] = acc_ref[:, cols] * factor + dot_nn(lhs, probs)
            max_ref[0:1, cols] = new_max
            hist_ref[0, 0:1, cols] = new_max

    @pl.when(step % 2 == 0)
    def _():
        softmax_step(even_ref, even_top_ref, odd_ref, odd_top_ref)

    @pl.when(step % 2 == 1)
    def _():
        softmax_step(odd_ref, odd_top_ref, even_ref, even_top_ref)

    @pl.when(diag == 1)
    def _():
        inv = 1.0 / acc_ref[HD : HD + 1, :]
        out_ref[0] = acc_ref[:HD, :] * inv
        stat_ref[0, 0:1, :] = max_ref[0:1, :]
        stat_ref[0, 1:2, :] = inv


def half_of(step, split_ref):
    return (step > split_ref[0]).astype(jnp.int32)


def block_of(step, split_ref):
    return step - half_of(step, split_ref) * (split_ref[0] + 1)


def forward_call(split, ids, kv_chunks, queries):
    whole = pl.BlockSpec((2 * BLK, 2 * HD), lambda i, s, d: (0, 0))
    wide = GROUP * BLK
    return pl.pallas_call(
        forward_kernel,
        grid_spec=pltpu.PrefetchScalarGridSpec(
            num_scalar_prefetch=2,
            grid=(STEPS,),
            in_specs=[whole] * 8 + [pl.BlockSpec((2 * BLK, GROUP * HD), lambda i, s, d: (0, 0))],
            out_specs=[
                VMEM_WHOLE,
                pl.BlockSpec((1, HD, wide), lambda i, s, d: (half_of(i, s), 0, 0)),
                pl.BlockSpec((1, 8, wide), lambda i, s, d: (half_of(i, s), 0, 0)),
                pl.BlockSpec((1, 1, wide), lambda i, s, d: (i, 0, 0)),
                pl.BlockSpec((16, BLK, 2 * HD), lambda i, s, d: (0, 0, 0)),
            ],
            scratch_shapes=[
                pltpu.VMEM((8, wide), jnp.float32),
                pltpu.VMEM((HD + 16, wide), jnp.float32),
                pltpu.VMEM((2, BLK, BLK), jnp.float32),
                pltpu.VMEM((GROUP, BLK, BLK), jnp.float32),
                pltpu.VMEM((GROUP, BLK, BLK), jnp.float32),
                pltpu.VMEM((8, wide), jnp.float32),
                pltpu.VMEM((8, wide), jnp.float32),
            ],
        ),
        out_shape=[
            jax.ShapeDtypeStruct((STEPS, GROUP, BLK, BLK), jnp.bfloat16),
            jax.ShapeDtypeStruct((2, HD, wide), jnp.float32),
            jax.ShapeDtypeStruct((2, 8, wide), jnp.float32),
            jax.ShapeDtypeStruct((STEPS, 1, wide), jnp.float32),
            jax.ShapeDtypeStruct((16, BLK, 2 * HD), jnp.bfloat16),
        ],
        compiler_params=PARAMS,
        cost_estimate=pl.CostEstimate(
            flops=2 * 2 * STEPS * wide * BLK * HD,
            bytes_accessed=13 << 20,
            transcendentals=STEPS * wide * BLK,
        ),
    )(split, ids, *kv_chunks, queries)


def grad_kernel(rows_ref, *refs):
    pieces = refs[:7]
    weight_ref, out_ref, lhs_ref, acc_ref = refs[7:]
    step = pl.program_id(0)
    depth = lhs_ref.shape[1]

    @pl.when(step == 0)
    def _():
        acc_ref[...] = jnp.zeros_like(acc_ref)

    for j, piece in enumerate(pieces):
        size = piece.shape[0]
        lhs_ref[pl.ds(pl.multiple_of(rows_ref[j], 64), size), :] = piece[...]
    start = pl.multiple_of(step * depth, depth)
    acc_ref[...] += dot_nt(lhs_ref[...], weight_ref[:, pl.ds(start, depth)])

    @pl.when(step == pl.num_programs(0) - 1)
    def _():
        out_ref[...] = acc_ref[...].astype(jnp.bfloat16)


def grad_call(rows, pieces, out_weight):
    depth = 1024
    total = out_weight.shape[0]
    return pl.pallas_call(
        grad_kernel,
        grid_spec=pltpu.PrefetchScalarGridSpec(
            num_scalar_prefetch=1,
            grid=(out_weight.shape[1] // depth,),
            in_specs=[pl.BlockSpec((p.shape[0], depth), lambda i, w: (0, i)) for p in pieces]
            + [VMEM_WHOLE],
            out_specs=pl.BlockSpec((2 * BLK, total), lambda i, w: (0, 0)),
            scratch_shapes=[
                pltpu.VMEM((2 * BLK, depth), jnp.bfloat16),
                pltpu.VMEM((2 * BLK, total), jnp.float32),
            ],
        ),
        out_shape=jax.ShapeDtypeStruct((2 * BLK, total), jnp.bfloat16),
        compiler_params=PARAMS,
        cost_estimate=pl.CostEstimate(
            flops=2 * 2 * BLK * total * out_weight.shape[1],
            bytes_accessed=9 << 20,
            transcendentals=0,
        ),
    )(rows, *pieces, out_weight)


def norm_of(hist_ref, stat_ref, cols):
    gap = (hist_ref[0, 0:1, cols] - stat_ref[0, 0:1, cols]) * EXP2_SCALE
    return jnp.exp2(gap) * stat_ref[0, 1:2, cols]


def group_rows(ids_ref, chunk_ref, total_ref, group, x, index):
    chunk = chunk_ref[index]
    block = ids_ref[4 * group + 2 * x + chunk // 2]
    start = pl.multiple_of((chunk % 2) * 128, 128)
    return total_ref[block, pl.ds(start, 128), :]


def value_kernel(split_ref, ids_ref, chunk_ref, grad_ref, p_ref, stat_ref, hist_ref, *refs):
    group_refs = refs[:4]
    total_ref = refs[4]
    step = pl.program_id(0)
    half, kb, _ = step_args(step, split_ref[0])

    @pl.when(step == 0)
    def _():
        total_ref[...] = jnp.zeros_like(total_ref)

    start = pl.multiple_of(half * BLK, BLK)
    dv = jnp.zeros((BLK, HD), jnp.float32)
    for h in range(GROUP):
        norm = norm_of(hist_ref, stat_ref, slice(h * BLK, (h + 1) * BLK))
        probs = (p_ref[step, h].astype(jnp.float32) * norm).astype(jnp.bfloat16)
        dv = dv + dot_nn(probs, grad_ref[pl.ds(start, BLK), h * HD : (h + 1) * HD])
    total_ref[kb] += dv

    @pl.when(step == STEPS - 1)
    def _():
        for g, g_ref in enumerate(group_refs):
            for x in range(2):
                for j in range(4):
                    rows = group_rows(ids_ref, chunk_ref, total_ref, g, x, j)
                    g_ref[x, j * 128 : (j + 1) * 128, :] = rows.astype(jnp.bfloat16)


def value_call(split, ids, chunks, grad, saved):
    probs, _, stats, hist, _ = saved
    wide = GROUP * BLK
    group_spec = pl.BlockSpec((2, 2 * BLK, HD), lambda i, s, d, c: (0, 0, 0))
    return pl.pallas_call(
        value_kernel,
        grid_spec=pltpu.PrefetchScalarGridSpec(
            num_scalar_prefetch=3,
            grid=(STEPS,),
            in_specs=[
                pl.BlockSpec((2 * BLK, GROUP * HD), lambda i, s, d, c: (0, 0)),
                VMEM_WHOLE,
                pl.BlockSpec((1, 8, wide), lambda i, s, d, c: (half_of(i, s), 0, 0)),
                pl.BlockSpec((1, 1, wide), lambda i, s, d, c: (i, 0, 0)),
            ],
            out_specs=[group_spec] * 4,
            scratch_shapes=[pltpu.VMEM((16, BLK, HD), jnp.float32)],
        ),
        out_shape=[jax.ShapeDtypeStruct((2, 2 * BLK, HD), jnp.bfloat16)] * 4,
        compiler_params=PARAMS,
        cost_estimate=pl.CostEstimate(
            flops=2 * STEPS * wide * BLK * HD, bytes_accessed=11 << 20, transcendentals=0
        ),
        name="attn_value_grad",
    )(split, ids, chunks, grad, probs, stats, hist)


def key_kernel(split_ref, ids_ref, chunk_ref, grad_ref, q_ref, p_ref, kv_ref, next_ref, out_ref, stat_ref,
               hist_ref, *refs):
    dq_ref = refs[0]
    far_refs, rest_refs = refs[1:5], refs[5:9]
    delta_ref, dqt_ref, total_ref, even_ref, odd_ref = refs[9:]
    step = pl.program_id(0)
    split = split_ref[0]
    half, kb, diag = step_args(step, split)

    def grad_probs_step(at, value_blk, gp_ref):
        at_half = (at > split).astype(jnp.int32)
        start = pl.multiple_of(at_half * BLK, BLK)
        for h in range(GROUP):
            gp_ref[h] = dot_nt(
                value_blk, grad_ref[pl.ds(start, BLK), h * HD : (h + 1) * HD]
            )

    @pl.when(step == 0)
    def _():
        total_ref[...] = jnp.zeros_like(total_ref)
        dqt_ref[...] = jnp.zeros_like(dqt_ref)
        grad_probs_step(step, kv_ref[0, :, HD:], even_ref)

    start = pl.multiple_of(half * BLK, BLK)

    @pl.when(kb == 0)
    def _():
        for h in range(GROUP):
            cols = slice(h * BLK, (h + 1) * BLK)
            grad = grad_ref[pl.ds(start, BLK), h * HD : (h + 1) * HD]
            grad_t = jnp.transpose(grad.astype(jnp.float32))
            delta_ref[0:1, cols] = jnp.sum(out_ref[0, :, cols] * grad_t, axis=0, keepdims=True)

    def main_step(now, later):
        grad_probs_step(jnp.minimum(step + 1, STEPS - 1), next_ref[0, :, HD:], later)
        key_t = jnp.transpose(kv_ref[0, :, :HD].astype(jnp.float32)).astype(jnp.bfloat16)
        keep = jnp.where(kb == 0, 0.0, 1.0)
        dk = jnp.zeros((BLK, HD), jnp.float32)
        for h in range(GROUP):
            cols = slice(h * BLK, (h + 1) * BLK)
            probs = p_ref[step, h].astype(jnp.float32) * norm_of(hist_ref, stat_ref, cols)
            dscore = (probs * (now[h] - delta_ref[0:1, cols])).astype(jnp.bfloat16)
            dk = dk + dot_nn(dscore, q_ref[pl.ds(start, BLK), h * HD : (h + 1) * HD])
            dqt_ref[:, cols] = dqt_ref[:, cols] * keep + dot_nn(key_t, dscore)
        total_ref[kb] += dk

    @pl.when(step % 2 == 0)
    def _():
        main_step(even_ref, odd_ref)

    @pl.when(step % 2 == 1)
    def _():
        main_step(odd_ref, even_ref)

    @pl.when(diag == 1)
    def _():
        for h in range(GROUP):
            cols = slice(h * BLK, (h + 1) * BLK)
            dq_ref[:, h * HD : (h + 1) * HD] = jnp.transpose(dqt_ref[:, cols] * SCALE).astype(
                jnp.bfloat16
            )

    @pl.when(step == STEPS - 1)
    def _():
        for g in range(4):
            for x in range(2):
                for j in range(4):
                    rows = group_rows(ids_ref, chunk_ref, total_ref, g, x, j)
                    rows = (rows * SCALE).astype(jnp.bfloat16)
                    if j == 0:
                        far_refs[g][x] = rows
                    else:
                        rest_refs[g][x, (j - 1) * 128 : j * 128, :] = rows


def key_call(split, ids, chunks, grad, saved, queries):
    probs, outs, stats, hist, kv_sorted = saved
    wide = GROUP * BLK
    shapes = [(2, 128, HD)] * 4 + [(2, 2 * BLK - 128, HD)] * 4
    whole = pl.BlockSpec((2 * BLK, GROUP * HD), lambda i, s, d, c: (0, 0))

    def next_block(i, s, d, c):
        return (block_of(jnp.minimum(i + 1, STEPS - 1), s), 0, 0)

    return pl.pallas_call(
        key_kernel,
        grid_spec=pltpu.PrefetchScalarGridSpec(
            num_scalar_prefetch=3,
            grid=(STEPS,),
            in_specs=[
                whole,
                whole,
                VMEM_WHOLE,
                pl.BlockSpec((1, BLK, 2 * HD), lambda i, s, d, c: (block_of(i, s), 0, 0)),
                pl.BlockSpec((1, BLK, 2 * HD), next_block),
                pl.BlockSpec((1, HD, wide), lambda i, s, d, c: (half_of(i, s), 0, 0)),
                pl.BlockSpec((1, 8, wide), lambda i, s, d, c: (half_of(i, s), 0, 0)),
                pl.BlockSpec((1, 1, wide), lambda i, s, d, c: (i, 0, 0)),
            ],
            out_specs=[pl.BlockSpec((BLK, GROUP * HD), lambda i, s, d, c: (half_of(i, s), 0))]
            + [pl.BlockSpec(shape, lambda i, s, d, c: (0, 0, 0)) for shape in shapes],
            scratch_shapes=[
                pltpu.VMEM((8, wide), jnp.float32),
                pltpu.VMEM((HD, wide), jnp.float32),
                pltpu.VMEM((16, BLK, HD), jnp.float32),
                pltpu.VMEM((GROUP, BLK, BLK), jnp.float32),
                pltpu.VMEM((GROUP, BLK, BLK), jnp.float32),
            ],
        ),
        out_shape=[jax.ShapeDtypeStruct((2 * BLK, GROUP * HD), jnp.bfloat16)]
        + [jax.ShapeDtypeStruct(shape, jnp.bfloat16) for shape in shapes],
        compiler_params=PARAMS,
        cost_estimate=pl.CostEstimate(
            flops=2 * 3 * STEPS * wide * BLK * HD, bytes_accessed=14 << 20, transcendentals=0
        ),
    )(split, ids, chunks, grad, queries, probs, kv_sorted, kv_sorted, outs, stats, hist)


def per_device(
    stretch_order,
    queries,
    key_rows,
    value_rows,
    out_grad,
    query_weight,
    key_weight,
    value_weight,
    output_weight,
):
    send = lax.ppermute
    tp = lax.axis_index(TP)
    ctx = lax.axis_index(CTX)
    own_x, own_z = ctx // 4, ctx % 4
    bf16 = jnp.bfloat16

    chunk = out_grad[0]
    half_rows = chunk.shape[0] // 2
    top, low = chunk[:half_rows], chunk[half_rows:]
    left_top = send(top, TP, ring(4, 1))
    right_low = send(low, TP, ring(4, -1))
    far_top = send(left_top, TP, ring(4, 1))
    far_low = send(right_low, TP, ring(4, -1))
    left_low = send(low, TP, ring(4, 1))
    right_top = send(top, TP, ring(4, -1))

    kv_own = jnp.concatenate([key_rows[0], value_rows[0]], axis=1)
    kv_pair = send(kv_own, CTX, X_SWAP)
    along, crossed = {}, {}
    for distance, shift in ((2, 2), (1, -1), (3, 1)):
        along[distance] = send(kv_own, CTX, z_ring(shift))
    for distance, shift in ((1, -1), (3, 1)):
        crossed[distance] = send(kv_pair, CTX, z_ring(shift))
    crossed[2] = send(along[2], CTX, X_SWAP)
    kv_chunks = [kv_own, kv_pair]
    for distance in (1, 2, 3):
        kv_chunks += [along[distance], crossed[distance]]

    kv_weights = jnp.concatenate([key_weight[0], value_weight[0]], axis=1)
    kv_weights = lax.optimization_barrier(kv_weights)
    sent_weights = send(kv_weights, SECTION, ring(4, -1))

    index = jnp.arange(8, dtype=jnp.int32)
    source = ((own_x + index % 2) % 2) * 4 + (own_z + index // 2) % 4
    table = jnp.arange(8, dtype=jnp.int32)
    ids = jnp.sum(
        jnp.where(source[:, None, None] == table[None, :, None], stretch_order[None], 0), axis=1
    ).reshape(16)
    split = ids[:1]
    saved = forward_call(split, ids, kv_chunks, queries[0])

    left, right, far = (tp + 3) % 4, (tp + 1) % 4, (tp + 2) % 4
    pieces = (chunk, left_top, left_low, right_top, right_low, far_top, far_low)
    places = (2 * tp, 2 * left, 2 * left + 1, 2 * right, 2 * right + 1, 2 * far, 2 * far + 1)
    grad = grad_call(
        (jnp.stack(places) * half_rows).astype(jnp.int32), pieces, output_weight[0]
    )

    f32 = jnp.float32

    def along_z(groups):
        total = groups[0].astype(f32)
        for distance, shift in ((1, 1), (2, 2), (3, -1)):
            received = send(groups[distance], CTX, z_ring(shift))
            total = total + received.astype(f32)
        return total

    chunks = jnp.stack([far, left, tp, right]).astype(jnp.int32)
    groups, grad = lax.optimization_barrier((value_call(split, ids, chunks, grad, saved), grad))
    value_sum = along_z(groups)
    query_grad, *groups = key_call(split, ids, chunks, grad, saved, queries[0])
    *near_weights, query_grad = lax.optimization_barrier(
        (key_weight[0], value_weight[0], query_grad)
    )
    near_weights = jnp.concatenate(near_weights, axis=1)
    key_far_sum = along_z(groups[:4])
    key_rest_sum = along_z(groups[4:])

    def with_pair(total):
        received = send(total[1].astype(bf16), CTX, X_SWAP)
        return (total[0] + received.astype(f32)).astype(bf16)

    def chunk_of(array, distance):
        return lax.dynamic_slice_in_dim(array, ((tp + distance) % 4) * 128, 128, 0)

    query_terms = []
    for distance in range(4):
        query_terms.append(dot_nt(chunk_of(query_grad, distance), query_weight[0]))
    query_terms[0] = query_terms[0].astype(bf16)
    query_terms = [lax.optimization_barrier(term) for term in query_terms]
    own = send(query_terms[0], SECTION, ring(4, -1))

    value_grad = with_pair(value_sum)
    key_far = with_pair(key_far_sum)
    key_rest = with_pair(key_rest_sum)

    def rows_of(distance):
        j = (distance + 2) % 4
        key_rows = key_far if j == 0 else key_rest[(j - 1) * 128 : j * 128]
        return jnp.concatenate([key_rows, value_grad[j * 128 : (j + 1) * 128]], axis=1)

    def in_order(array):
        return lax.dynamic_slice_in_dim(
            jnp.concatenate([array, array], axis=0), ((2 - tp) % 4) * 128, array.shape[0], 0
        )

    def term_of(distance):
        return (query_terms[distance] + dot_nt(rows_of(distance), near_weights)).astype(bf16)

    far = term_of(2)
    from_left = send(far[:half_rows], TP, ring(4, 1))
    from_right = send(far[half_rows:], TP, ring(4, -1))
    right, left = lax.optimization_barrier((term_of(1), term_of(3)))
    joint = (SECTION, TP)
    low_a = send(right[half_rows:], joint, joint_ring(1))
    top_b = send(left[:half_rows], joint, joint_ring(-1))
    rows = send(rows_of(0), SECTION, ring(4, -1))
    own = lax.optimization_barrier(own.astype(f32) + dot_nt(rows, sent_weights))
    top_a = (right[:half_rows].astype(f32) + from_left.astype(f32)).astype(bf16)
    top_a = send(top_a, joint, joint_ring(1))
    low_b = (left[half_rows:].astype(f32) + from_right.astype(f32)).astype(bf16)
    low_b = send(low_b, joint, joint_ring(-1))
    sent = jnp.concatenate(
        [
            own[:half_rows] + top_a.astype(f32) + top_b.astype(f32),
            own[half_rows:] + low_a.astype(f32) + low_b.astype(f32),
        ],
        axis=0,
    ).astype(bf16)
    key_grad = in_order(jnp.concatenate([key_far, key_rest], axis=0))
    return (sent[None], key_grad[None], in_order(value_grad)[None])


def solution(mesh):
    placed = (
        P(),
        P(SECTION, CTX, TP),
        P(SECTION, CTX, TP),
        P(SECTION, CTX, TP),
        P(SECTION, (CTX, TP), None),
        P(SECTION, None, TP),
        P(SECTION, None, TP),
        P(SECTION, None, TP),
        P(SECTION, TP, None),
    )

    return jax.shard_map(
        per_device,
        mesh=mesh,
        in_specs=placed,
        out_specs=(
            P(SECTION, (CTX, TP), None),
            P(SECTION, CTX, TP),
            P(SECTION, CTX, TP),
        ),
        check_vma=False,
    )
```

```python
import jax
import jax.numpy as jnp
from jax import lax
from jax.experimental import pallas as pl
from jax.experimental.pallas import tpu as pltpu
from jax.sharding import PartitionSpec as P

HD = 128
BLK = 256
GROUP = 4
STEPS = 17
SCALE = HD ** (-0.5)
EXP2_SCALE = SCALE * 1.4426950408889634
NEG_LARGE = -1e30

VMEM_WHOLE = pl.BlockSpec(memory_space=pltpu.VMEM)
TP, CTX, SECTION = "tp", "ctx", "section"
PARAMS = pltpu.CompilerParams(vmem_limit_bytes=36 << 20)


def dot_nt(lhs, rhs):
    return lax.dot_general(lhs, rhs, (((1,), (1,)), ((), ())), preferred_element_type=jnp.float32)


def dot_nn(lhs, rhs):
    return lax.dot_general(lhs, rhs, (((1,), (0,)), ((), ())), preferred_element_type=jnp.float32)


def ring(size, shift):
    return [(i, (i + shift) % size) for i in range(size)]


def z_ring(shift):
    return [(x * 4 + z, x * 4 + (z + shift) % 4) for x in range(2) for z in range(4)]


X_SWAP = [(x * 4 + z, (1 - x) * 4 + z) for x in range(2) for z in range(4)]


def joint_ring(shift):
    return [(s * 4 + t, ((s - 1) % 4) * 4 + (t + shift) % 4) for s in range(4) for t in range(4)]


def step_block(step, split):
    half = (step > split).astype(jnp.int32)
    return half, step - half * (split + 1)


def step_args(step, split):
    half, kb = step_block(step, split)
    diag = ((step == split) | (step == STEPS - 1)).astype(jnp.int32)
    return half, kb, diag


def forward_kernel(split_ref, ids_ref, *refs):
    kv_refs = refs[:8]
    (
        q_ref, p_ref, out_ref, stat_ref, hist_ref, kvs_ref,
        max_ref, acc_ref, bias_ref, even_ref, odd_ref, even_top_ref, odd_top_ref,
    ) = refs[8:]
    step = pl.program_id(0)
    split = split_ref[0]
    _, kb, diag = step_args(step, split)

    def score_step(at, score_ref, top_ref):
        at_half, at_kb, at_diag = step_args(at, split)
        start = pl.multiple_of(at_half * BLK, BLK)
        key_blk = kvs_ref[at_kb, :, :HD]
        for h in range(GROUP):
            query = q_ref[pl.ds(start, BLK), h * HD : (h + 1) * HD]
            scores = dot_nt(key_blk, query) + bias_ref[at_diag]
            score_ref[h] = scores
            top_ref[0:1, h * BLK : (h + 1) * BLK] = jnp.max(scores, axis=0, keepdims=True)

    @pl.when(step == 0)
    def _():
        for j in range(8):
            for r in range(2):
                kvs_ref[ids_ref[2 * j + r]] = kv_refs[j][r * BLK : (r + 1) * BLK, :]
        gap = lax.broadcasted_iota(jnp.int32, (BLK, BLK), 0) - lax.broadcasted_iota(
            jnp.int32, (BLK, BLK), 1
        )
        bias_ref[0] = jnp.zeros((BLK, BLK), jnp.float32)
        bias_ref[1] = jnp.where(gap <= 0, 0.0, NEG_LARGE)
        max_ref[...] = jnp.full_like(max_ref, NEG_LARGE)
        acc_ref[...] = jnp.zeros_like(acc_ref)
        score_step(step, even_ref, even_top_ref)

    def softmax_step(now, now_top, later, later_top):
        score_step(jnp.minimum(step + 1, STEPS - 1), later, later_top)
        value_t = jnp.transpose(kvs_ref[kb, :, HD:].astype(jnp.float32)).astype(jnp.bfloat16)
        lhs = jnp.concatenate([value_t, jnp.ones((16, BLK), jnp.bfloat16)], axis=0)
        for h in range(GROUP):
            cols = slice(h * BLK, (h + 1) * BLK)
            old_max = jnp.where(kb == 0, NEG_LARGE, max_ref[0:1, cols])
            new_max = jnp.maximum(old_max, now_top[0:1, cols])
            probs = jnp.exp2((now[h] - new_max) * EXP2_SCALE).astype(jnp.bfloat16)
            p_ref[step, h] = probs
            factor = jnp.exp2((old_max - new_max) * EXP2_SCALE)
            acc_ref[:, cols] = acc_ref[:, cols] * factor + dot_nn(lhs, probs)
            max_ref[0:1, cols] = new_max
            hist_ref[0, 0:1, cols] = new_max

    @pl.when(step % 2 == 0)
    def _():
        softmax_step(even_ref, even_top_ref, odd_ref, odd_top_ref)

    @pl.when(step % 2 == 1)
    def _():
        softmax_step(odd_ref, odd_top_ref, even_ref, even_top_ref)

    @pl.when(diag == 1)
    def _():
        inv = 1.0 / acc_ref[HD : HD + 1, :]
        out_ref[0] = acc_ref[:HD, :] * inv
        stat_ref[0, 0:1, :] = max_ref[0:1, :]
        stat_ref[0, 1:2, :] = inv


def half_of(step, split_ref):
    return (step > split_ref[0]).astype(jnp.int32)


def block_of(step, split_ref):
    return step - half_of(step, split_ref) * (split_ref[0] + 1)


def forward_call(split, ids, kv_chunks, queries):
    whole = pl.BlockSpec((2 * BLK, 2 * HD), lambda i, s, d: (0, 0))
    wide = GROUP * BLK
    return pl.pallas_call(
        forward_kernel,
        grid_spec=pltpu.PrefetchScalarGridSpec(
            num_scalar_prefetch=2,
            grid=(STEPS,),
            in_specs=[whole] * 8 + [pl.BlockSpec((2 * BLK, GROUP * HD), lambda i, s, d: (0, 0))],
            out_specs=[
                VMEM_WHOLE,
                pl.BlockSpec((1, HD, wide), lambda i, s, d: (half_of(i, s), 0, 0)),
                pl.BlockSpec((1, 8, wide), lambda i, s, d: (half_of(i, s), 0, 0)),
                pl.BlockSpec((1, 1, wide), lambda i, s, d: (i, 0, 0)),
                pl.BlockSpec((16, BLK, 2 * HD), lambda i, s, d: (0, 0, 0)),
            ],
            scratch_shapes=[
                pltpu.VMEM((8, wide), jnp.float32),
                pltpu.VMEM((HD + 16, wide), jnp.float32),
                pltpu.VMEM((2, BLK, BLK), jnp.float32),
                pltpu.VMEM((GROUP, BLK, BLK), jnp.float32),
                pltpu.VMEM((GROUP, BLK, BLK), jnp.float32),
                pltpu.VMEM((8, wide), jnp.float32),
                pltpu.VMEM((8, wide), jnp.float32),
            ],
        ),
        out_shape=[
            jax.ShapeDtypeStruct((STEPS, GROUP, BLK, BLK), jnp.bfloat16),
            jax.ShapeDtypeStruct((2, HD, wide), jnp.float32),
            jax.ShapeDtypeStruct((2, 8, wide), jnp.float32),
            jax.ShapeDtypeStruct((STEPS, 1, wide), jnp.float32),
            jax.ShapeDtypeStruct((16, BLK, 2 * HD), jnp.bfloat16),
        ],
        compiler_params=PARAMS,
        cost_estimate=pl.CostEstimate(
            flops=2 * 2 * STEPS * wide * BLK * HD,
            bytes_accessed=13 << 20,
            transcendentals=STEPS * wide * BLK,
        ),
    )(split, ids, *kv_chunks, queries)


def grad_kernel(rows_ref, *refs):
    pieces = refs[:7]
    weight_ref, out_ref, lhs_ref, acc_ref = refs[7:]
    step = pl.program_id(0)
    depth = lhs_ref.shape[1]

    @pl.when(step == 0)
    def _():
        acc_ref[...] = jnp.zeros_like(acc_ref)

    for j, piece in enumerate(pieces):
        size = piece.shape[0]
        lhs_ref[pl.ds(pl.multiple_of(rows_ref[j], 64), size), :] = piece[...]
    start = pl.multiple_of(step * depth, depth)
    acc_ref[...] += dot_nt(lhs_ref[...], weight_ref[:, pl.ds(start, depth)])

    @pl.when(step == pl.num_programs(0) - 1)
    def _():
        out_ref[...] = acc_ref[...].astype(jnp.bfloat16)


def grad_call(rows, pieces, out_weight):
    depth = 2048
    total = out_weight.shape[0]
    return pl.pallas_call(
        grad_kernel,
        grid_spec=pltpu.PrefetchScalarGridSpec(
            num_scalar_prefetch=1,
            grid=(out_weight.shape[1] // depth,),
            in_specs=[pl.BlockSpec((p.shape[0], depth), lambda i, w: (0, i)) for p in pieces]
            + [VMEM_WHOLE],
            out_specs=pl.BlockSpec((2 * BLK, total), lambda i, w: (0, 0)),
            scratch_shapes=[
                pltpu.VMEM((2 * BLK, depth), jnp.bfloat16),
                pltpu.VMEM((2 * BLK, total), jnp.float32),
            ],
        ),
        out_shape=jax.ShapeDtypeStruct((2 * BLK, total), jnp.bfloat16),
        compiler_params=PARAMS,
        cost_estimate=pl.CostEstimate(
            flops=2 * 2 * BLK * total * out_weight.shape[1],
            bytes_accessed=9 << 20,
            transcendentals=0,
        ),
    )(rows, *pieces, out_weight)


def norm_of(hist_ref, stat_ref, cols):
    gap = (hist_ref[0, 0:1, cols] - stat_ref[0, 0:1, cols]) * EXP2_SCALE
    return jnp.exp2(gap) * stat_ref[0, 1:2, cols]


def group_rows(ids_ref, chunk_ref, total_ref, group, x, index):
    chunk = chunk_ref[index]
    block = ids_ref[4 * group + 2 * x + chunk // 2]
    start = pl.multiple_of((chunk % 2) * 128, 128)
    return total_ref[block, pl.ds(start, 128), :]


def value_kernel(split_ref, ids_ref, chunk_ref, grad_ref, p_ref, stat_ref, hist_ref, *refs):
    group_refs = refs[:4]
    total_ref = refs[4]
    step = pl.program_id(0)
    half, kb, _ = step_args(step, split_ref[0])

    @pl.when(step == 0)
    def _():
        total_ref[...] = jnp.zeros_like(total_ref)

    start = pl.multiple_of(half * BLK, BLK)
    dv = jnp.zeros((BLK, HD), jnp.float32)
    for h in range(GROUP):
        norm = norm_of(hist_ref, stat_ref, slice(h * BLK, (h + 1) * BLK))
        probs = (p_ref[step, h].astype(jnp.float32) * norm).astype(jnp.bfloat16)
        dv = dv + dot_nn(probs, grad_ref[pl.ds(start, BLK), h * HD : (h + 1) * HD])
    total_ref[kb] += dv

    @pl.when(step == STEPS - 1)
    def _():
        for g, g_ref in enumerate(group_refs):
            for x in range(2):
                for j in range(4):
                    rows = group_rows(ids_ref, chunk_ref, total_ref, g, x, j)
                    g_ref[x, j * 128 : (j + 1) * 128, :] = rows.astype(jnp.bfloat16)


def value_call(split, ids, chunks, grad, saved):
    probs, _, stats, hist, _ = saved
    wide = GROUP * BLK
    group_spec = pl.BlockSpec((2, 2 * BLK, HD), lambda i, s, d, c: (0, 0, 0))
    return pl.pallas_call(
        value_kernel,
        grid_spec=pltpu.PrefetchScalarGridSpec(
            num_scalar_prefetch=3,
            grid=(STEPS,),
            in_specs=[
                pl.BlockSpec((2 * BLK, GROUP * HD), lambda i, s, d, c: (0, 0)),
                VMEM_WHOLE,
                pl.BlockSpec((1, 8, wide), lambda i, s, d, c: (half_of(i, s), 0, 0)),
                pl.BlockSpec((1, 1, wide), lambda i, s, d, c: (i, 0, 0)),
            ],
            out_specs=[group_spec] * 4,
            scratch_shapes=[pltpu.VMEM((16, BLK, HD), jnp.float32)],
        ),
        out_shape=[jax.ShapeDtypeStruct((2, 2 * BLK, HD), jnp.bfloat16)] * 4,
        compiler_params=PARAMS,
        cost_estimate=pl.CostEstimate(
            flops=2 * STEPS * wide * BLK * HD, bytes_accessed=11 << 20, transcendentals=0
        ),
        name="attn_value_grad",
    )(split, ids, chunks, grad, probs, stats, hist)


def key_kernel(split_ref, ids_ref, chunk_ref, grad_ref, q_ref, p_ref, kv_ref, next_ref, out_ref, stat_ref,
               hist_ref, *refs):
    dq_ref = refs[0]
    far_refs, rest_refs = refs[1:5], refs[5:9]
    delta_ref, dqt_ref, total_ref, even_ref, odd_ref = refs[9:]
    step = pl.program_id(0)
    split = split_ref[0]
    half, kb, diag = step_args(step, split)

    def grad_probs_step(at, value_blk, gp_ref):
        at_half = (at > split).astype(jnp.int32)
        start = pl.multiple_of(at_half * BLK, BLK)
        for h in range(GROUP):
            gp_ref[h] = dot_nt(
                value_blk, grad_ref[pl.ds(start, BLK), h * HD : (h + 1) * HD]
            )

    @pl.when(step == 0)
    def _():
        total_ref[...] = jnp.zeros_like(total_ref)
        dqt_ref[...] = jnp.zeros_like(dqt_ref)
        grad_probs_step(step, kv_ref[0, :, HD:], even_ref)

    start = pl.multiple_of(half * BLK, BLK)

    @pl.when(kb == 0)
    def _():
        for h in range(GROUP):
            cols = slice(h * BLK, (h + 1) * BLK)
            grad = grad_ref[pl.ds(start, BLK), h * HD : (h + 1) * HD]
            grad_t = jnp.transpose(grad.astype(jnp.float32))
            delta_ref[0:1, cols] = jnp.sum(out_ref[0, :, cols] * grad_t, axis=0, keepdims=True)

    def main_step(now, later):
        grad_probs_step(jnp.minimum(step + 1, STEPS - 1), next_ref[0, :, HD:], later)
        key_t = jnp.transpose(kv_ref[0, :, :HD].astype(jnp.float32)).astype(jnp.bfloat16)
        keep = jnp.where(kb == 0, 0.0, 1.0)
        dk = jnp.zeros((BLK, HD), jnp.float32)
        for h in range(GROUP):
            cols = slice(h * BLK, (h + 1) * BLK)
            probs = p_ref[step, h].astype(jnp.float32) * norm_of(hist_ref, stat_ref, cols)
            dscore = (probs * (now[h] - delta_ref[0:1, cols])).astype(jnp.bfloat16)
            dk = dk + dot_nn(dscore, q_ref[pl.ds(start, BLK), h * HD : (h + 1) * HD])
            dqt_ref[:, cols] = dqt_ref[:, cols] * keep + dot_nn(key_t, dscore)
        total_ref[kb] += dk

    @pl.when(step % 2 == 0)
    def _():
        main_step(even_ref, odd_ref)

    @pl.when(step % 2 == 1)
    def _():
        main_step(odd_ref, even_ref)

    @pl.when(diag == 1)
    def _():
        for h in range(GROUP):
            cols = slice(h * BLK, (h + 1) * BLK)
            dq_ref[:, h * HD : (h + 1) * HD] = jnp.transpose(dqt_ref[:, cols] * SCALE).astype(
                jnp.bfloat16
            )

    @pl.when(step == STEPS - 1)
    def _():
        for g in range(4):
            for x in range(2):
                for j in range(4):
                    rows = group_rows(ids_ref, chunk_ref, total_ref, g, x, j)
                    rows = (rows * SCALE).astype(jnp.bfloat16)
                    if j == 0:
                        far_refs[g][x] = rows
                    else:
                        rest_refs[g][x, (j - 1) * 128 : j * 128, :] = rows


def key_call(split, ids, chunks, grad, saved, queries):
    probs, outs, stats, hist, kv_sorted = saved
    wide = GROUP * BLK
    shapes = [(2, 128, HD)] * 4 + [(2, 2 * BLK - 128, HD)] * 4
    whole = pl.BlockSpec((2 * BLK, GROUP * HD), lambda i, s, d, c: (0, 0))

    def next_block(i, s, d, c):
        return (block_of(jnp.minimum(i + 1, STEPS - 1), s), 0, 0)

    return pl.pallas_call(
        key_kernel,
        grid_spec=pltpu.PrefetchScalarGridSpec(
            num_scalar_prefetch=3,
            grid=(STEPS,),
            in_specs=[
                whole,
                whole,
                VMEM_WHOLE,
                pl.BlockSpec((1, BLK, 2 * HD), lambda i, s, d, c: (block_of(i, s), 0, 0)),
                pl.BlockSpec((1, BLK, 2 * HD), next_block),
                pl.BlockSpec((1, HD, wide), lambda i, s, d, c: (half_of(i, s), 0, 0)),
                pl.BlockSpec((1, 8, wide), lambda i, s, d, c: (half_of(i, s), 0, 0)),
                pl.BlockSpec((1, 1, wide), lambda i, s, d, c: (i, 0, 0)),
            ],
            out_specs=[pl.BlockSpec((BLK, GROUP * HD), lambda i, s, d, c: (half_of(i, s), 0))]
            + [pl.BlockSpec(shape, lambda i, s, d, c: (0, 0, 0)) for shape in shapes],
            scratch_shapes=[
                pltpu.VMEM((8, wide), jnp.float32),
                pltpu.VMEM((HD, wide), jnp.float32),
                pltpu.VMEM((16, BLK, HD), jnp.float32),
                pltpu.VMEM((GROUP, BLK, BLK), jnp.float32),
                pltpu.VMEM((GROUP, BLK, BLK), jnp.float32),
            ],
        ),
        out_shape=[jax.ShapeDtypeStruct((2 * BLK, GROUP * HD), jnp.bfloat16)]
        + [jax.ShapeDtypeStruct(shape, jnp.bfloat16) for shape in shapes],
        compiler_params=PARAMS,
        cost_estimate=pl.CostEstimate(
            flops=2 * 3 * STEPS * wide * BLK * HD, bytes_accessed=14 << 20, transcendentals=0
        ),
    )(split, ids, chunks, grad, queries, probs, kv_sorted, kv_sorted, outs, stats, hist)


def per_device(
    stretch_order,
    queries,
    key_rows,
    value_rows,
    out_grad,
    query_weight,
    key_weight,
    value_weight,
    output_weight,
):
    send = lax.ppermute
    tp = lax.axis_index(TP)
    ctx = lax.axis_index(CTX)
    own_x, own_z = ctx // 4, ctx % 4
    bf16 = jnp.bfloat16

    chunk = out_grad[0]
    half_rows = chunk.shape[0] // 2
    top, low = chunk[:half_rows], chunk[half_rows:]
    left_top = send(top, TP, ring(4, 1))
    right_low = send(low, TP, ring(4, -1))
    far_top = send(left_top, TP, ring(4, 1))
    far_low = send(right_low, TP, ring(4, -1))
    left_low = send(low, TP, ring(4, 1))
    right_top = send(top, TP, ring(4, -1))

    kv_own = jnp.concatenate([key_rows[0], value_rows[0]], axis=1)
    kv_pair = send(kv_own, CTX, X_SWAP)
    along, crossed = {}, {}
    for distance, shift in ((2, 2), (1, -1), (3, 1)):
        along[distance] = send(kv_own, CTX, z_ring(shift))
    for distance, shift in ((1, -1), (3, 1)):
        crossed[distance] = send(kv_pair, CTX, z_ring(shift))
    crossed[2] = send(along[2], CTX, X_SWAP)
    kv_chunks = [kv_own, kv_pair]
    for distance in (1, 2, 3):
        kv_chunks += [along[distance], crossed[distance]]

    kv_weights = jnp.concatenate([key_weight[0], value_weight[0]], axis=1)
    kv_weights = lax.optimization_barrier(kv_weights)
    sent_weights = send(kv_weights, SECTION, ring(4, -1))

    index = jnp.arange(8, dtype=jnp.int32)
    source = ((own_x + index % 2) % 2) * 4 + (own_z + index // 2) % 4
    table = jnp.arange(8, dtype=jnp.int32)
    ids = jnp.sum(
        jnp.where(source[:, None, None] == table[None, :, None], stretch_order[None], 0), axis=1
    ).reshape(16)
    split = ids[:1]
    saved = forward_call(split, ids, kv_chunks, queries[0])

    left, right, far = (tp + 3) % 4, (tp + 1) % 4, (tp + 2) % 4
    pieces = (chunk, left_top, left_low, right_top, right_low, far_top, far_low)
    places = (2 * tp, 2 * left, 2 * left + 1, 2 * right, 2 * right + 1, 2 * far, 2 * far + 1)
    grad = grad_call(
        (jnp.stack(places) * half_rows).astype(jnp.int32), pieces, output_weight[0]
    )

    f32 = jnp.float32

    def along_z(groups):
        total = groups[0].astype(f32)
        for distance, shift in ((1, 1), (2, 2), (3, -1)):
            received = send(groups[distance], CTX, z_ring(shift))
            total = total + received.astype(f32)
        return total

    chunks = jnp.stack([far, left, tp, right]).astype(jnp.int32)
    groups, grad = lax.optimization_barrier((value_call(split, ids, chunks, grad, saved), grad))
    value_sum = along_z(groups)
    query_grad, *groups = key_call(split, ids, chunks, grad, saved, queries[0])
    *near_weights, query_grad = lax.optimization_barrier(
        (key_weight[0], value_weight[0], query_grad)
    )
    near_weights = jnp.concatenate(near_weights, axis=1)
    key_far_sum = along_z(groups[:4])
    key_rest_sum = along_z(groups[4:])

    def with_pair(total):
        received = send(total[1].astype(bf16), CTX, X_SWAP)
        return (total[0] + received.astype(f32)).astype(bf16)

    def chunk_of(array, distance):
        return lax.dynamic_slice_in_dim(array, ((tp + distance) % 4) * 128, 128, 0)

    query_terms = []
    for distance in range(4):
        query_terms.append(dot_nt(chunk_of(query_grad, distance), query_weight[0]))
    for distance in (0, 1, 3):
        query_terms[distance] = query_terms[distance].astype(bf16)
    query_terms = [lax.optimization_barrier(term) for term in query_terms]
    own = send(query_terms[0], SECTION, ring(4, -1))

    value_grad = with_pair(value_sum)
    key_far = with_pair(key_far_sum)
    key_rest = with_pair(key_rest_sum)

    def rows_of(distance):
        j = (distance + 2) % 4
        key_rows = key_far if j == 0 else key_rest[(j - 1) * 128 : j * 128]
        return jnp.concatenate([key_rows, value_grad[j * 128 : (j + 1) * 128]], axis=1)

    def in_order(array):
        return lax.dynamic_slice_in_dim(
            jnp.concatenate([array, array], axis=0), ((2 - tp) % 4) * 128, array.shape[0], 0
        )

    def term_of(distance):
        return (query_terms[distance] + dot_nt(rows_of(distance), near_weights)).astype(bf16)

    far = term_of(2)
    from_left = send(far[:half_rows], TP, ring(4, 1))
    from_right = send(far[half_rows:], TP, ring(4, -1))
    right, left = lax.optimization_barrier((term_of(1), term_of(3)))
    joint = (SECTION, TP)
    low_a = send(right[half_rows:], joint, joint_ring(1))
    top_b = send(left[:half_rows], joint, joint_ring(-1))
    rows = send(rows_of(0), SECTION, ring(4, -1))
    own = lax.optimization_barrier(own.astype(f32) + dot_nt(rows, sent_weights))
    top_a = (right[:half_rows].astype(f32) + from_left.astype(f32)).astype(bf16)
    top_a = send(top_a, joint, joint_ring(1))
    low_b = (left[half_rows:].astype(f32) + from_right.astype(f32)).astype(bf16)
    low_b = send(low_b, joint, joint_ring(-1))
    sent = jnp.concatenate(
        [
            own[:half_rows] + top_a.astype(f32) + top_b.astype(f32),
            own[half_rows:] + low_a.astype(f32) + low_b.astype(f32),
        ],
        axis=0,
    ).astype(bf16)
    key_grad = in_order(jnp.concatenate([key_far, key_rest], axis=0))
    return (sent[None], key_grad[None], in_order(value_grad)[None])


def solution(mesh):
    placed = (
        P(),
        P(SECTION, CTX, TP),
        P(SECTION, CTX, TP),
        P(SECTION, CTX, TP),
        P(SECTION, (CTX, TP), None),
        P(SECTION, None, TP),
        P(SECTION, None, TP),
        P(SECTION, None, TP),
        P(SECTION, TP, None),
    )

    return jax.shard_map(
        per_device,
        mesh=mesh,
        in_specs=placed,
        out_specs=(
            P(SECTION, (CTX, TP), None),
            P(SECTION, CTX, TP),
            P(SECTION, CTX, TP),
        ),
        check_vma=False,
    )
```
